32 devices in a mesh: dp: 16 (over z, y, core), tensor: 2 (over x).
Axes of the slice: x: 2, y: 2, z: 4, core: 2. Of those that a mesh axis runs over, the one named last changes fastest.
Arguments:
- hidden_in: bfloat16 [2, 8192, 1024], P(None, ('dp', 'tensor')), may hold values from -6 to 6
- segment_ids: int32 [2, 16, 512], P(None, 'dp'), may hold values from 0 to 3, never falling along the last dimension, each value on 1 to 256 neighbouring positions
- out_grad: bfloat16 [2, 8192, 1024], P(None, ('dp', 'tensor')), may hold values from -6 to 6
- w_query: bfloat16 [1024, 1024], P(None, 'tensor'), may hold values from -0.1875 to 0.1875
- b_query: bfloat16 [1024], P('tensor'), may hold values from -1.75 to 1.75
- w_key: bfloat16 [1024, 1024], P(None, 'tensor'), may hold values from -0.1875 to 0.1875
- w_value: bfloat16 [1024, 1024], P(None, 'tensor'), may hold values from -0.1875 to 0.1875
- b_value: bfloat16 [1024], P('tensor'), may hold values from -1.75 to 1.75
- w_out: bfloat16 [1024, 1024], P('tensor'), may hold values from -0.75 to 0.75
- b_out: bfloat16 [1024], replicated, may hold values from -1.75 to 1.75
- attn_gain: bfloat16 [1024], replicated, may hold values from 0.099609375 to 1.8984375
- attn_shift: bfloat16 [1024], replicated, may hold values from -3 to 3
- w_up: bfloat16 [1024, 4096], P(None, 'tensor'), may hold values from -0.1875 to 0.1875
- b_up: bfloat16 [4096], P('tensor'), may hold values from -1.75 to 1.75
- w_down: bfloat16 [4096, 1024], P('tensor'), may hold values from -0.09375 to 0.09375
- b_down: bfloat16 [1024], replicated, may hold values from -1.75 to 1.75
- ffn_gain: bfloat16 [1024], replicated, may hold values from 0.099609375 to 1.8984375
- ffn_shift: bfloat16 [1024], replicated, may hold values from -3 to 3
Outputs:
- output: bfloat16 [2, 8192, 1024], P(None, ('dp', 'tensor'))
- grad_input: bfloat16 [2, 8192, 1024], P(None, ('dp', 'tensor'))
- grad_w_query: float32 [1024, 1024], P('dp', 'tensor')
- grad_b_query: float32 [1024], P('tensor')
- grad_w_key: float32 [1024, 1024], P('dp', 'tensor')
- grad_w_value: float32 [1024, 1024], P('dp', 'tensor')
- grad_b_value: float32 [1024], P('tensor')
- grad_w_out: float32 [1024, 1024], P('tensor', 'dp')
- grad_b_out: float32 [1024], replicated
- grad_attn_gain: float32 [1024], replicated
- grad_attn_shift: float32 [1024], replicated
- grad_w_up: float32 [1024, 4096], P('dp', 'tensor')
- grad_b_up: float32 [4096], P('tensor')
- grad_w_down: float32 [4096, 1024], P('tensor', 'dp')
- grad_b_down: float32 [1024], replicated
- grad_ffn_gain: float32 [1024], replicated
- grad_ffn_shift: float32 [1024], replicated
The draws below stay inside these ranges and needn't reach their ends.
Inputs may be any that keep to these rules, and one draw needn't show every extreme that they name: `segment_ids`: along each packed row the ids never fall, every id from 0 to 3 occurs, and each covers 1 to 256 tokens; a token attends only to tokens of its own row with its own id.
All inputs are finite; a program needn't handle non-finite values.
Results may differ from the reference program's by a relative error of at most 0.02.
Values may be sent and summed in bfloat16 or wider, within the bound.
No kernel may reach another device: no remote copies, remote signals or barrier semaphores. Data moves between devices by JAX's collectives and lax.ppermute only.
A program may use at most 192 MiB of HBM per device.

```python
import math
import jax
import jax.numpy as jnp
import numpy as np
from jax import lax

D = 1024
HEADS = 16
HD = 64
FF = 4096
LEN = 512
MICRO = 2
ROWS_MB = 16
TOK_MB = 8192


def with_spikes(values, stream_key, source, target, parts, factor):
    owner, partner = [(jnp.arange(values.shape[axis_at]) // (values.shape[axis_at] // parts)).reshape([-1 if axis == axis_at else 1 for axis in range(values.ndim)]) for axis_at in (source, target)]
    chosen = jax.random.permutation(stream_key, parts)[partner]
    strong = (owner == chosen) | (owner == (partner + parts // 2) % parts)
    return jnp.where(strong, factor * values, values)


def level_of(rng, shape, shards, least, top_value):
    loudness = 1.0
    for dim, blocks in shards:
        draws = jax.random.uniform(jax.random.fold_in(jax.random.fold_in(rng, 6), dim), (blocks,), jnp.float32, least / len(shards), top_value / len(shards))
        loudness = loudness * jnp.repeat(jnp.exp(draws), shape[dim] // blocks).reshape((-1,) + (1,) * (len(shape) - 1 - dim))
    return loudness


def split_up(amount, total, most, slope):
    weights = [(1 << 20) // math.isqrt(standing ** slope) + 1 for standing in range(2, amount + 1)]
    rest, holding = total - most - (amount - 1), [1] * (amount - 1)
    while rest > 0:
        free = [i for i in range(amount - 1) if holding[i] < most]
        mass, budget = sum([weights[i] for i in free]), rest
        for i in free:
            extra = min(most - holding[i], max(1, budget * weights[i] // mass), rest)
            holding[i] = holding[i] + extra
            rest = rest - extra
    return np.array([most] + holding)


def uneven_parts(own_key, count, total, reach, skew):
    if count == 2:
        one = jax.random.randint(own_key, (), max(1, total - reach), min(reach, total - 1) + 1)
        return jnp.stack([one, total - one])
    lengths = jnp.asarray(split_up(count, total, reach, skew), jnp.int32)
    pairs = (count - 1) // 2
    giver, taker = lengths[1:1 + 2 * pairs:2], lengths[2:2 + 2 * pairs:2]
    slack = jnp.minimum(giver - 1, reach - taker)
    moved = jax.random.randint(jax.random.fold_in(own_key, 1), (pairs,), 0, 1 << 20) % (slack + 1)
    lengths = lengths.at[1:1 + 2 * pairs:2].set(giver - moved).at[2:2 + 2 * pairs:2].set(taker + moved)
    return lengths[jax.random.permutation(jax.random.fold_in(own_key, 2), count)]


def normal_values(key, shape, deviation, reach, split=(), kind=jnp.bfloat16):
    loudness = level_of(key, shape, split, -0.22, 0.18) if split else 1.0
    drawn = jax.random.normal(key, shape, jnp.float32) * deviation * loudness
    return jnp.minimum(jnp.maximum(drawn, -reach), reach).astype(kind)


def gaussian_with(own_key, extent, scale, reach, cuts, heavy, dtype=jnp.bfloat16):
    values = scale * jax.random.normal(own_key, extent, jnp.float32)
    if cuts:
        values = values * level_of(own_key, extent, cuts, -0.22, 0.18)
    return jnp.clip(with_spikes(values, jax.random.fold_in(own_key, 3), *heavy), -reach, reach).astype(dtype)


def setup_inputs(seed: int = 0) -> dict:
    key_list = jax.random.split(jax.random.key(seed), 19)
    hidden_in = normal_values(key_list[0], (MICRO, TOK_MB, D), 1.0, 6.0, ((1, 32),))
    segment_ids = jax.vmap(lambda own: jnp.searchsorted(jnp.cumsum(uneven_parts(own, 4, LEN, LEN // 2, 1)), jnp.arange(LEN), side="right"))(jax.random.split(key_list[1], MICRO * ROWS_MB)).reshape((MICRO, ROWS_MB, LEN)).astype(jnp.int32)
    out_grad = gaussian_with(key_list[2], (MICRO, TOK_MB, D), 1.0, 6.0, ((1, 32),), (1, 2, 32, 2.75))
    w_query = normal_values(key_list[3], (D, D), D ** -0.5, 0.1875, ((1, 2),))
    b_query = normal_values(key_list[4], (D,), 0.3, 1.75, ((0, 2),))
    w_key = normal_values(key_list[5], (D, D), D ** -0.5, 0.1875, ((1, 2),))
    w_value = normal_values(key_list[6], (D, D), D ** -0.5, 0.1875, ((1, 2),))
    b_value = normal_values(key_list[7], (D,), 0.3, 1.75, ((0, 2),))
    w_out = normal_values(key_list[8], (D, D), (D // 16) ** -0.5, 0.75, ((0, 2),))
    b_out = normal_values(key_list[9], (D,), 0.3, 1.75)
    attn_gain = jnp.clip(1.0 + 0.18 * jax.random.normal(key_list[10], (D,), jnp.float32), 0.099609375, 1.8984375).astype(jnp.bfloat16)
    attn_shift = normal_values(key_list[11], (D,), 0.5, 3.0)
    w_up = normal_values(key_list[12], (D, FF), D ** -0.5, 0.1875, ((1, 2),))
    b_up = normal_values(key_list[13], (FF,), 0.3, 1.75, ((0, 2),))
    w_down = normal_values(key_list[14], (FF, D), FF ** -0.5, 0.09375, ((0, 2),))
    b_down = normal_values(key_list[15], (D,), 0.3, 1.75)
    ffn_gain = jnp.clip(1.0 + 0.18 * jax.random.normal(key_list[16], (D,), jnp.float32), 0.099609375, 1.8984375).astype(jnp.bfloat16)
    ffn_shift = normal_values(key_list[17], (D,), 0.5, 3.0)
    return dict(hidden_in=hidden_in, segment_ids=segment_ids, out_grad=out_grad, w_query=w_query, b_query=b_query, w_key=w_key, w_value=w_value, b_value=b_value, w_out=w_out, b_out=b_out, attn_gain=attn_gain, attn_shift=attn_shift, w_up=w_up, b_up=b_up, w_down=w_down, b_down=b_down, ffn_gain=ffn_gain, ffn_shift=ffn_shift)


@jax.custom_vjp
def low(v):
    return lax.optimization_barrier(v.astype(jnp.bfloat16)).astype(jnp.float32)

@jax.custom_vjp
def low_back(v):
    return v

def low_keep(v):
    return (low(v), None)

def low_pass(kept, grad):
    return (grad,)

def back_keep(v):
    return (v, None)

def back_low(kept, grad):
    return (low(grad),)
low.defvjp(low_keep, low_pass)
low_back.defvjp(back_keep, back_low)

def matmul(former, latter):
    return jnp.dot(former, latter, precision=lax.Precision.HIGHEST, preferred_element_type=jnp.float32)

def layer_norm(inputs, scale_vec, offset):
    centre = inputs - lax.optimization_barrier(jnp.mean(inputs, axis=-1, keepdims=True))
    spread = lax.optimization_barrier(jnp.mean(centre * centre, axis=-1, keepdims=True))
    return centre * lax.rsqrt(spread + 1e-12) * scale_vec + offset

def attend(packed):
    queries, keys_row, values_row, seg_row = packed
    length = queries.shape[0]
    q_heads = queries.reshape(length, HEADS, HD)
    k_heads = keys_row.reshape(length, HEADS, HD)
    v_heads = values_row.reshape(length, HEADS, HD)
    scores = low_back(jnp.einsum('qhd,khd->hqk', q_heads, k_heads, precision=lax.Precision.HIGHEST)) * (1.0 / math.sqrt(HD))
    same_doc = seg_row[:, None] == seg_row[None, :]
    scores = jnp.where(same_doc[None], scores, -1e+30)
    probs = jax.nn.softmax(scores, axis=-1)
    context = jnp.einsum('hqk,khd->qhd', low(probs), v_heads, precision=lax.Precision.HIGHEST)
    return low(low_back(context.reshape(length, HEADS * HD)))

def forward(params, tokens, seg_rows):
    w_query, b_query, w_key, w_value, b_value, w_out, b_out, attn_gain, attn_shift, w_up, b_up, w_down, b_down, ffn_gain, ffn_shift = params
    rows = seg_rows.shape[0]
    rounded = low(tokens)
    queries = low(low_back(matmul(rounded, w_query) + b_query))
    keys_all = low(low_back(matmul(rounded, w_key)))
    values_all = low(low_back(matmul(rounded, w_value) + b_value))
    context = lax.map(jax.checkpoint(attend), (queries.reshape(rows, LEN, D), keys_all.reshape(rows, LEN, D), values_all.reshape(rows, LEN, D), seg_rows))
    context = context.reshape(rows * LEN, D)
    resid_one = low_back(matmul(context, w_out)) + b_out + tokens
    hidden_one = layer_norm(resid_one, attn_gain, attn_shift)
    pre_act = low_back(matmul(low(hidden_one), w_up) + b_up)
    activation = low(jax.nn.gelu(pre_act, approximate=False))
    resid_two = low_back(matmul(activation, w_down)) + b_down + hidden_one
    return layer_norm(resid_two, ffn_gain, ffn_shift)

def reference(hidden_in, segment_ids, out_grad, w_query, b_query, w_key, w_value, b_value, w_out, b_out, attn_gain, attn_shift, w_up, b_up, w_down, b_down, ffn_gain, ffn_shift):
    params = tuple((weight.astype(jnp.float32) for weight in (w_query, b_query, w_key, w_value, b_value, w_out, b_out, attn_gain, attn_shift, w_up, b_up, w_down, b_down, ffn_gain, ffn_shift)))
    tokens = hidden_in.astype(jnp.float32).reshape(-1, 8 * LEN, D)
    cotangent = out_grad.astype(jnp.float32).reshape(-1, 8 * LEN, D)
    seg_groups = segment_ids.reshape(-1, 8, LEN)

    def group_step(totals, packed):
        block_in, block_cot, block_seg = packed

        def apply_layer(weights, inputs):
            return forward(weights, inputs, block_seg)
        result, pullback = jax.vjp(apply_layer, params, block_in)
        weight_grads, input_grad = pullback(block_cot)
        totals = jax.tree.map(lambda former, latter: former + latter, totals, weight_grads)
        return (totals, (result, input_grad))
    start = tuple((jnp.zeros_like(weight) for weight in params))
    totals, (results, input_grads) = lax.scan(group_step, start, (tokens, cotangent, seg_groups))
    grad_w_query, grad_b_query, grad_w_key, grad_w_value, grad_b_value, grad_w_out, grad_b_out, grad_attn_gain, grad_attn_shift, grad_w_up, grad_b_up, grad_w_down, grad_b_down, grad_ffn_gain, grad_ffn_shift = totals
    output = results.reshape(MICRO, TOK_MB, D).astype(jnp.bfloat16)
    grad_input = input_grads.reshape(MICRO, TOK_MB, D).astype(jnp.bfloat16)
    return (output, grad_input, grad_w_query, grad_b_query, grad_w_key, grad_w_value, grad_b_value, grad_w_out, grad_b_out, grad_attn_gain, grad_attn_shift, grad_w_up, grad_b_up, grad_w_down, grad_b_down, grad_ffn_gain, grad_ffn_shift)
```

```python
from functools import partial, reduce
import math

import jax
import jax.numpy as jnp
from jax import lax
from jax.experimental import pallas as pl
from jax.experimental.pallas import tpu as pltpu
from jax.sharding import PartitionSpec as P

HD = 64
MICRO = 2


def layer_norm(inputs, scale_vec, offset):
    centre = inputs - jnp.mean(inputs, axis=-1, keepdims=True)
    spread = jnp.mean(centre * centre, axis=-1, keepdims=True)
    return centre * lax.rsqrt(spread + 1e-12) * scale_vec + offset


def gelu_exact(inputs):
    return jax.nn.gelu(inputs, approximate=False)


def matmul(former, latter):
    return jnp.dot(former, latter, preferred_element_type=jnp.float32)


def inner_rows(former, latter):
    return lax.dot_general(
        former, latter, (((0,), (0,)), ((), ())), preferred_element_type=jnp.float32
    )


def inner_cols(former, latter):
    return lax.dot_general(
        former, latter, (((1,), (1,)), ((), ())), preferred_element_type=jnp.float32
    )


def head_split(block):
    return block.reshape(block.shape[0], block.shape[1] // HD, HD)


def masked_scores(queries, key_rows, seg_row):
    scores = jnp.einsum(
        "qhd,khd->hqk",
        head_split(queries),
        head_split(key_rows),
        preferred_element_type=jnp.float32,
    ) * (1.0 / math.sqrt(HD))
    same_doc = seg_row[:, None] == seg_row[None, :]
    return jnp.where(same_doc[None], scores, -1e30)


def attend_row(packed):
    queries, key_rows, value_rows, seg_row = packed
    scores = masked_scores(queries, key_rows, seg_row)
    highest = jnp.max(scores, axis=-1, keepdims=True)
    logsum = highest + jnp.log(jnp.sum(jnp.exp(scores - highest), axis=-1, keepdims=True))
    probs_low = jnp.exp(scores - logsum).astype(jnp.bfloat16)
    context = jnp.einsum(
        "hqk,khd->qhd", probs_low, head_split(value_rows), preferred_element_type=jnp.float32
    )
    return (context.reshape(queries.shape).astype(jnp.bfloat16), logsum[..., 0])


def attend_back(packed):
    queries, key_rows, value_rows, seg_row, logsum, grad_ctx = packed
    scores = masked_scores(queries, key_rows, seg_row)
    probs = jnp.exp(scores - logsum[..., None])
    grad_heads = head_split(grad_ctx)
    grad_probs = jnp.einsum(
        "qhd,khd->hqk", grad_heads, head_split(value_rows), preferred_element_type=jnp.float32
    )
    centred = grad_probs - jnp.sum(probs * grad_probs, axis=-1, keepdims=True)
    grad_scores = (probs * centred * (1.0 / math.sqrt(HD))).astype(jnp.bfloat16)
    grad_query = jnp.einsum(
        "hqk,khd->qhd", grad_scores, head_split(key_rows), preferred_element_type=jnp.float32
    )
    grad_key = jnp.einsum(
        "hqk,qhd->khd", grad_scores, head_split(queries), preferred_element_type=jnp.float32
    )
    grad_value = jnp.einsum(
        "hqk,qhd->khd", probs.astype(jnp.bfloat16), grad_heads, preferred_element_type=jnp.float32
    )
    flat_shape = queries.shape
    return jnp.concatenate(
        [
            grad_query.reshape(flat_shape),
            grad_key.reshape(flat_shape),
            grad_value.reshape(flat_shape),
        ],
        axis=1,
    ).astype(jnp.bfloat16)


def add_trees(former, latter):
    return jax.tree.map(jnp.add, former, latter)


def on_device(
    hidden_in,
    segment_ids,
    out_grad,
    w_query,
    b_query,
    w_key,
    w_value,
    b_value,
    w_out,
    b_out,
    attn_gain,
    attn_shift,
    w_up,
    b_up,
    w_down,
    b_down,
    ffn_gain,
    ffn_shift,
):
    local_width = w_query.shape[1]
    packed_rows = segment_ids.shape[1]
    length = segment_ids.shape[2]
    w_qkv = jnp.concatenate([w_query, w_key, w_value], axis=1)
    b_qkv = jnp.concatenate([b_query, jnp.zeros_like(b_query), b_value]).astype(jnp.float32)
    b_out32 = b_out.astype(jnp.float32)
    b_up32 = b_up.astype(jnp.float32)
    b_down32 = b_down.astype(jnp.float32)
    attn_gain32 = attn_gain.astype(jnp.float32)
    attn_shift32 = attn_shift.astype(jnp.float32)
    ffn_gain32 = ffn_gain.astype(jnp.float32)
    ffn_shift32 = ffn_shift.astype(jnp.float32)

    def to_rows(block):
        return block.reshape(packed_rows, length, block.shape[1])

    outputs = []
    input_grads = []
    weight_terms = []
    small_terms = []
    for micro_step in range(MICRO):
        tokens_low = hidden_in[micro_step]
        tokens = tokens_low.astype(jnp.float32)
        seg_rows = segment_ids[micro_step]
        full_rows = lax.all_gather(tokens_low, "tensor", axis=0, tiled=True)
        qkv_low = (matmul(full_rows, w_qkv) + b_qkv).astype(jnp.bfloat16)
        queries = qkv_low[:, :local_width]
        key_rows = qkv_low[:, local_width : 2 * local_width]
        value_rows = qkv_low[:, 2 * local_width :]
        context, logsums = lax.map(
            attend_row, (to_rows(queries), to_rows(key_rows), to_rows(value_rows), seg_rows)
        )
        context = context.reshape(-1, local_width)
        attn_part = lax.psum_scatter(
            matmul(context, w_out).astype(jnp.bfloat16), "tensor", scatter_dimension=0, tiled=True
        ).astype(jnp.float32)
        resid_one = attn_part + b_out32 + tokens
        hidden_one, norm_one_back = jax.vjp(layer_norm, resid_one, attn_gain32, attn_shift32)
        hidden_low = hidden_one.astype(jnp.bfloat16)
        hidden_rows = lax.all_gather(hidden_low, "tensor", axis=0, tiled=True)
        pre_act = matmul(hidden_rows, w_up) + b_up32
        activation, gelu_back = jax.vjp(gelu_exact, pre_act)
        gelu_low = activation.astype(jnp.bfloat16)
        ffn_part = lax.psum_scatter(
            matmul(gelu_low, w_down).astype(jnp.bfloat16), "tensor", scatter_dimension=0, tiled=True
        ).astype(jnp.float32)
        resid_two = ffn_part + b_down32 + hidden_one
        result, norm_two_back = jax.vjp(layer_norm, resid_two, ffn_gain32, ffn_shift32)
        outputs.append(result.astype(jnp.bfloat16))
        grad_two, grad_ffn_gain, grad_ffn_shift = norm_two_back(
            out_grad[micro_step].astype(jnp.float32)
        )
        grad_two_low = grad_two.astype(jnp.bfloat16)
        grad_two_rows = lax.all_gather(grad_two_low, "tensor", axis=0, tiled=True)
        grad_down = inner_rows(gelu_low, grad_two_rows)
        grad_act = inner_cols(grad_two_rows, w_down)
        grad_pre = gelu_back(grad_act)[0].astype(jnp.bfloat16)
        grad_up = inner_rows(hidden_rows, grad_pre)
        grad_hidden = (
            lax.psum_scatter(
                inner_cols(grad_pre, w_up).astype(jnp.bfloat16),
                "tensor",
                scatter_dimension=0,
                tiled=True,
            ).astype(jnp.float32)
            + grad_two
        )
        grad_one, grad_attn_gain, grad_attn_shift = norm_one_back(grad_hidden)
        grad_one_low = grad_one.astype(jnp.bfloat16)
        grad_one_rows = lax.all_gather(grad_one_low, "tensor", axis=0, tiled=True)
        grad_wout = inner_rows(context, grad_one_rows)
        grad_ctx = inner_cols(grad_one_rows, w_out).astype(jnp.bfloat16)
        grad_qkv = lax.map(
            attend_back,
            (
                to_rows(queries),
                to_rows(key_rows),
                to_rows(value_rows),
                seg_rows,
                logsums,
                to_rows(grad_ctx),
            ),
        )
        grad_qkv = grad_qkv.reshape(-1, 3 * local_width)
        grad_wqkv = inner_rows(full_rows, grad_qkv)
        grad_in = (
            lax.psum_scatter(
                inner_cols(grad_qkv, w_qkv).astype(jnp.bfloat16),
                "tensor",
                scatter_dimension=0,
                tiled=True,
            ).astype(jnp.float32)
            + grad_one
        )
        input_grads.append(grad_in.astype(jnp.bfloat16))
        small_terms.append(
            (
                jnp.sum(grad_qkv.astype(jnp.float32), axis=0),
                jnp.sum(grad_pre.astype(jnp.float32), axis=0),
                jnp.sum(grad_one, axis=0),
                grad_attn_gain,
                grad_attn_shift,
                jnp.sum(grad_two, axis=0),
                grad_ffn_gain,
                grad_ffn_shift,
            )
        )
        weight_set = (grad_wqkv, grad_up, grad_wout, grad_down)
        weight_terms.append(weight_set)
    summed = reduce(add_trees, weight_terms)
    summed = (
        lax.psum_scatter(
            summed[0].astype(jnp.bfloat16), "dp", scatter_dimension=0, tiled=True
        ).astype(jnp.float32),
        lax.psum_scatter(
            summed[1].astype(jnp.bfloat16), "dp", scatter_dimension=0, tiled=True
        ).astype(jnp.float32),
        lax.psum_scatter(
            summed[2].astype(jnp.bfloat16), "dp", scatter_dimension=1, tiled=True
        ).astype(jnp.float32),
        lax.psum_scatter(
            summed[3].astype(jnp.bfloat16), "dp", scatter_dimension=1, tiled=True
        ).astype(jnp.float32),
    )
    red_qkv, red_up, red_wout, red_down = summed
    small = reduce(add_trees, small_terms)
    bias_qkv, bias_up = lax.psum((small[0], small[1]), "dp")
    norm_bout, norm_again, norm_ashift, norm_bdown, norm_fgain, norm_fshift = lax.psum(
        (small[2], small[3], small[4], small[5], small[6], small[7]), ("dp", "tensor")
    )
    output = jnp.stack(outputs, axis=0)
    grad_input = jnp.stack(input_grads, axis=0)
    return (
        output,
        grad_input,
        red_qkv[:, :local_width],
        bias_qkv[:local_width],
        red_qkv[:, local_width : 2 * local_width],
        red_qkv[:, 2 * local_width :],
        bias_qkv[2 * local_width :],
        red_wout,
        norm_bout,
        norm_again,
        norm_ashift,
        red_up,
        bias_up,
        red_down,
        norm_bdown,
        norm_fgain,
        norm_fshift,
    )


def dot_nn(former, latter):
    return jnp.dot(former, latter, preferred_element_type=jnp.float32)


def dot_tn(former, latter):
    return lax.dot_general(
        former, latter, (((0,), (0,)), ((), ())), preferred_element_type=jnp.float32
    )


def dot_nt(former, latter):
    return lax.dot_general(
        former, latter, (((1,), (1,)), ((), ())), preferred_element_type=jnp.float32
    )


def head_pair(block):
    lane = lax.broadcasted_iota(jnp.int32, block.shape, 1)
    zero = jnp.zeros_like(block)
    return (jnp.where(lane < HD, block, zero), jnp.where(lane < HD, zero, block))


def attend_kernel(seg_col_ref, seg_row_ref, q_ref, k_ref, v_ref, ctx_ref, lse_ref, mask_ref):
    mask_ref[...] = jnp.where(seg_col_ref[...] == seg_row_ref[...], 0.0, -1e30)
    for i in range(q_ref.shape[1] // (2 * HD)):
        cols = slice(2 * HD * i, 2 * HD * (i + 1))
        q_pair = q_ref[:, cols] * jnp.bfloat16(1.0 / math.sqrt(HD))
        outs = []
        for h, q_one in enumerate(head_pair(q_pair)):
            scores = dot_nt(k_ref[:, cols], q_one) + mask_ref[...]
            highest = jnp.max(scores, axis=0, keepdims=True)
            raised = jnp.exp(scores - highest)
            total = jnp.sum(raised, axis=0, keepdims=True)
            lse_ref[i, h : h + 1, :] = highest + jnp.log(total)
            mixed = dot_tn(v_ref[:, cols], raised.astype(jnp.bfloat16))
            outs.append(mixed[h * HD : (h + 1) * HD] * (1.0 / total))
        ctx_ref[:, cols] = jnp.concatenate(outs, axis=0).T.astype(jnp.bfloat16)


def attend_back_kernel(
    seg_col_ref, seg_row_ref, q_ref, k_ref, v_ref, lse_ref, g_ref, grad_ref, mask_ref
):
    mask_ref[...] = jnp.where(seg_col_ref[...] == seg_row_ref[...], 0.0, -1e30)
    scale = 1.0 / math.sqrt(HD)
    width = q_ref.shape[1]
    for i in range(width // (2 * HD)):
        cols = slice(2 * HD * i, 2 * HD * (i + 1))
        q_pair = q_ref[:, cols] * jnp.bfloat16(scale)
        grad_q, grad_k, grad_v = [], 0.0, 0.0
        for h, (q_one, g_one) in enumerate(zip(head_pair(q_pair), head_pair(g_ref[:, cols]))):
            scores = dot_nt(k_ref[:, cols], q_one) + mask_ref[...]
            probs = jnp.exp(scores - lse_ref[i, h : h + 1, :])
            grad_p = dot_nt(v_ref[:, cols], g_one)
            delta = jnp.sum(probs * grad_p, axis=0, keepdims=True)
            grad_s = (probs * (grad_p - delta)).astype(jnp.bfloat16)
            grad_v = grad_v + dot_nn(probs.astype(jnp.bfloat16), g_one)
            grad_k = grad_k + dot_nn(grad_s, q_one)
            grad_q.append(dot_tn(k_ref[:, cols], grad_s)[h * HD : (h + 1) * HD])
        at = 2 * HD * i
        grad_q = (jnp.concatenate(grad_q, axis=0) * scale).T
        for n, grad in enumerate((grad_q, grad_k, grad_v)):
            grad_ref[:, n * width + at : n * width + at + 2 * HD] = grad.astype(jnp.bfloat16)


def in_vmem(count):
    return [pl.BlockSpec(memory_space=pltpu.VMEM) for _ in range(count)]


def attend_heads(queries, key_rows, value_rows, seg):
    length, width = queries.shape
    return pl.pallas_call(
        attend_kernel,
        out_shape=(
            jax.ShapeDtypeStruct((length, width), jnp.bfloat16),
            jax.ShapeDtypeStruct((width // (2 * HD), 2, length), jnp.float32),
        ),
        in_specs=in_vmem(5),
        out_specs=tuple(in_vmem(2)),
        scratch_shapes=[pltpu.VMEM((length, length), jnp.float32)],
        compiler_params=pltpu.CompilerParams(vmem_limit_bytes=40 << 20),
        cost_estimate=pl.CostEstimate(
            flops=8 * length * length * width,
            transcendentals=length * length * (width // HD),
            bytes_accessed=8 * length * width,
        ),
        name="attend",
    )(seg[:, None], seg[None, :], queries, key_rows, value_rows)


def attend_heads_back(queries, key_rows, value_rows, seg, lse, grad_ctx):
    length, width = queries.shape
    return pl.pallas_call(
        attend_back_kernel,
        out_shape=jax.ShapeDtypeStruct((length, 3 * width), jnp.bfloat16),
        in_specs=in_vmem(7),
        out_specs=in_vmem(1)[0],
        scratch_shapes=[pltpu.VMEM((length, length), jnp.float32)],
        compiler_params=pltpu.CompilerParams(vmem_limit_bytes=40 << 20),
        cost_estimate=pl.CostEstimate(
            flops=20 * length * length * width,
            transcendentals=length * length * (width // HD),
            bytes_accessed=14 * length * width,
        ),
        name="attend_back",
    )(seg[:, None], seg[None, :], queries, key_rows, value_rows, lse, grad_ctx)


def take_kernel(eighth_ref, *refs):
    weights, (one_ref, up_ref, down_ref), sems = refs[:6], refs[6:9], refs[9]
    copies = []

    def start(source, target):
        copies.append(pltpu.make_async_copy(source, target, sems.at[len(copies)]))
        copies[-1].start()

    def rows_of(ref):
        rows = ref.shape[0] // 8
        return pl.ds(pl.multiple_of(eighth_ref[0] * rows, 16), rows)

    at = 0
    cols = one_ref.shape[1]
    for ref in weights[:4]:
        rows = ref.shape[0] // 8
        for col in range(0, ref.shape[1], cols):
            start(ref.at[rows_of(ref), col : col + cols], one_ref.at[at : at + rows])
            at += rows
    start(weights[4].at[rows_of(weights[4])], up_ref)
    start(weights[5].at[rows_of(weights[5])], down_ref)
    for copy in copies:
        copy.wait()


def take(eighth, weights):
    blocks = [(w.shape[0] // 8, w.shape[1]) for w in weights]
    local = blocks[0][1]
    one = (sum(rows * cols for rows, cols in blocks[:4]) // local, local)
    shapes = [one] + blocks[4:]
    parts = sum(cols // local for _, cols in blocks[:4]) + 2
    return pl.pallas_call(
        take_kernel,
        in_specs=[pl.BlockSpec(memory_space=pltpu.SMEM)]
        + [pl.BlockSpec(memory_space=pl.ANY) for _ in weights],
        out_specs=tuple(in_vmem(3)),
        out_shape=tuple(jax.ShapeDtypeStruct(shape, jnp.bfloat16) for shape in shapes),
        scratch_shapes=[pltpu.SemaphoreType.DMA((parts,))],
        compiler_params=pltpu.CompilerParams(vmem_limit_bytes=40 << 20),
        name="take",
    )(eighth.reshape(1), *weights)


def pieces_of(total, most):
    return [slice(at, min(at + most, total)) for at in range(0, total, most)]


def sent_kernel(rows_ref, near_ref, far_ref, out_ref):
    keep = out_ref.shape[0]
    for rows in pieces_of(keep, 256):
        block = rows_ref[keep + rows.start : keep + rows.stop, :]
        for ref, at in ((near_ref, 0), (far_ref, near_ref.shape[1])):
            for cols in pieces_of(ref.shape[1], 512):
                out_ref[rows, at + cols.start : at + cols.stop] = dot_nn(
                    block, ref[:, cols]
                ).astype(jnp.bfloat16)


def kept_kernel(rows_ref, near_ref, far_ref, got_ref, own_ref, away_ref, held_ref, sent_ref):
    half = got_ref.shape[0] // 2
    for rows in (0, half):
        block = rows_ref[rows : rows + half, :]
        for ref, at, first in ((near_ref, 0, own_ref), (far_ref, near_ref.shape[1], away_ref)):
            for cols in pieces_of(ref.shape[1], 512):
                there = slice(at + cols.start, at + cols.stop)
                total = dot_nn(block, ref[:, cols]) + got_ref[rows : rows + half, there].astype(
                    jnp.float32
                )
                total = total.astype(jnp.bfloat16)
                if rows == 0:
                    first[:, cols] = total
                else:
                    held_ref[:, there] = total[: half // 2]
                    sent_ref[:, there] = total[half // 2 :]


def grad_sent(feature_block, near, far):
    keep = feature_block.shape[0] // 2
    cols = near.shape[1] + far.shape[1]
    return pl.pallas_call(
        sent_kernel,
        out_shape=jax.ShapeDtypeStruct((keep, cols), jnp.bfloat16),
        in_specs=in_vmem(3),
        out_specs=in_vmem(1)[0],
        compiler_params=pltpu.CompilerParams(vmem_limit_bytes=40 << 20),
        cost_estimate=pl.CostEstimate(
            flops=2 * keep * cols * near.shape[0],
            transcendentals=0,
            bytes_accessed=2 * cols * (keep + near.shape[0]),
        ),
        name="grad_sent",
    )(feature_block, near, far)


def grad_kept(feature_block, near, far, got):
    keep = feature_block.shape[0] // 2
    one, two = near.shape[1], far.shape[1]
    shapes = ((keep // 2, one), (keep // 2, two), (keep // 4, one + two), (keep // 4, one + two))
    return pl.pallas_call(
        kept_kernel,
        out_shape=tuple(jax.ShapeDtypeStruct(shape, jnp.bfloat16) for shape in shapes),
        in_specs=in_vmem(4),
        out_specs=tuple(in_vmem(4)),
        compiler_params=pltpu.CompilerParams(vmem_limit_bytes=40 << 20),
        cost_estimate=pl.CostEstimate(
            flops=2 * keep * (one + two) * near.shape[0],
            transcendentals=0,
            bytes_accessed=2 * (one + two) * (2 * keep + near.shape[0]),
        ),
        name="grad_kept",
    )(feature_block, near, far, got)


def gelu_pair(pre):
    cdf = 0.5 * (1.0 + lax.erf(pre * (1.0 / math.sqrt(2.0))))
    pdf = jnp.exp(-0.5 * pre * pre) * (1.0 / math.sqrt(2.0 * math.pi))
    return (pre * cdf).astype(jnp.bfloat16), (cdf + pre * pdf).astype(jnp.bfloat16)


def normed(resid):
    centre = resid - jnp.mean(resid, axis=-1, keepdims=True)
    root = lax.rsqrt(jnp.mean(centre * centre, axis=-1, keepdims=True) + 1e-12)
    return centre * root, root


def normed_back(grad, gain, unit, root):
    inner = grad * gain
    mean = jnp.mean(inner, axis=-1, keepdims=True)
    along = jnp.mean(inner * unit, axis=-1, keepdims=True)
    return root * (inner - mean - unit * along)


def lay_kernel(layout, eighth_ref, *refs):
    ins, outs = refs[: len(layout)], refs[len(layout) :]
    for source, places in zip(ins, layout):
        for mask, at, rows, which, col in places:
            cols = source.shape[1]
            where = pl.multiple_of((eighth_ref[0] ^ mask) * (outs[which].shape[0] // 8), 16)
            offset = pl.multiple_of(where + (col >> 16), 16)
            outs[which][pl.ds(offset, rows), (col & 65535) : (col & 65535) + cols] = source[
                at : at + rows, :
            ]


def lay(eighth, sources, layout, shapes):
    return pl.pallas_call(
        partial(lay_kernel, layout),
        out_shape=tuple(jax.ShapeDtypeStruct(shape, jnp.bfloat16) for shape in shapes),
        in_specs=[pl.BlockSpec(memory_space=pltpu.SMEM)]
        + [pl.BlockSpec(memory_space=pltpu.VMEM) for _ in sources],
        out_specs=tuple(pl.BlockSpec(memory_space=pltpu.VMEM) for _ in shapes),
        compiler_params=pltpu.CompilerParams(vmem_limit_bytes=40 << 20),
        cost_estimate=pl.CostEstimate(
            flops=0,
            transcendentals=0,
            bytes_accessed=4 * sum(math.prod(shape) for shape in shapes),
        ),
        name="lay",
    )(eighth.reshape(1), *sources)


def tie(*values):
    return lax.optimization_barrier(values)


def add_low(former, latter):
    return (former.astype(jnp.float32) + latter.astype(jnp.float32)).astype(jnp.bfloat16)


class Reduction:
    def __init__(self, arrays, bits, send_over):
        self.bits = list(bits)
        lead = (2,) * len(self.bits)
        self.kept = [a.reshape(lead + (a.shape[0] >> len(lead),) + a.shape[1:]) for a in arrays]
        self.send_over = send_over
        self.flying = None

    def send(self, step):
        if step == "side":
            self.kept, sent = self.kept[:1], self.kept[1]
        else:
            axis = self.bits.index(step)
            self.bits.remove(step)
            pairs = [
                [lax.index_in_dim(a, i, axis, keepdims=False) for i in range(2)] for a in self.kept
            ]
            self.kept = [pair[0] for pair in pairs]
            sent = jnp.concatenate([pair[1] for pair in pairs], axis=-1)
        shape = sent.shape
        self.flying = self.send_over(sent.reshape(-1, shape[-1]), step).reshape(shape)

    def land(self, last=False):
        add = add_low
        if last:
            def add(former, latter):
                return former.astype(jnp.float32) + latter.astype(jnp.float32)
        got = jnp.split(self.flying, len(self.kept), axis=-1)
        self.kept = [add(*pair) for pair in zip(self.kept, got)]
        self.flying = None

    def total(self):
        return self.kept[0].reshape(-1, self.kept[0].shape[-1])


def joined(former, latter):
    both = Reduction([], [], former.send_over)
    both.bits = ["part"] + former.bits
    both.kept = [jnp.stack([former.kept[0], latter.kept[0]])]
    return both


def row_on_device(
    groups,
    hidden_in,
    segment_ids,
    out_grad,
    w_query,
    b_query,
    w_key,
    w_value,
    b_value,
    w_out,
    b_out,
    attn_gain,
    attn_shift,
    w_up,
    b_up,
    w_down,
    b_down,
    ffn_gain,
    ffn_shift,
):
    side = lax.axis_index("tensor")
    place = lax.axis_index("dp")
    half = hidden_in.shape[1]
    width = hidden_in.shape[2]
    local = w_query.shape[1]
    depth = groups.bit_length() - 1
    f32 = jnp.float32
    bf16 = jnp.bfloat16

    def over(block):
        return lax.ppermute(block, "tensor", [(0, 1), (1, 0)])

    def across(block, mask):
        return lax.ppermute(block, "dp", [(i, i ^ mask) for i in range(groups)])

    def send(block, step):
        return over(block) if step == "side" else across(block, 1 << step)

    def pick(pair):
        return lax.dynamic_index_in_dim(pair, side, 0, keepdims=False), lax.dynamic_index_in_dim(
            pair, 1 - side, 0, keepdims=False
        )

    eighth = place & 7

    def eighth_of(weight):
        rows = weight.shape[0] // 8
        return lax.dynamic_slice_in_dim(weight, eighth * rows, rows, 0)

    tokens_own, tokens_away = pick(hidden_in)
    fly_tokens = over(tokens_away)
    piece_one, piece_up, piece_down = take(eighth, (w_query, w_key, w_value, w_out, w_up, w_down))
    fly_one = over(piece_one)
    seg_own, _ = pick(segment_ids[:, 0])
    seg = jnp.where(
        side == 0, seg_own, jnp.concatenate([seg_own[half:], seg_own[:half]], axis=0)
    )

    def first_hop(piece):
        rows = piece.shape[0] // 2
        return across(piece[:rows], 2), across(piece[rows:], 4)

    def second_hop(piece, first):
        rows = piece.shape[0] // 2
        near = jnp.concatenate([piece[:rows], first[0]], axis=0)
        far = jnp.concatenate([piece[rows:], first[1]], axis=0)
        held = jnp.concatenate([near, far], axis=0)
        return held, across(near, 4), across(far, 2), across(held, 1)

    def third_hop(near, far):
        held = jnp.concatenate([near, far], axis=0)
        return held, across(held, 1)

    near_far = tuple(
        tuple((mask ^ flip, far) for mask, far in blocks)
        for blocks in (((0, 0), (2, 0), (0, 1), (4, 1)), ((4, 0), (6, 0), (2, 1), (6, 1)))
        for flip in (0, 1)
    )

    def gathered(sources, cuts, shapes):
        rows = sources[0].shape[0] // 4
        layout = tuple(
            tuple(
                (mask, i * rows + at, count, which, col)
                for i, (mask, far) in enumerate(blocks)
                for at, count, which, col in cuts[far]
            )
            for blocks in near_far
        )
        return lay(eighth, sources, layout, shapes)

    block_rows = width // groups
    order = jnp.arange(width, dtype=jnp.int32)
    fine = order // (block_rows // 2)
    wanted = fine >> depth
    for bit in range(1, depth):
        wanted = wanted | (((fine >> (depth - 1 - bit)) & 1) << bit)
    source = (wanted ^ place) * block_rows + ((fine >> (depth - 1)) & 1) * (block_rows // 2)
    source = source + order % (block_rows // 2)
    sorter = (source[:, None] == order[None, :]).astype(bf16)

    def feature_rows(block):
        return dot_nt(sorter, block).astype(bf16)

    tokens_got, sorter, seg, piece_up, piece_down = tie(
        fly_tokens, sorter, seg, piece_up, piece_down
    )
    fly_up_x = over(piece_up)
    tokens_low = jnp.concatenate([tokens_own, tokens_got], axis=0)
    cut = b_query.shape[0]
    biases = jnp.concatenate([b_query, b_value, b_up])
    biases_low = biases
    biases = biases.astype(f32)

    def project(w_q, w_k, w_v, bias):
        return (
            (dot_nn(tokens_low, w_q) + bias[:cut]).astype(bf16),
            dot_nn(tokens_low, w_k).astype(bf16),
            (dot_nn(tokens_low, w_v) + bias[cut : 2 * cut]).astype(bf16),
        )

    qkv_a = project(w_query, w_key, w_value, biases)
    qkv_a, one, piece_down, tokens_low, biases_low = tie(
        qkv_a, fly_one, piece_down, tokens_low, biases_low
    )
    one_first = first_hop(one)
    ctx_a, lse_a = attend_heads(*qkv_a, seg)
    ctx_a, one_first, tokens_low, up, biases_low = tie(
        ctx_a, one_first, tokens_low, fly_up_x, biases_low
    )
    one_held, one_near, one_far, one_core = second_hop(one, one_first)
    fly_down_x = over(piece_down)
    fly_biases = over(biases_low)
    tokens_rows = feature_rows(tokens_low)
    tokens_rows, one_core, tokens_low, up, fly_biases = tie(
        tokens_rows, one_core, tokens_low, up, fly_biases
    )
    biases_b = fly_biases.astype(f32)
    up_first = first_hop(up)
    one_near, one_far, tokens_low, down = tie(one_near, one_far, tokens_low, fly_down_x)
    one_last, one_last_core = third_hop(one_near, one_far)
    one_last_core, tokens_low, out_grad = tie(one_last_core, tokens_low, out_grad)
    grads_own, grads_away = pick(out_grad)
    fly_grads = over(grads_away)
    rows = width // 8
    part = rows // 2
    w_query_b, w_key_b, w_value_b, w_out_b = gathered(
        (one_held, one_core, one_last, one_last_core),
        (
            ((0, rows, 0, 0), (rows, rows, 1, 0)),
            ((0, rows, 2, 0),)
            + tuple(
                (rows + i * (local // 8), local // 8, 3, i * local) for i in range(width // local)
            ),
        ),
        (w_query.shape, w_key.shape, w_value.shape, w_out.shape),
    )

    qkv_b = project(w_query_b, w_key_b, w_value_b, biases_b)
    qkv_b, up_first = tie(qkv_b, up_first)
    up_held, up_near, up_far, up_core = second_hop(up, up_first)
    ctx_b, lse_b = attend_heads(*qkv_b, seg)
    ctx_b, up_core, ctx_a, down = tie(ctx_b, up_core, ctx_a, down)
    down_first = first_hop(down)
    resid_one = (
        dot_nn(ctx_a, w_out)
        + dot_nn(ctx_b, w_out_b)
        + b_out.astype(f32)
        + tokens_low.astype(f32)
    )
    unit_one, root_one = normed(resid_one)
    attn_gain32 = attn_gain.astype(f32)
    hidden_one = unit_one * attn_gain32 + attn_shift.astype(f32)
    hidden_low = hidden_one.astype(bf16)
    act_a, slope_a = gelu_pair(dot_nn(hidden_low, w_up) + biases[2 * cut :])
    act_a, slope_a, hidden_low, up_near, up_far, fly_grads, down_first = tie(
        act_a, slope_a, hidden_low, up_near, up_far, fly_grads, down_first
    )
    up_last, up_last_core = third_hop(up_near, up_far)
    down_held, down_near, down_far, down_core = second_hop(down, down_first)
    ffn_a = dot_nn(act_a, w_down)
    hidden_rows = feature_rows(hidden_low)
    ffn_a, hidden_rows, hidden_low, up_last_core = tie(
        ffn_a, hidden_rows, hidden_low, up_last_core
    )
    (w_up_b,) = gathered(
        (up_held, up_core, up_last, up_last_core),
        (((0, part, 0, 0),), ((0, part, 0, part << 16),)),
        (w_up.shape,),
    )
    act_b, slope_b = gelu_pair(dot_nn(hidden_low, w_up_b) + biases_b[2 * cut :])
    act_b, slope_b, down_near, down_far, down_core = tie(
        act_b, slope_b, down_near, down_far, down_core
    )
    down_last, down_last_core = third_hop(down_near, down_far)
    act_b, down_last_core = tie(act_b, down_last_core)
    part = w_down.shape[0] // 16
    (w_down_b,) = gathered(
        (down_held, down_core, down_last, down_last_core),
        (((0, part, 0, 0),), ((0, part, 0, part << 16),)),
        (w_down.shape,),
    )
    resid_two = ffn_a + dot_nn(act_b, w_down_b) + b_down.astype(f32) + hidden_one
    unit_two, root_two = normed(resid_two)
    ffn_gain32 = ffn_gain.astype(f32)
    output = (unit_two * ffn_gain32 + ffn_shift.astype(f32)).astype(bf16)

    keep = width // 2
    ones = jnp.ones((8, 2 * half), bf16)

    def sent_rows(feature_block, other):
        return across(dot_nn(feature_block[keep:], other).astype(bf16), 1)

    def kept_rows(feature_block, other, got):
        return (dot_nn(feature_block[:keep], other) + got.astype(f32)).astype(bf16)

    places = list(range(1, depth))

    def two_reductions(feature_block, near, far, got):
        own, away, held, sent = grad_kept(feature_block, near, far, got)
        own, away, held, sent = tie(own, away, held, sent)
        one = Reduction([own], places, send)
        one.flying = over(away)
        one.flying = one.flying.reshape((2,) * len(places) + (-1, away.shape[1]))
        two = Reduction([held[:, : near.shape[1]], held[:, near.shape[1] :]], places[1:], send)
        two.flying = across(sent, 2).reshape((2,) * len(places[1:]) + (-1, sent.shape[1]))
        return one, two

    def over_tokens(block):
        if block.dtype == bf16:
            return dot_nn(ones, block)[0]
        return jnp.sum(block, axis=0)

    def land(carry, *reductions, last=False):
        carry, flying = tie(carry, [red.flying for red in reductions])
        for red, got in zip(reductions, flying):
            red.flying = got
            red.land(last)
        return carry

    grad_out = jnp.concatenate([grads_own, fly_grads], axis=0).astype(f32)
    grad_two = normed_back(grad_out, ffn_gain32, unit_two, root_two)
    grad_two_low = grad_two.astype(bf16)
    two_rows = feature_rows(grad_two_low)
    two_rows, output, grad_two_low = tie(two_rows, output, grad_two_low)
    fly_output = over(output[half:])
    got = across(grad_sent(two_rows, act_a, act_b), 1)
    grad_pre_b = (dot_nt(grad_two_low, w_down_b) * slope_b.astype(f32)).astype(bf16)
    two_rows, got, grad_two_low, grad_pre_b = tie(two_rows, got, grad_two_low, grad_pre_b)
    down_one, down_two = two_reductions(two_rows, act_a, act_b, got)
    grad_two_low, down_one.kept, down_two.kept, fly_output = tie(
        grad_two_low, down_one.kept, down_two.kept, fly_output
    )
    grad_pre_a = (dot_nt(grad_two_low, w_down) * slope_a.astype(f32)).astype(bf16)
    got = across(grad_sent(hidden_rows, grad_pre_a, grad_pre_b), 1)
    grad_hidden = dot_nt(grad_pre_a, w_up) + dot_nt(grad_pre_b, w_up_b) + grad_two
    grad_hidden, grad_pre_a, grad_pre_b, got, hidden_rows = tie(
        grad_hidden, grad_pre_a, grad_pre_b, got, hidden_rows
    )
    up_one, up_two = two_reductions(hidden_rows, grad_pre_a, grad_pre_b, got)
    grad_hidden, up_one.kept, up_two.kept = land(
        (grad_hidden, up_one.kept, up_two.kept), down_one, down_two
    )
    down_one.send(1)
    down_two.send("side")
    grad_one = normed_back(grad_hidden, attn_gain32, unit_one, root_one)
    grad_one_low = grad_one.astype(bf16)
    one_rows = feature_rows(grad_one_low)
    grad_one_low, one_rows = tie(grad_one_low, one_rows)
    got_ab = sent_rows(one_rows, jnp.concatenate([ctx_a, ctx_b], axis=1))
    grad_ctx_b = dot_nt(grad_one_low, w_out_b).astype(bf16)
    grad_ctx_a = dot_nt(grad_one_low, w_out).astype(bf16)
    grad_ctx_a, grad_ctx_b, got_ab, one_rows = tie(grad_ctx_a, grad_ctx_b, got_ab, one_rows)
    red_out = Reduction(
        [
            kept_rows(one_rows, ctx_a, got_ab[:, : ctx_a.shape[1]]),
            kept_rows(one_rows, ctx_b, got_ab[:, ctx_a.shape[1] :]),
        ],
        ["part"] + places,
        send,
    )
    grad_ctx_b, red_out.kept = tie(grad_ctx_b, red_out.kept)
    red_out.send(2)
    grad_qkv_b = attend_heads_back(*qkv_b, seg, lse_b, grad_ctx_b)
    grad_ctx_a, grad_qkv_b = land((grad_ctx_a, grad_qkv_b), red_out)
    grad_qkv_a = attend_heads_back(*qkv_a, seg, lse_a, grad_ctx_a)
    grad_qkv_a, grad_qkv_b = land((grad_qkv_a, grad_qkv_b), up_one, up_two)
    up_one.send(1)
    up_two.send("side")
    got = across(grad_sent(tokens_rows, grad_qkv_a, grad_qkv_b), 1)
    grad_in = grad_one
    for grad, weights in (
        (grad_qkv_b, (w_query_b, w_key_b, w_value_b)),
        (grad_qkv_a, (w_query, w_key, w_value)),
    ):
        for i, weight in enumerate(weights):
            grad_in = grad_in + dot_nt(grad[:, i * local : (i + 1) * local], weight)
    grad_in = grad_in.astype(bf16)
    grad_in, grad_qkv_a, grad_qkv_b, got = land(
        (grad_in, grad_qkv_a, grad_qkv_b, got), down_one, down_two
    )
    red_out.send(3)
    red_down = joined(down_one, down_two)
    red_down.send(2)
    first, second = two_reductions(tokens_rows, grad_qkv_a, grad_qkv_b, got)

    sums_a, sums_b = over_tokens(grad_qkv_a), over_tokens(grad_qkv_b)
    near = jnp.concatenate([sums_a[:cut], sums_a[2 * cut :], over_tokens(grad_pre_a)])
    far = jnp.concatenate([sums_b[:cut], sums_b[2 * cut :], over_tokens(grad_pre_b)])
    shared = jnp.concatenate(
        [
            over_tokens(b)
            for b in (
                grad_one,
                grad_hidden * unit_one,
                grad_hidden,
                grad_two,
                grad_out * unit_two,
                grad_out,
            )
        ]
    )
    far = jnp.concatenate([far, shared])
    near = jnp.concatenate([near, shared])
    near, far, grad_in = land((near, far, grad_in), up_one, up_two)
    red_up = joined(up_one, up_two)
    red_up.send(2)
    fly_in = over(grad_in[half:])
    near, far = land((near, far), red_down)
    red_down.send(3)
    near, far = land((near, far), red_out)
    red_out.send(1)
    near, far = land((near, far), first, second)
    first.send(1)
    second.send("side")
    near, far = land((near, far), red_up)
    red_up.send(3)
    near, far, fly_in = tie(near, far, fly_in)
    got = over(far)
    near, got = land((near, got), red_out)
    red_out.send("side")
    small = near + got
    small = land(small, red_down, last=True)
    got = across(small, 1)
    small = land(small, first, second)
    red_qkv = joined(first, second)
    red_qkv.send(2)
    small, got = land((small, got), red_up, last=True)
    small = small + got
    small = land(small, red_out, last=True)
    got = across(small, 2)
    small, got = tie(small, got)
    small = small + got
    got = across(small, 4)
    small, got = land((small, got), red_qkv)
    red_qkv.send(3)
    small = small + got
    got = across(small, 8)
    small, got = land((small, got), red_qkv, last=True)
    small = small + got

    pieces = []
    at = 0
    for size in (cut, cut, b_up.shape[0]) + (width,) * 6:
        pieces.append(small[at : at + size])
        at += size

    def to_owners(mine, theirs):
        return jnp.where(side == 0, jnp.stack([mine, theirs]), jnp.stack([theirs, mine]))

    grad_qkv = red_qkv.total()
    return (
        to_owners(output[:half], fly_output),
        to_owners(grad_in[:half], fly_in),
        grad_qkv[:, :local],
        pieces[0],
        grad_qkv[:, local : 2 * local],
        grad_qkv[:, 2 * local :],
        pieces[1],
        red_out.total().T,
        pieces[3],
        pieces[4],
        pieces[5],
        red_up.total(),
        pieces[2],
        red_down.total().T,
        pieces[6],
        pieces[7],
        pieces[8],
    )


def solution(mesh):
    placed = (
        P(None, ("dp", "tensor"), None),
        P(None, "dp", None),
        P(None, ("dp", "tensor"), None),
        P(None, "tensor"),
        P("tensor"),
        P(None, "tensor"),
        P(None, "tensor"),
        P("tensor"),
        P("tensor", None),
        P(),
        P(),
        P(),
        P(None, "tensor"),
        P("tensor"),
        P("tensor", None),
        P(),
        P(),
        P(),
    )
    body = on_device
    groups = mesh.shape["dp"]
    if mesh.shape["tensor"] == MICRO and groups == 16:
        body = partial(row_on_device, groups)
    return jax.shard_map(
        body,
        mesh=mesh,
        in_specs=placed,
        out_specs=(
            P(None, ("dp", "tensor"), None),
            P(None, ("dp", "tensor"), None),
            P("dp", "tensor"),
            P("tensor"),
            P("dp", "tensor"),
            P("dp", "tensor"),
            P("tensor"),
            P("tensor", "dp"),
            P(),
            P(),
            P(),
            P("dp", "tensor"),
            P("tensor"),
            P("tensor", "dp"),
            P(),
            P(),
            P(),
        ),
        check_vma=False,
    )
```

```python
from functools import partial, reduce
import math

import jax
import jax.numpy as jnp
from jax import lax
from jax.experimental import pallas as pl
from jax.experimental.pallas import tpu as pltpu
from jax.sharding import PartitionSpec as P

HD = 64
MICRO = 2


def layer_norm(inputs, scale_vec, offset):
    centre = inputs - jnp.mean(inputs, axis=-1, keepdims=True)
    spread = jnp.mean(centre * centre, axis=-1, keepdims=True)
    return centre * lax.rsqrt(spread + 1e-12) * scale_vec + offset


def gelu_exact(inputs):
    return jax.nn.gelu(inputs, approximate=False)


def matmul(former, latter):
    return jnp.dot(former, latter, preferred_element_type=jnp.float32)


def inner_rows(former, latter):
    return lax.dot_general(
        former, latter, (((0,), (0,)), ((), ())), preferred_element_type=jnp.float32
    )


def inner_cols(former, latter):
    return lax.dot_general(
        former, latter, (((1,), (1,)), ((), ())), preferred_element_type=jnp.float32
    )


def head_split(block):
    return block.reshape(block.shape[0], block.shape[1] // HD, HD)


def masked_scores(queries, key_rows, seg_row):
    scores = jnp.einsum(
        "qhd,khd->hqk",
        head_split(queries),
        head_split(key_rows),
        preferred_element_type=jnp.float32,
    ) * (1.0 / math.sqrt(HD))
    same_doc = seg_row[:, None] == seg_row[None, :]
    return jnp.where(same_doc[None], scores, -1e30)


def attend_row(packed):
    queries, key_rows, value_rows, seg_row = packed
    scores = masked_scores(queries, key_rows, seg_row)
    highest = jnp.max(scores, axis=-1, keepdims=True)
    logsum = highest + jnp.log(jnp.sum(jnp.exp(scores - highest), axis=-1, keepdims=True))
    probs_low = jnp.exp(scores - logsum).astype(jnp.bfloat16)
    context = jnp.einsum(
        "hqk,khd->qhd", probs_low, head_split(value_rows), preferred_element_type=jnp.float32
    )
    return (context.reshape(queries.shape).astype(jnp.bfloat16), logsum[..., 0])


def attend_back(packed):
    queries, key_rows, value_rows, seg_row, logsum, grad_ctx = packed
    scores = masked_scores(queries, key_rows, seg_row)
    probs = jnp.exp(scores - logsum[..., None])
    grad_heads = head_split(grad_ctx)
    grad_probs = jnp.einsum(
        "qhd,khd->hqk", grad_heads, head_split(value_rows), preferred_element_type=jnp.float32
    )
    centred = grad_probs - jnp.sum(probs * grad_probs, axis=-1, keepdims=True)
    grad_scores = (probs * centred * (1.0 / math.sqrt(HD))).astype(jnp.bfloat16)
    grad_query = jnp.einsum(
        "hqk,khd->qhd", grad_scores, head_split(key_rows), preferred_element_type=jnp.float32
    )
    grad_key = jnp.einsum(
        "hqk,qhd->khd", grad_scores, head_split(queries), preferred_element_type=jnp.float32
    )
    grad_value = jnp.einsum(
        "hqk,qhd->khd", probs.astype(jnp.bfloat16), grad_heads, preferred_element_type=jnp.float32
    )
    flat_shape = queries.shape
    return jnp.concatenate(
        [
            grad_query.reshape(flat_shape),
            grad_key.reshape(flat_shape),
            grad_value.reshape(flat_shape),
        ],
        axis=1,
    ).astype(jnp.bfloat16)


def add_trees(former, latter):
    return jax.tree.map(jnp.add, former, latter)


def on_device(
    hidden_in,
    segment_ids,
    out_grad,
    w_query,
    b_query,
    w_key,
    w_value,
    b_value,
    w_out,
    b_out,
    attn_gain,
    attn_shift,
    w_up,
    b_up,
    w_down,
    b_down,
    ffn_gain,
    ffn_shift,
):
    local_width = w_query.shape[1]
    packed_rows = segment_ids.shape[1]
    length = segment_ids.shape[2]
    w_qkv = jnp.concatenate([w_query, w_key, w_value], axis=1)
    b_qkv = jnp.concatenate([b_query, jnp.zeros_like(b_query), b_value]).astype(jnp.float32)
    b_out32 = b_out.astype(jnp.float32)
    b_up32 = b_up.astype(jnp.float32)
    b_down32 = b_down.astype(jnp.float32)
    attn_gain32 = attn_gain.astype(jnp.float32)
    attn_shift32 = attn_shift.astype(jnp.float32)
    ffn_gain32 = ffn_gain.astype(jnp.float32)
    ffn_shift32 = ffn_shift.astype(jnp.float32)

    def to_rows(block):
        return block.reshape(packed_rows, length, block.shape[1])

    outputs = []
    input_grads = []
    weight_terms = []
    small_terms = []
    for micro_step in range(MICRO):
        tokens_low = hidden_in[micro_step]
        tokens = tokens_low.astype(jnp.float32)
        seg_rows = segment_ids[micro_step]
        full_rows = lax.all_gather(tokens_low, "tensor", axis=0, tiled=True)
        qkv_low = (matmul(full_rows, w_qkv) + b_qkv).astype(jnp.bfloat16)
        queries = qkv_low[:, :local_width]
        key_rows = qkv_low[:, local_width : 2 * local_width]
        value_rows = qkv_low[:, 2 * local_width :]
        context, logsums = lax.map(
            attend_row, (to_rows(queries), to_rows(key_rows), to_rows(value_rows), seg_rows)
        )
        context = context.reshape(-1, local_width)
        attn_part = lax.psum_scatter(
            matmul(context, w_out).astype(jnp.bfloat16), "tensor", scatter_dimension=0, tiled=True
        ).astype(jnp.float32)
        resid_one = attn_part + b_out32 + tokens
        hidden_one, norm_one_back = jax.vjp(layer_norm, resid_one, attn_gain32, attn_shift32)
        hidden_low = hidden_one.astype(jnp.bfloat16)
        hidden_rows = lax.all_gather(hidden_low, "tensor", axis=0, tiled=True)
        pre_act = matmul(hidden_rows, w_up) + b_up32
        activation, gelu_back = jax.vjp(gelu_exact, pre_act)
        gelu_low = activation.astype(jnp.bfloat16)
        ffn_part = lax.psum_scatter(
            matmul(gelu_low, w_down).astype(jnp.bfloat16), "tensor", scatter_dimension=0, tiled=True
        ).astype(jnp.float32)
        resid_two = ffn_part + b_down32 + hidden_one
        result, norm_two_back = jax.vjp(layer_norm, resid_two, ffn_gain32, ffn_shift32)
        outputs.append(result.astype(jnp.bfloat16))
        grad_two, grad_ffn_gain, grad_ffn_shift = norm_two_back(
            out_grad[micro_step].astype(jnp.float32)
        )
        grad_two_low = grad_two.astype(jnp.bfloat16)
        grad_two_rows = lax.all_gather(grad_two_low, "tensor", axis=0, tiled=True)
        grad_down = inner_rows(gelu_low, grad_two_rows)
        grad_act = inner_cols(grad_two_rows, w_down)
        grad_pre = gelu_back(grad_act)[0].astype(jnp.bfloat16)
        grad_up = inner_rows(hidden_rows, grad_pre)
        grad_hidden = (
            lax.psum_scatter(
                inner_cols(grad_pre, w_up).astype(jnp.bfloat16),
                "tensor",
                scatter_dimension=0,
                tiled=True,
            ).astype(jnp.float32)
            + grad_two
        )
        grad_one, grad_attn_gain, grad_attn_shift = norm_one_back(grad_hidden)
        grad_one_low = grad_one.astype(jnp.bfloat16)
        grad_one_rows = lax.all_gather(grad_one_low, "tensor", axis=0, tiled=True)
        grad_wout = inner_rows(context, grad_one_rows)
        grad_ctx = inner_cols(grad_one_rows, w_out).astype(jnp.bfloat16)
        grad_qkv = lax.map(
            attend_back,
            (
                to_rows(queries),
                to_rows(key_rows),
                to_rows(value_rows),
                seg_rows,
                logsums,
                to_rows(grad_ctx),
            ),
        )
        grad_qkv = grad_qkv.reshape(-1, 3 * local_width)
        grad_wqkv = inner_rows(full_rows, grad_qkv)
        grad_in = (
            lax.psum_scatter(
                inner_cols(grad_qkv, w_qkv).astype(jnp.bfloat16),
                "tensor",
                scatter_dimension=0,
                tiled=True,
            ).astype(jnp.float32)
            + grad_one
        )
        input_grads.append(grad_in.astype(jnp.bfloat16))
        small_terms.append(
            (
                jnp.sum(grad_qkv.astype(jnp.float32), axis=0),
                jnp.sum(grad_pre.astype(jnp.float32), axis=0),
                jnp.sum(grad_one, axis=0),
                grad_attn_gain,
                grad_attn_shift,
                jnp.sum(grad_two, axis=0),
                grad_ffn_gain,
                grad_ffn_shift,
            )
        )
        weight_set = (grad_wqkv, grad_up, grad_wout, grad_down)
        weight_terms.append(weight_set)
    summed = reduce(add_trees, weight_terms)
    summed = (
        lax.psum_scatter(
            summed[0].astype(jnp.bfloat16), "dp", scatter_dimension=0, tiled=True
        ).astype(jnp.float32),
        lax.psum_scatter(
            summed[1].astype(jnp.bfloat16), "dp", scatter_dimension=0, tiled=True
        ).astype(jnp.float32),
        lax.psum_scatter(
            summed[2].astype(jnp.bfloat16), "dp", scatter_dimension=1, tiled=True
        ).astype(jnp.float32),
        lax.psum_scatter(
            summed[3].astype(jnp.bfloat16), "dp", scatter_dimension=1, tiled=True
        ).astype(jnp.float32),
    )
    red_qkv, red_up, red_wout, red_down = summed
    small = reduce(add_trees, small_terms)
    bias_qkv, bias_up = lax.psum((small[0], small[1]), "dp")
    norm_bout, norm_again, norm_ashift, norm_bdown, norm_fgain, norm_fshift = lax.psum(
        (small[2], small[3], small[4], small[5], small[6], small[7]), ("dp", "tensor")
    )
    output = jnp.stack(outputs, axis=0)
    grad_input = jnp.stack(input_grads, axis=0)
    return (
        output,
        grad_input,
        red_qkv[:, :local_width],
        bias_qkv[:local_width],
        red_qkv[:, local_width : 2 * local_width],
        red_qkv[:, 2 * local_width :],
        bias_qkv[2 * local_width :],
        red_wout,
        norm_bout,
        norm_again,
        norm_ashift,
        red_up,
        bias_up,
        red_down,
        norm_bdown,
        norm_fgain,
        norm_fshift,
    )


def dot_nn(former, latter):
    return jnp.dot(former, latter, preferred_element_type=jnp.float32)


def dot_tn(former, latter):
    return lax.dot_general(
        former, latter, (((0,), (0,)), ((), ())), preferred_element_type=jnp.float32
    )


def dot_nt(former, latter):
    return lax.dot_general(
        former, latter, (((1,), (1,)), ((), ())), preferred_element_type=jnp.float32
    )


def head_pair(block):
    lane = lax.broadcasted_iota(jnp.int32, block.shape, 1)
    zero = jnp.zeros_like(block)
    return (jnp.where(lane < HD, block, zero), jnp.where(lane < HD, zero, block))


def in_vmem(count):
    return [pl.BlockSpec(memory_space=pltpu.VMEM) for _ in range(count)]


def call(kernel, name, outs, *args, scalars=0, scratch=(), products=0):
    out_shape = tuple(jax.ShapeDtypeStruct(shape, dtype) for shape, dtype in outs)
    moved = sum(math.prod(a.shape) * a.dtype.itemsize for a in (*args, *out_shape))
    return pl.pallas_call(
        kernel,
        out_shape=out_shape,
        in_specs=[pl.BlockSpec(memory_space=pltpu.SMEM) for _ in range(scalars)]
        + in_vmem(len(args) - scalars),
        out_specs=tuple(in_vmem(len(outs))),
        scratch_shapes=list(scratch),
        compiler_params=pltpu.CompilerParams(vmem_limit_bytes=16 << 20),
        cost_estimate=pl.CostEstimate(
            flops=2 * products, transcendentals=0, bytes_accessed=moved
        ),
        name=name,
    )(*args)


def pieces_of(total, most):
    return [slice(at, min(at + most, total)) for at in range(0, total, most)]


def low(block):
    return block.astype(jnp.bfloat16)


def wide(block):
    return block.astype(jnp.float32)


def heads_kernel(
    seg_col_ref, seg_row_ref, x_ref, wq_ref, wk_ref, wv_ref, bias_ref,
    q_ref, k_ref, v_ref, ctx_ref, lse_ref, mask_ref,
):
    mask_ref[...] = jnp.where(seg_col_ref[...] == seg_row_ref[...], 0.0, -1e30)
    for rows in pieces_of(x_ref.shape[0], 256):
        x = x_ref[rows, :]
        for cols in pieces_of(wq_ref.shape[1], 256):
            q_ref[rows, cols] = low(dot_nn(x, wq_ref[:, cols]) + bias_ref[0:1, cols])
            k_ref[rows, cols] = low(dot_nn(x, wk_ref[:, cols]))
            v_ref[rows, cols] = low(dot_nn(x, wv_ref[:, cols]) + bias_ref[1:2, cols])
    for i in range(q_ref.shape[1] // (2 * HD)):
        cols = slice(2 * HD * i, 2 * HD * (i + 1))
        q_pair = q_ref[:, cols] * jnp.bfloat16(1.0 / math.sqrt(HD))
        outs = []
        for h, q_one in enumerate(head_pair(q_pair)):
            scores = dot_nt(k_ref[:, cols], q_one) + mask_ref[...]
            highest = jnp.max(scores, axis=0, keepdims=True)
            raised = jnp.exp(scores - highest)
            total = jnp.sum(raised, axis=0, keepdims=True)
            lse_ref[i, h : h + 1, :] = highest + jnp.log(total)
            mixed = dot_tn(v_ref[:, cols], low(raised))
            outs.append(mixed[h * HD : (h + 1) * HD] * (1.0 / total))
        ctx_ref[:, cols] = low(jnp.concatenate(outs, axis=0).T)


def heads(x, w_q, w_k, w_v, bias, seg):
    length, width = x.shape[0], w_q.shape[1]
    flat = ((length, width), jnp.bfloat16)
    return call(
        heads_kernel,
        "heads",
        (flat, flat, flat, flat, ((width // (2 * HD), 2, length), jnp.float32)),
        seg[:, None], seg[None, :], x, w_q, w_k, w_v, bias,
        products=length * width * (3 * x.shape[1] + 2 * length),
        scratch=[pltpu.VMEM((length, length), jnp.float32)],
    )


def heads_back_kernel(
    seg_col_ref, seg_row_ref, q_ref, k_ref, v_ref, lse_ref, g_ref, w_ref,
    grad_ref, sum_ref, ctx_ref, mask_ref,
):
    mask_ref[...] = jnp.where(seg_col_ref[...] == seg_row_ref[...], 0.0, -1e30)
    scale = 1.0 / math.sqrt(HD)
    width = q_ref.shape[1]
    for rows in pieces_of(g_ref.shape[0], 256):
        for cols in pieces_of(width, 256):
            ctx_ref[rows, cols] = low(dot_nt(g_ref[rows, :], w_ref[cols, :]))
    for i in range(width // (2 * HD)):
        cols = slice(2 * HD * i, 2 * HD * (i + 1))
        q_pair = q_ref[:, cols] * jnp.bfloat16(scale)
        grad_q, grad_k, grad_v = [], 0.0, 0.0
        for h, (q_one, g_one) in enumerate(zip(head_pair(q_pair), head_pair(ctx_ref[:, cols]))):
            scores = dot_nt(k_ref[:, cols], q_one) + mask_ref[...]
            probs = jnp.exp(scores - lse_ref[i, h : h + 1, :])
            grad_p = dot_nt(v_ref[:, cols], g_one)
            delta = jnp.sum(probs * grad_p, axis=0, keepdims=True)
            grad_s = low(probs * (grad_p - delta))
            grad_v = grad_v + dot_nn(low(probs), g_one)
            grad_k = grad_k + dot_nn(grad_s, q_one)
            grad_q.append(dot_tn(k_ref[:, cols], grad_s)[h * HD : (h + 1) * HD])
        grad_q = (jnp.concatenate(grad_q, axis=0) * scale).T
        for n, grad in enumerate((grad_q, grad_k, grad_v)):
            there = slice(n * width + 2 * HD * i, n * width + 2 * HD * (i + 1))
            grad = low(grad)
            grad_ref[:, there] = grad
            sum_ref[:, there] = jnp.sum(wide(grad), axis=0, keepdims=True)


def heads_back(qkv, lse, seg, grad_one_low, w_out):
    length, width = qkv[0].shape
    return call(
        heads_back_kernel,
        "heads_back",
        (((length, 3 * width), jnp.bfloat16), ((1, 3 * width), jnp.float32)),
        seg[:, None], seg[None, :], *qkv, lse, grad_one_low, w_out,
        products=length * width * (w_out.shape[1] + 5 * length),
        scratch=[
            pltpu.VMEM((length, width), jnp.bfloat16),
            pltpu.VMEM((length, length), jnp.float32),
        ],
    )


B_OUT, GAIN_ONE, SHIFT_ONE, B_DOWN, GAIN_TWO, SHIFT_TWO = range(6)


def row_of(ref, row):
    return ref[row : row + 1, :]


def row_norm(resid):
    centre = resid - jnp.mean(resid, axis=-1, keepdims=True)
    root = lax.rsqrt(jnp.mean(centre * centre, axis=-1, keepdims=True) + 1e-12)
    return centre * root, root


def row_norm_back(grad, gain, unit, root):
    inner = grad * gain
    mean = jnp.mean(inner, axis=-1, keepdims=True)
    along = jnp.mean(inner * unit, axis=-1, keepdims=True)
    return root * (inner - mean - unit * along)


def store_turned(depth, place, turned, out_ref, cols):
    rows = turned.shape[0] >> depth
    for block in range(1 << depth):
        step = block ^ place
        where = step & 1
        for bit in range(1, depth):
            where = where * 2 + ((step >> bit) & 1)
        out_ref[pl.ds(pl.multiple_of(where * rows, 16), rows), cols] = turned[
            block * rows : (block + 1) * rows
        ]


def norm_one_kernel(
    depth, place_ref, ctx_a_ref, ctx_b_ref, w_a_ref, w_b_ref, x_ref, par_ref,
    unit_ref, root_ref, low_ref, turned_ref, tokens_ref, sum_ref,
):
    for cols in pieces_of(x_ref.shape[1], 256):
        sum_ref[:, cols] = dot_nn(ctx_a_ref[...], w_a_ref[:, cols]) + dot_nn(
            ctx_b_ref[...], w_b_ref[:, cols]
        )
    for rows in pieces_of(x_ref.shape[0], 128):
        x = x_ref[rows, :]
        unit, root = row_norm(sum_ref[rows, :] + row_of(par_ref, B_OUT) + wide(x))
        unit_ref[rows, :] = unit
        root_ref[rows, :] = root
        hidden = low(unit * row_of(par_ref, GAIN_ONE) + row_of(par_ref, SHIFT_ONE))
        low_ref[rows, :] = hidden
        store_turned(depth, place_ref[0], hidden.T, turned_ref, rows)
        store_turned(depth, place_ref[0], x.T, tokens_ref, rows)


def norm_one(depth, place, ctx_a, ctx_b, w_a, w_b, x, par):
    flat, turned = (x.shape, jnp.bfloat16), (x.shape[::-1], jnp.bfloat16)
    return call(
        partial(norm_one_kernel, depth),
        "norm_one",
        ((x.shape, jnp.float32), ((x.shape[0], 1), jnp.float32), flat, turned, turned),
        place.reshape(1), ctx_a, ctx_b, w_a, w_b, x, par,
        scalars=1,
        scratch=[pltpu.VMEM(x.shape, jnp.float32)],
        products=2 * ctx_a.shape[0] * w_a.shape[0] * w_a.shape[1],
    )


def up_kernel(x_ref, w_ref, bias_ref, act_ref, slope_ref):
    for cols in pieces_of(w_ref.shape[1], 256):
        at = cols.start % bias_ref.shape[1]
        row = 2 + cols.start // bias_ref.shape[1]
        bias = bias_ref[row : row + 1, at : at + 256]
        for rows in pieces_of(x_ref.shape[0], 256):
            pre = dot_nn(x_ref[rows, :], w_ref[:, cols]) + bias
            act_ref[rows, cols], slope_ref[rows, cols] = gelu_pair(pre)


def up(x, w, bias):
    flat = ((x.shape[0], w.shape[1]), jnp.bfloat16)
    products = x.shape[0] * w.shape[0] * w.shape[1]
    return call(up_kernel, "up", (flat, flat), x, w, bias, products=products)


def down_kernel(act_ref, w_ref, out_ref):
    for rows in pieces_of(act_ref.shape[0], 256):
        for cols in pieces_of(w_ref.shape[1], 256):
            out_ref[rows, cols] = dot_nn(act_ref[rows, :], w_ref[:, cols])


def down(act, w):
    out = ((act.shape[0], w.shape[1]), jnp.float32)
    products = act.shape[0] * w.shape[0] * w.shape[1]
    return call(down_kernel, "down", (out,), act, w, products=products)[0]


def norm_two_kernel(
    depth, place_ref, ffn_ref, act_ref, w_ref, unit_one_ref, par_ref, grad_ref,
    out_ref, two_ref, low_ref, turned_ref, sum_ref,
):
    for cols in pieces_of(w_ref.shape[1], 256):
        two_ref[:, cols] = ffn_ref[:, cols] + dot_nn(act_ref[...], w_ref[:, cols])
    sum_ref[...] = jnp.zeros_like(sum_ref)
    for rows in pieces_of(act_ref.shape[0], 128):
        hidden = unit_one_ref[rows, :] * row_of(par_ref, GAIN_ONE) + row_of(par_ref, SHIFT_ONE)
        unit, root = row_norm(two_ref[rows, :] + row_of(par_ref, B_DOWN) + hidden)
        gain = row_of(par_ref, GAIN_TWO)
        out_ref[rows, :] = low(unit * gain + row_of(par_ref, SHIFT_TWO))
        grad = wide(grad_ref[rows, :])
        two = row_norm_back(grad, gain, unit, root)
        two_ref[rows, :] = two
        two_low = low(two)
        low_ref[rows, :] = two_low
        store_turned(depth, place_ref[0], two_low.T, turned_ref, rows)
        for i, term in enumerate((two, grad * unit, grad)):
            sum_ref[i : i + 1, :] += jnp.sum(term, axis=0, keepdims=True)


def norm_two(depth, place, ffn, act, w, unit_one, par, grad_out):
    shape = grad_out.shape
    flat = (shape, jnp.bfloat16)
    return call(
        partial(norm_two_kernel, depth),
        "norm_two",
        (flat, (shape, jnp.float32), flat, (shape[::-1], jnp.bfloat16), ((3, shape[1]), jnp.float32)),
        place.reshape(1), ffn, act, w, unit_one, par, grad_out,
        scalars=1,
        products=act.shape[0] * w.shape[0] * w.shape[1],
    )


def pre_kernel(grad_ref, w_ref, slope_ref, out_ref, sum_ref):
    for cols in pieces_of(w_ref.shape[0], 256):
        total = 0.0
        for rows in pieces_of(grad_ref.shape[0], 256):
            grad = low(dot_nt(grad_ref[rows, :], w_ref[cols, :]) * wide(slope_ref[rows, cols]))
            out_ref[rows, cols] = grad
            total = total + jnp.sum(wide(grad), axis=0, keepdims=True)
        sum_ref[:, cols] = total


def pre_back(grad, w, slope):
    return call(
        pre_kernel, "pre_back", ((slope.shape, jnp.bfloat16), ((1, slope.shape[1]), jnp.float32)),
        grad, w, slope,
        products=grad.shape[0] * w.shape[0] * w.shape[1],
    )


def one_kernel(
    depth, place_ref, pre_a_ref, pre_b_ref, w_a_ref, w_b_ref, two_ref, unit_ref, root_ref, par_ref,
    one_ref, low_ref, turned_ref, sum_ref,
):
    for cols in pieces_of(one_ref.shape[1], 256):
        one_ref[:, cols] = dot_nt(pre_a_ref[...], w_a_ref[cols, :]) + dot_nt(
            pre_b_ref[...], w_b_ref[cols, :]
        )
    sum_ref[...] = jnp.zeros_like(sum_ref)
    for rows in pieces_of(pre_a_ref.shape[0], 128):
        grad = one_ref[rows, :] + two_ref[rows, :]
        unit = unit_ref[rows, :]
        one = row_norm_back(grad, row_of(par_ref, GAIN_ONE), unit, root_ref[rows, :])
        one_ref[rows, :] = one
        one_low = low(one)
        low_ref[rows, :] = one_low
        store_turned(depth, place_ref[0], one_low.T, turned_ref, rows)
        for i, term in enumerate((one, grad * unit, grad)):
            sum_ref[i : i + 1, :] += jnp.sum(term, axis=0, keepdims=True)


def one_back(depth, place, pre_a, pre_b, w_a, w_b, two, unit, root, par):
    shape = two.shape
    return call(
        partial(one_kernel, depth),
        "one_back",
        (
            (shape, jnp.float32),
            (shape, jnp.bfloat16),
            (shape[::-1], jnp.bfloat16),
            ((3, shape[1]), jnp.float32),
        ),
        place.reshape(1), pre_a, pre_b, w_a, w_b, two, unit, root, par,
        scalars=1,
        products=2 * pre_a.shape[0] * w_a.shape[0] * w_a.shape[1],
    )


def input_kernel(one_ref, a_ref, b_ref, *refs):
    weights, out_ref = refs[:6], refs[6]
    width = weights[0].shape[1]
    for rows in pieces_of(one_ref.shape[0], 256):
        for cols in pieces_of(one_ref.shape[1], 256):
            total = one_ref[rows, cols]
            for i, w_ref in enumerate(weights):
                grad_ref = (a_ref, b_ref)[i // 3]
                part = slice((i % 3) * width, (i % 3 + 1) * width)
                total = total + dot_nt(grad_ref[rows, part], w_ref[cols, :])
            out_ref[rows, cols] = low(total)


def input_back(grad_one, grad_a, grad_b, weights):
    return call(
        input_kernel, "input_back", ((grad_one.shape, jnp.bfloat16),),
        grad_one, grad_a, grad_b, *weights,
        products=2 * grad_a.shape[0] * grad_a.shape[1] * grad_one.shape[1],
    )[0]


def take_kernel(index_ref, *refs):
    weights, (one_ref, up_ref, down_ref), sems = refs[:6], refs[6:9], refs[9]
    copies = []

    def start(source, target):
        copies.append(pltpu.make_async_copy(source, target, sems.at[len(copies)]))
        copies[-1].start()

    def rows_of(ref):
        rows = ref.shape[0] // 8
        return pl.ds(pl.multiple_of(index_ref[0] * rows, 16), rows)

    at = 0
    cols = one_ref.shape[1]
    for ref in weights[:4]:
        rows = ref.shape[0] // 8
        for col in range(0, ref.shape[1], cols):
            start(ref.at[rows_of(ref), col : col + cols], one_ref.at[at : at + rows])
            at += rows
    start(weights[4].at[rows_of(weights[4])], up_ref)
    rows = weights[5].shape[0] // 4
    start(weights[5].at[pl.ds(pl.multiple_of(index_ref[8] * rows, 16), rows)], down_ref)
    for copy in copies:
        copy.wait()


def take(indices, weights):
    blocks = [(w.shape[0] // 8, w.shape[1]) for w in weights]
    local = blocks[0][1]
    one = (sum(rows * cols for rows, cols in blocks[:4]) // local, local)
    shapes = [one, blocks[4], (2 * blocks[5][0], blocks[5][1])]
    parts = sum(cols // local for _, cols in blocks[:4]) + 2
    return pl.pallas_call(
        take_kernel,
        in_specs=[pl.BlockSpec(memory_space=pltpu.SMEM)]
        + [pl.BlockSpec(memory_space=pltpu.HBM) for _ in weights],
        out_specs=tuple(in_vmem(3)),
        out_shape=tuple(jax.ShapeDtypeStruct(shape, jnp.bfloat16) for shape in shapes),
        scratch_shapes=[pltpu.SemaphoreType.DMA((parts,))],
        cost_estimate=pl.CostEstimate(
            flops=0, transcendentals=0, bytes_accessed=4 * sum(r * c for r, c in shapes)
        ),
        compiler_params=pltpu.CompilerParams(vmem_limit_bytes=16 << 20),
        name="take",
    )(indices, *weights)


def sent_kernel(rows_ref, near_ref, far_ref, *out_refs):
    half = out_refs[0].shape[0]
    for n, out_ref in enumerate(out_refs):
        ref = (near_ref, far_ref)[n // 2]
        at = (2 + n % 2) * half
        for cols in pieces_of(ref.shape[1], 512):
            out_ref[:, cols] = low(dot_nn(rows_ref[at : at + half, :], ref[:, cols]))


def kept_kernel(core_ref, rows_ref, near_ref, far_ref, *refs):
    got, (kept_ref, sent_ref) = refs[:4], refs[4:]
    half = got[0].shape[0]

    def part(row, side, cols):
        ref = (near_ref, far_ref)[side]
        total = dot_nn(rows_ref[row * half : (row + 1) * half, :], ref[:, cols])
        return low(total + wide(got[2 * side + row][:, cols]))

    for cols in pieces_of(near_ref.shape[1], 512):
        kept_ref[0, :, cols] = part(0, 0, cols)
        sent_ref[1, :, cols] = part(1, 1, cols)
        one, two = part(1, 0, cols), part(0, 1, cols)

        @pl.when(core_ref[0] == 0)
        def _():
            kept_ref[1, :, cols] = one
            sent_ref[0, :, cols] = two

        @pl.when(core_ref[0] != 0)
        def _():
            kept_ref[1, :, cols] = two
            sent_ref[0, :, cols] = one


def grad_sent(feature_block, near, far):
    half = feature_block.shape[0] // 4
    outs = tuple(((half, block.shape[1]), jnp.bfloat16) for block in (near, near, far, far))
    products = 4 * half * near.shape[0] * near.shape[1]
    return call(sent_kernel, "grad_sent", outs, feature_block, near, far, products=products)


def grad_kept(core, feature_block, near, far, got):
    shape = ((2, feature_block.shape[0] // 4, near.shape[1]), jnp.bfloat16)
    return call(
        kept_kernel, "grad_kept", (shape, shape), core.reshape(1), feature_block, near, far, *got,
        scalars=1,
        products=feature_block.shape[0] * near.shape[0] * near.shape[1],
    )


def gelu_pair(pre):
    cdf = 0.5 * (1.0 + lax.erf(pre * (1.0 / math.sqrt(2.0))))
    pdf = jnp.exp(-0.5 * pre * pre) * (1.0 / math.sqrt(2.0 * math.pi))
    return (pre * cdf).astype(jnp.bfloat16), (cdf + pre * pdf).astype(jnp.bfloat16)


def lay_kernel(layout, index_ref, *refs):
    ins, outs = refs[: len(layout)], refs[len(layout) :]
    for source, places in zip(ins, layout):
        for slot, unit, at, rows, which, col in places:
            offset = pl.multiple_of(index_ref[slot] * unit, 16)
            outs[which][pl.ds(offset, rows), col : col + source.shape[1]] = source[
                at : at + rows, :
            ]


def lay(indices, sources, layout, shapes):
    outs = tuple((shape, jnp.bfloat16) for shape in shapes)
    return call(partial(lay_kernel, layout), "lay", outs, indices, *sources, scalars=1)


def tie(*values):
    return lax.optimization_barrier(values)


def add_low(former, latter):
    return (former.astype(jnp.float32) + latter.astype(jnp.float32)).astype(jnp.bfloat16)


class Reduction:
    def __init__(self, kept, sent, step, send_over):
        self.kept = kept
        self.send_over = send_over
        self.flying = send_over(sent, step)

    def send(self, step):
        rows = self.kept.shape[0] // 2
        self.flying = self.send_over(self.kept[rows:], step)
        self.kept = self.kept[:rows]

    def land(self, last=False):
        total = self.kept.astype(jnp.float32) + self.flying.astype(jnp.float32)
        self.kept = total if last else total.astype(jnp.bfloat16)
        self.flying = None


def row_on_device(
    groups,
    hidden_in,
    segment_ids,
    out_grad,
    w_query,
    b_query,
    w_key,
    w_value,
    b_value,
    w_out,
    b_out,
    attn_gain,
    attn_shift,
    w_up,
    b_up,
    w_down,
    b_down,
    ffn_gain,
    ffn_shift,
):
    side = lax.axis_index("tensor")
    place = lax.axis_index("dp")
    half = hidden_in.shape[1]
    width = hidden_in.shape[2]
    local = w_query.shape[1]
    depth = groups.bit_length() - 1
    f32 = jnp.float32
    bf16 = jnp.bfloat16

    def over(block):
        return lax.ppermute(block, "tensor", [(0, 1), (1, 0)])

    def across(block, mask):
        return lax.ppermute(block, "dp", [(i, i ^ mask) for i in range(groups)])

    sides = 2

    def by_core(block, ways):
        pairs = []
        for i in range(groups):
            mask, flip = ways[i & 1]
            pairs += [(i * sides + s, (i ^ mask) * sides + (s ^ flip)) for s in range(sides)]
        return lax.ppermute(block, ("dp", "tensor"), pairs)

    ways = {
        "one": ((0, 1), (2, 0)),
        "two": ((2, 0), (0, 1)),
        "near": ((2, 0), (4, 0)),
        "far": ((4, 0), (2, 0)),
        "side": ((0, 1), (0, 1)),
    }

    def send(block, step):
        return across(block, 1 << step) if isinstance(step, int) else by_core(block, ways[step])

    def pick(pair):
        return lax.dynamic_index_in_dim(pair, side, 0, keepdims=False), lax.dynamic_index_in_dim(
            pair, 1 - side, 0, keepdims=False
        )

    core = place & 1
    eighth = place & 7
    first, second = 2 << core, 4 >> core
    low_bit, high_bit = (place >> 1) & 1, 2 + ((place >> 2) & 1)
    quarter = jnp.where(core == 0, low_bit, high_bit)
    other = jnp.where(core == 0, high_bit, low_bit)
    indices = jnp.stack(
        [eighth ^ mask for mask in (0, first, second, 6, 1, second ^ 1, first ^ 1, 7)]
        + [quarter, quarter ^ 1, other, other ^ 1]
    )
    eighths = ((0, 1), (2, 3), (4, 5), (6, 7))

    def second_hop(piece, got):
        held = jnp.concatenate([piece, got], axis=0)
        return held, send(held, "far")

    def gathered(sources, slots, cuts, shapes):
        layout = []
        for source in slots:
            rows = sources[len(layout)].shape[0] // len(source)
            layout.append(
                tuple(
                    (slot, unit, i * rows + at, count, which, col)
                    for i, slot in enumerate(source)
                    for at, count, unit, which, col in cuts
                )
            )
        return lay(indices, sources, tuple(layout), shapes)

    tokens_own, tokens_away = pick(hidden_in)
    tokens_away, indices = tie(tokens_away, indices)
    fly_tokens = over(tokens_away)
    piece_one, piece_up, piece_down = take(indices, (w_query, w_key, w_value, w_out, w_up, w_down))
    fly_one = over(piece_one)
    biases = jnp.concatenate([b_query, b_value, b_up])
    par = jnp.stack([b_out, attn_gain, attn_shift, b_down, ffn_gain, ffn_shift]).astype(f32)
    seg_own, _ = pick(segment_ids[:, 0])
    seg = jnp.where(
        side == 0, seg_own, jnp.concatenate([seg_own[half:], seg_own[:half]], axis=0)
    )
    cut = b_query.shape[0]
    tokens_got, biases, piece_up, par, seg = tie(fly_tokens, biases, piece_up, par, seg)
    fly_biases = over(biases)
    biases = biases.reshape(-1, cut).astype(f32)
    tokens_low = jnp.concatenate([tokens_own, tokens_got], axis=0)
    *qkv_a, ctx_a, lse_a = heads(tokens_low, w_query, w_key, w_value, biases, seg)
    ctx_a, one, biases_b, piece_up, piece_down = tie(
        ctx_a, fly_one, fly_biases, piece_up, piece_down
    )
    biases_b = biases_b.reshape(-1, cut).astype(f32)
    fly_one = send(one, "near")
    fly_up_x = over(piece_up)
    ctx_a, fly_one, up_piece, piece_down = tie(ctx_a, fly_one, fly_up_x, piece_down)
    one_held, fly_one = second_hop(one, fly_one)
    one_core = across(one_held, 1)
    fly_up = send(up_piece, "near")
    part = piece_down.shape[0] // 2
    fly_down_a = over(piece_down[:part])
    ctx_a, one_last, one_core, fly_up, down_a, piece_down = tie(
        ctx_a, fly_one, one_core, fly_up, fly_down_a, piece_down
    )
    one_last_core = across(one_last, 1)
    up_held, fly_up = second_hop(up_piece, fly_up)
    up_core = across(up_held, 1)
    fly_down_b = over(piece_down[part:])
    one_last_core, ctx_a = tie(one_last_core, ctx_a)
    rows = width // 8
    small_rows = local // 8
    w_query_b, w_key_b, w_value_b, w_out_b = gathered(
        (one_held, one_last, one_core, one_last_core),
        eighths,
        tuple((i * rows, rows, rows, i, 0) for i in range(3))
        + tuple(
            (3 * rows + i * small_rows, small_rows, small_rows, 3, i * local)
            for i in range(width // local)
        ),
        (w_query.shape, w_key.shape, w_value.shape, w_out.shape),
    )
    *qkv_b, ctx_b, lse_b = heads(tokens_low, w_query_b, w_key_b, w_value_b, biases_b, seg)
    ctx_b, up_last, up_core, down_b, out_grad = tie(ctx_b, fly_up, up_core, fly_down_b, out_grad)
    up_last_core = across(up_last, 1)
    down_piece = jnp.concatenate([down_a, down_b], axis=0)
    fly_down = send(down_piece, "near")
    down_core = across(down_piece, 1)
    grads_own, grads_away = pick(out_grad)
    fly_grads = over(grads_away)
    unit_one, root_one, hidden_low, hidden_rows, tokens_rows = norm_one(
        depth, place, ctx_a, ctx_b, w_out, w_out_b, tokens_low, par
    )
    act_a, slope_a = up(hidden_low, w_up, biases)
    ffn_a = down(act_a, w_down)
    ffn_a, up_last_core, hidden_low = tie(ffn_a, up_last_core, hidden_low)
    (w_up_b,) = gathered(
        (up_held, up_last, up_core, up_last_core),
        eighths,
        ((0, rows, rows, 0, 0),),
        (w_up.shape,),
    )
    act_b, slope_b = up(hidden_low, w_up_b, biases_b)
    act_b, fly_down, down_core, fly_grads, down_piece = tie(
        act_b, fly_down, down_core, fly_grads, down_piece
    )
    down_last_core = across(fly_down, 1)
    act_b, down_last_core = tie(act_b, down_last_core)
    part = w_down.shape[0] // 4
    (w_down_b,) = gathered(
        (down_piece, fly_down, down_core, down_last_core),
        ((8,), (9,), (10,), (11,)),
        ((0, part, part, 0, 0),),
        (w_down.shape,),
    )
    grad_out = jnp.concatenate([grads_own, fly_grads], axis=0)
    output, grad_two, grad_two_low, two_rows, sums_two = norm_two(
        depth, place, ffn_a, act_b, w_down_b, unit_one, par, grad_out
    )

    def land(carry, *reductions, last=False):
        carry, flying = tie(carry, [red.flying for red in reductions])
        for red, got in zip(reductions, flying):
            red.flying = got
            red.land(last)
        return carry

    def reduction(feature_block, near, far, got):
        kept, sent = tie(*grad_kept(core, feature_block, near, far, got))
        return Reduction(kept, sent, "one", send)

    def blocks_of(red):
        kept = red.kept.reshape(-1, red.kept.shape[-1])
        red.kept = kept.reshape(2, kept.shape[0] // 2, kept.shape[1])

    def core_sums(feature_block, near, far):
        return [across(block, 1) for block in grad_sent(feature_block, near, far)]

    fly_output = over(output[half:])
    got = core_sums(two_rows, act_a, act_b)
    pre_b, sum_pre_b = pre_back(grad_two_low, w_down_b, slope_b)
    two_rows, got, grad_two_low, pre_b = tie(two_rows, got, grad_two_low, pre_b)
    red_down = reduction(two_rows, act_a, act_b, got)
    grad_two_low, red_down.kept, fly_output = tie(grad_two_low, red_down.kept, fly_output)
    pre_a, sum_pre_a = pre_back(grad_two_low, w_down, slope_a)
    got = core_sums(hidden_rows, pre_a, pre_b)
    grad_one, grad_one_low, one_rows, sums_one = one_back(
        depth, place, pre_a, pre_b, w_up, w_up_b, grad_two, unit_one, root_one, par
    )
    grad_one_low, one_rows, pre_a, pre_b, got, hidden_rows = tie(
        grad_one_low, one_rows, pre_a, pre_b, got, hidden_rows
    )
    red_up = reduction(hidden_rows, pre_a, pre_b, got)
    grad_one_low, one_rows, red_up.kept = land((grad_one_low, one_rows, red_up.kept), red_down)
    red_down.send("two")
    got = core_sums(one_rows, ctx_a, ctx_b)
    grad_qkv_b, sum_qkv_b = heads_back(qkv_b, lse_b, seg, grad_one_low, w_out_b)
    grad_one_low, grad_qkv_b, got, one_rows = tie(grad_one_low, grad_qkv_b, got, one_rows)
    red_out = reduction(one_rows, ctx_a, ctx_b, got)
    grad_one_low, red_out.kept = tie(grad_one_low, red_out.kept)
    grad_qkv_a, sum_qkv_a = heads_back(qkv_a, lse_a, seg, grad_one_low, w_out)
    near = [sum_qkv_a[0, :cut], sum_qkv_a[0, 2 * cut :], sum_pre_a[0]]
    far = [sum_qkv_b[0, :cut], sum_qkv_b[0, 2 * cut :], sum_pre_b[0]]
    small = jnp.concatenate(near + far + [sums_one.reshape(-1), sums_two.reshape(-1)])
    size = 2 * cut + b_up.shape[0]
    got = core_sums(tokens_rows, grad_qkv_a, grad_qkv_b)
    more = across(small, 1)
    small, more, grad_qkv_a, grad_qkv_b, got = tie(small, more, grad_qkv_a, grad_qkv_b, got)
    small = small + more
    more = across(small, 8)
    red_qkv = reduction(tokens_rows, grad_qkv_a, grad_qkv_b, got)
    small, more, grad_qkv_a, grad_qkv_b, red_qkv.kept = land(
        (small, more, grad_qkv_a, grad_qkv_b, red_qkv.kept), red_down, red_up
    )
    small = small + more
    more = across(small, 4)
    blocks_of(red_down)
    red_down.send(2)
    red_up.send("two")
    grad_in = input_back(
        grad_one, grad_qkv_a, grad_qkv_b, (w_query, w_key, w_value, w_query_b, w_key_b, w_value_b)
    )
    small, more, grad_in = tie(small, more, grad_in)
    small = small + more
    small, grad_in = land((small, grad_in), red_out)
    red_out.send("two")
    small, grad_in = land((small, grad_in), red_down)
    blocks_of(red_down)
    red_down.send(3)
    small, grad_in = land((small, grad_in), red_qkv)
    red_qkv.send("two")
    fly_in = over(grad_in[half:])
    small = land(small, red_up)
    blocks_of(red_up)
    red_up.send(2)
    small = land(small, red_down, last=True)
    small = land(small, red_out)
    blocks_of(red_out)
    red_out.send(2)
    small = land(small, red_qkv)
    blocks_of(red_qkv)
    red_qkv.send(2)
    small = land(small, red_up)
    blocks_of(red_up)
    red_up.send(3)
    small, fly_in = land((small, fly_in), red_out)
    blocks_of(red_out)
    red_out.send(3)
    got = over(small[size:])
    small = jnp.concatenate([small[:size], small[2 * size :]])
    small, got = land((small, got), red_qkv)
    blocks_of(red_qkv)
    red_qkv.send(3)
    small = small + got
    got = across(small, 2)
    small, got = land((small, got), red_up, red_out, last=True)
    small = small + got
    small = land(small, red_qkv, last=True)

    pieces = []
    at = 0
    for size in (cut, cut, b_up.shape[0]) + (width,) * 6:
        pieces.append(small[at : at + size])
        at += size

    def to_owners(mine, theirs):
        return jnp.where(side == 0, jnp.stack([mine, theirs]), jnp.stack([theirs, mine]))

    red_out, red_up, red_down, grad_qkv = (
        red.kept.reshape(-1, red.kept.shape[-1]) for red in (red_out, red_up, red_down, red_qkv)
    )
    return (
        to_owners(output[:half], fly_output),
        to_owners(grad_in[:half], fly_in),
        grad_qkv[:, :local],
        pieces[0],
        grad_qkv[:, local : 2 * local],
        grad_qkv[:, 2 * local :],
        pieces[1],
        red_out.T,
        pieces[3],
        pieces[4],
        pieces[5],
        red_up,
        pieces[2],
        red_down.T,
        pieces[6],
        pieces[7],
        pieces[8],
    )


def solution(mesh):
    placed = (
        P(None, ("dp", "tensor"), None),
        P(None, "dp", None),
        P(None, ("dp", "tensor"), None),
        P(None, "tensor"),
        P("tensor"),
        P(None, "tensor"),
        P(None, "tensor"),
        P("tensor"),
        P("tensor", None),
        P(),
        P(),
        P(),
        P(None, "tensor"),
        P("tensor"),
        P("tensor", None),
        P(),
        P(),
        P(),
    )
    body = on_device
    groups = mesh.shape["dp"]
    if mesh.shape["tensor"] == MICRO and groups == 16:
        body = partial(row_on_device, groups)
    return jax.shard_map(
        body,
        mesh=mesh,
        in_specs=placed,
        out_specs=(
            P(None, ("dp", "tensor"), None),
            P(None, ("dp", "tensor"), None),
            P("dp", "tensor"),
            P("tensor"),
            P("dp", "tensor"),
            P("dp", "tensor"),
            P("tensor"),
            P("tensor", "dp"),
            P(),
            P(),
            P(),
            P("dp", "tensor"),
            P("tensor"),
            P("tensor", "dp"),
            P(),
            P(),
            P(),
        ),
        check_vma=False,
    )
```

```python
from functools import partial, reduce
import math

import jax
import jax.numpy as jnp
from jax import lax
from jax.experimental import pallas as pl
from jax.experimental.pallas import tpu as pltpu
from jax.sharding import PartitionSpec as P

HD = 64
MICRO = 2


def layer_norm(inputs, scale_vec, offset):
    centre = inputs - jnp.mean(inputs, axis=-1, keepdims=True)
    spread = jnp.mean(centre * centre, axis=-1, keepdims=True)
    return centre * lax.rsqrt(spread + 1e-12) * scale_vec + offset


def gelu_exact(inputs):
    return jax.nn.gelu(inputs, approximate=False)


def matmul(former, latter):
    return jnp.dot(former, latter, preferred_element_type=jnp.float32)


def inner_rows(former, latter):
    return lax.dot_general(
        former, latter, (((0,), (0,)), ((), ())), preferred_element_type=jnp.float32
    )


def inner_cols(former, latter):
    return lax.dot_general(
        former, latter, (((1,), (1,)), ((), ())), preferred_element_type=jnp.float32
    )


def head_split(block):
    return block.reshape(block.shape[0], block.shape[1] // HD, HD)


def masked_scores(queries, key_rows, seg_row):
    scores = jnp.einsum(
        "qhd,khd->hqk",
        head_split(queries),
        head_split(key_rows),
        preferred_element_type=jnp.float32,
    ) * (1.0 / math.sqrt(HD))
    same_doc = seg_row[:, None] == seg_row[None, :]
    return jnp.where(same_doc[None], scores, -1e30)


def attend_row(packed):
    queries, key_rows, value_rows, seg_row = packed
    scores = masked_scores(queries, key_rows, seg_row)
    highest = jnp.max(scores, axis=-1, keepdims=True)
    logsum = highest + jnp.log(jnp.sum(jnp.exp(scores - highest), axis=-1, keepdims=True))
    probs_low = jnp.exp(scores - logsum).astype(jnp.bfloat16)
    context = jnp.einsum(
        "hqk,khd->qhd", probs_low, head_split(value_rows), preferred_element_type=jnp.float32
    )
    return (context.reshape(queries.shape).astype(jnp.bfloat16), logsum[..., 0])


def attend_back(packed):
    queries, key_rows, value_rows, seg_row, logsum, grad_ctx = packed
    scores = masked_scores(queries, key_rows, seg_row)
    probs = jnp.exp(scores - logsum[..., None])
    grad_heads = head_split(grad_ctx)
    grad_probs = jnp.einsum(
        "qhd,khd->hqk", grad_heads, head_split(value_rows), preferred_element_type=jnp.float32
    )
    centred = grad_probs - jnp.sum(probs * grad_probs, axis=-1, keepdims=True)
    grad_scores = (probs * centred * (1.0 / math.sqrt(HD))).astype(jnp.bfloat16)
    grad_query = jnp.einsum(
        "hqk,khd->qhd", grad_scores, head_split(key_rows), preferred_element_type=jnp.float32
    )
    grad_key = jnp.einsum(
        "hqk,qhd->khd", grad_scores, head_split(queries), preferred_element_type=jnp.float32
    )
    grad_value = jnp.einsum(
        "hqk,qhd->khd", probs.astype(jnp.bfloat16), grad_heads, preferred_element_type=jnp.float32
    )
    flat_shape = queries.shape
    return jnp.concatenate(
        [
            grad_query.reshape(flat_shape),
            grad_key.reshape(flat_shape),
            grad_value.reshape(flat_shape),
        ],
        axis=1,
    ).astype(jnp.bfloat16)


def add_trees(former, latter):
    return jax.tree.map(jnp.add, former, latter)


def on_device(
    hidden_in,
    segment_ids,
    out_grad,
    w_query,
    b_query,
    w_key,
    w_value,
    b_value,
    w_out,
    b_out,
    attn_gain,
    attn_shift,
    w_up,
    b_up,
    w_down,
    b_down,
    ffn_gain,
    ffn_shift,
):
    local_width = w_query.shape[1]
    packed_rows = segment_ids.shape[1]
    length = segment_ids.shape[2]
    w_qkv = jnp.concatenate([w_query, w_key, w_value], axis=1)
    b_qkv = jnp.concatenate([b_query, jnp.zeros_like(b_query), b_value]).astype(jnp.float32)
    b_out32 = b_out.astype(jnp.float32)
    b_up32 = b_up.astype(jnp.float32)
    b_down32 = b_down.astype(jnp.float32)
    attn_gain32 = attn_gain.astype(jnp.float32)
    attn_shift32 = attn_shift.astype(jnp.float32)
    ffn_gain32 = ffn_gain.astype(jnp.float32)
    ffn_shift32 = ffn_shift.astype(jnp.float32)

    def to_rows(block):
        return block.reshape(packed_rows, length, block.shape[1])

    outputs = []
    input_grads = []
    weight_terms = []
    small_terms = []
    for micro_step in range(MICRO):
        tokens_low = hidden_in[micro_step]
        tokens = tokens_low.astype(jnp.float32)
        seg_rows = segment_ids[micro_step]
        full_rows = lax.all_gather(tokens_low, "tensor", axis=0, tiled=True)
        qkv_low = (matmul(full_rows, w_qkv) + b_qkv).astype(jnp.bfloat16)
        queries = qkv_low[:, :local_width]
        key_rows = qkv_low[:, local_width : 2 * local_width]
        value_rows = qkv_low[:, 2 * local_width :]
        context, logsums = lax.map(
            attend_row, (to_rows(queries), to_rows(key_rows), to_rows(value_rows), seg_rows)
        )
        context = context.reshape(-1, local_width)
        attn_part = lax.psum_scatter(
            matmul(context, w_out).astype(jnp.bfloat16), "tensor", scatter_dimension=0, tiled=True
        ).astype(jnp.float32)
        resid_one = attn_part + b_out32 + tokens
        hidden_one, norm_one_back = jax.vjp(layer_norm, resid_one, attn_gain32, attn_shift32)
        hidden_low = hidden_one.astype(jnp.bfloat16)
        hidden_rows = lax.all_gather(hidden_low, "tensor", axis=0, tiled=True)
        pre_act = matmul(hidden_rows, w_up) + b_up32
        activation, gelu_back = jax.vjp(gelu_exact, pre_act)
        gelu_low = activation.astype(jnp.bfloat16)
        ffn_part = lax.psum_scatter(
            matmul(gelu_low, w_down).astype(jnp.bfloat16), "tensor", scatter_dimension=0, tiled=True
        ).astype(jnp.float32)
        resid_two = ffn_part + b_down32 + hidden_one
        result, norm_two_back = jax.vjp(layer_norm, resid_two, ffn_gain32, ffn_shift32)
        outputs.append(result.astype(jnp.bfloat16))
        grad_two, grad_ffn_gain, grad_ffn_shift = norm_two_back(
            out_grad[micro_step].astype(jnp.float32)
        )
        grad_two_low = grad_two.astype(jnp.bfloat16)
        grad_two_rows = lax.all_gather(grad_two_low, "tensor", axis=0, tiled=True)
        grad_down = inner_rows(gelu_low, grad_two_rows)
        grad_act = inner_cols(grad_two_rows, w_down)
        grad_pre = gelu_back(grad_act)[0].astype(jnp.bfloat16)
        grad_up = inner_rows(hidden_rows, grad_pre)
        grad_hidden = (
            lax.psum_scatter(
                inner_cols(grad_pre, w_up).astype(jnp.bfloat16),
                "tensor",
                scatter_dimension=0,
                tiled=True,
            ).astype(jnp.float32)
            + grad_two
        )
        grad_one, grad_attn_gain, grad_attn_shift = norm_one_back(grad_hidden)
        grad_one_low = grad_one.astype(jnp.bfloat16)
        grad_one_rows = lax.all_gather(grad_one_low, "tensor", axis=0, tiled=True)
        grad_wout = inner_rows(context, grad_one_rows)
        grad_ctx = inner_cols(grad_one_rows, w_out).astype(jnp.bfloat16)
        grad_qkv = lax.map(
            attend_back,
            (
                to_rows(queries),
                to_rows(key_rows),
                to_rows(value_rows),
                seg_rows,
                logsums,
                to_rows(grad_ctx),
            ),
        )
        grad_qkv = grad_qkv.reshape(-1, 3 * local_width)
        grad_wqkv = inner_rows(full_rows, grad_qkv)
        grad_in = (
            lax.psum_scatter(
                inner_cols(grad_qkv, w_qkv).astype(jnp.bfloat16),
                "tensor",
                scatter_dimension=0,
                tiled=True,
            ).astype(jnp.float32)
            + grad_one
        )
        input_grads.append(grad_in.astype(jnp.bfloat16))
        small_terms.append(
            (
                jnp.sum(grad_qkv.astype(jnp.float32), axis=0),
                jnp.sum(grad_pre.astype(jnp.float32), axis=0),
                jnp.sum(grad_one, axis=0),
                grad_attn_gain,
                grad_attn_shift,
                jnp.sum(grad_two, axis=0),
                grad_ffn_gain,
                grad_ffn_shift,
            )
        )
        weight_set = (grad_wqkv, grad_up, grad_wout, grad_down)
        weight_terms.append(weight_set)
    summed = reduce(add_trees, weight_terms)
    summed = (
        lax.psum_scatter(
            summed[0].astype(jnp.bfloat16), "dp", scatter_dimension=0, tiled=True
        ).astype(jnp.float32),
        lax.psum_scatter(
            summed[1].astype(jnp.bfloat16), "dp", scatter_dimension=0, tiled=True
        ).astype(jnp.float32),
        lax.psum_scatter(
            summed[2].astype(jnp.bfloat16), "dp", scatter_dimension=1, tiled=True
        ).astype(jnp.float32),
        lax.psum_scatter(
            summed[3].astype(jnp.bfloat16), "dp", scatter_dimension=1, tiled=True
        ).astype(jnp.float32),
    )
    red_qkv, red_up, red_wout, red_down = summed
    small = reduce(add_trees, small_terms)
    bias_qkv, bias_up = lax.psum((small[0], small[1]), "dp")
    norm_bout, norm_again, norm_ashift, norm_bdown, norm_fgain, norm_fshift = lax.psum(
        (small[2], small[3], small[4], small[5], small[6], small[7]), ("dp", "tensor")
    )
    output = jnp.stack(outputs, axis=0)
    grad_input = jnp.stack(input_grads, axis=0)
    return (
        output,
        grad_input,
        red_qkv[:, :local_width],
        bias_qkv[:local_width],
        red_qkv[:, local_width : 2 * local_width],
        red_qkv[:, 2 * local_width :],
        bias_qkv[2 * local_width :],
        red_wout,
        norm_bout,
        norm_again,
        norm_ashift,
        red_up,
        bias_up,
        red_down,
        norm_bdown,
        norm_fgain,
        norm_fshift,
    )


def dot_nn(former, latter):
    return jnp.dot(former, latter, preferred_element_type=jnp.float32)


def dot_tn(former, latter):
    return lax.dot_general(
        former, latter, (((0,), (0,)), ((), ())), preferred_element_type=jnp.float32
    )


def dot_nt(former, latter):
    return lax.dot_general(
        former, latter, (((1,), (1,)), ((), ())), preferred_element_type=jnp.float32
    )


def head_pair(block):
    lane = lax.broadcasted_iota(jnp.int32, block.shape, 1)
    zero = jnp.zeros_like(block)
    return (jnp.where(lane < HD, block, zero), jnp.where(lane < HD, zero, block))


def in_vmem(count):
    return [pl.BlockSpec(memory_space=pltpu.VMEM) for _ in range(count)]


def call(kernel, name, outs, *args, scalars=0, scratch=(), products=0):
    out_shape = tuple(jax.ShapeDtypeStruct(shape, dtype) for shape, dtype in outs)
    moved = sum(math.prod(a.shape) * a.dtype.itemsize for a in (*args, *out_shape))
    return pl.pallas_call(
        kernel,
        out_shape=out_shape,
        in_specs=[pl.BlockSpec(memory_space=pltpu.SMEM) for _ in range(scalars)]
        + in_vmem(len(args) - scalars),
        out_specs=tuple(in_vmem(len(outs))),
        scratch_shapes=list(scratch),
        compiler_params=pltpu.CompilerParams(vmem_limit_bytes=16 << 20),
        cost_estimate=pl.CostEstimate(
            flops=2 * products, transcendentals=0, bytes_accessed=moved
        ),
        name=name,
    )(*args)


def pieces_of(total, most):
    return [slice(at, min(at + most, total)) for at in range(0, total, most)]


def low(block):
    return block.astype(jnp.bfloat16)


def wide(block):
    return block.astype(jnp.float32)


def heads_kernel(
    seg_col_ref, seg_row_ref, x_ref, wq_ref, wk_ref, wv_ref, bias_ref,
    q_ref, k_ref, v_ref, ctx_ref, lse_ref, mask_ref,
):
    mask_ref[...] = jnp.where(seg_col_ref[...] == seg_row_ref[...], 0.0, -1e30)
    for rows in pieces_of(x_ref.shape[0], 256):
        x = x_ref[rows, :]
        for cols in pieces_of(wq_ref.shape[1], 256):
            q_ref[rows, cols] = low(dot_nn(x, wq_ref[:, cols]) + bias_ref[0:1, cols])
            k_ref[rows, cols] = low(dot_nn(x, wk_ref[:, cols]))
            v_ref[rows, cols] = low(dot_nn(x, wv_ref[:, cols]) + bias_ref[1:2, cols])
    for i in range(q_ref.shape[1] // (2 * HD)):
        cols = slice(2 * HD * i, 2 * HD * (i + 1))
        q_pair = q_ref[:, cols] * jnp.bfloat16(1.0 / math.sqrt(HD))
        outs = []
        for h, q_one in enumerate(head_pair(q_pair)):
            scores = dot_nt(k_ref[:, cols], q_one) + mask_ref[...]
            highest = jnp.max(scores, axis=0, keepdims=True)
            raised = jnp.exp(scores - highest)
            total = jnp.sum(raised, axis=0, keepdims=True)
            lse_ref[i, h : h + 1, :] = highest + jnp.log(total)
            mixed = dot_tn(v_ref[:, cols], low(raised))
            outs.append(mixed[h * HD : (h + 1) * HD] * (1.0 / total))
        ctx_ref[:, cols] = low(jnp.concatenate(outs, axis=0).T)


def heads(x, w_q, w_k, w_v, bias, seg):
    length, width = x.shape[0], w_q.shape[1]
    flat = ((length, width), jnp.bfloat16)
    return call(
        heads_kernel,
        "heads",
        (flat, flat, flat, flat, ((width // (2 * HD), 2, length), jnp.float32)),
        seg[:, None], seg[None, :], x, w_q, w_k, w_v, bias,
        products=length * width * (3 * x.shape[1] + 2 * length),
        scratch=[pltpu.VMEM((length, length), jnp.float32)],
    )


def heads_back_kernel(
    seg_col_ref, seg_row_ref, q_ref, k_ref, v_ref, lse_ref, g_ref, w_ref,
    grad_ref, sum_ref, ctx_ref, mask_ref,
):
    mask_ref[...] = jnp.where(seg_col_ref[...] == seg_row_ref[...], 0.0, -1e30)
    scale = 1.0 / math.sqrt(HD)
    width = q_ref.shape[1]
    for rows in pieces_of(g_ref.shape[0], 256):
        for cols in pieces_of(width, 256):
            ctx_ref[rows, cols] = low(dot_nt(g_ref[rows, :], w_ref[cols, :]))
    for i in range(width // (2 * HD)):
        cols = slice(2 * HD * i, 2 * HD * (i + 1))
        q_pair = q_ref[:, cols] * jnp.bfloat16(scale)
        grad_q, grad_k, grad_v = [], 0.0, 0.0
        for h, (q_one, g_one) in enumerate(zip(head_pair(q_pair), head_pair(ctx_ref[:, cols]))):
            scores = dot_nt(k_ref[:, cols], q_one) + mask_ref[...]
            probs = jnp.exp(scores - lse_ref[i, h : h + 1, :])
            grad_p = dot_nt(v_ref[:, cols], g_one)
            delta = jnp.sum(probs * grad_p, axis=0, keepdims=True)
            grad_s = low(probs * (grad_p - delta))
            grad_v = grad_v + dot_nn(low(probs), g_one)
            grad_k = grad_k + dot_nn(grad_s, q_one)
            grad_q.append(dot_tn(k_ref[:, cols], grad_s)[h * HD : (h + 1) * HD])
        grad_q = (jnp.concatenate(grad_q, axis=0) * scale).T
        for n, grad in enumerate((grad_q, grad_k, grad_v)):
            there = slice(n * width + 2 * HD * i, n * width + 2 * HD * (i + 1))
            grad = low(grad)
            grad_ref[:, there] = grad
            sum_ref[:, there] = jnp.sum(wide(grad), axis=0, keepdims=True)


def heads_back(qkv, lse, seg, grad_one_low, w_out):
    length, width = qkv[0].shape
    return call(
        heads_back_kernel,
        "heads_back",
        (((length, 3 * width), jnp.bfloat16), ((1, 3 * width), jnp.float32)),
        seg[:, None], seg[None, :], *qkv, lse, grad_one_low, w_out,
        products=length * width * (w_out.shape[1] + 5 * length),
        scratch=[
            pltpu.VMEM((length, width), jnp.bfloat16),
            pltpu.VMEM((length, length), jnp.float32),
        ],
    )


B_OUT, GAIN_ONE, SHIFT_ONE, B_DOWN, GAIN_TWO, SHIFT_TWO = range(6)


def row_of(ref, row):
    return ref[row : row + 1, :]


def row_norm(resid):
    centre = resid - jnp.mean(resid, axis=-1, keepdims=True)
    root = lax.rsqrt(jnp.mean(centre * centre, axis=-1, keepdims=True) + 1e-12)
    return centre * root, root


def row_norm_back(grad, gain, unit, root):
    inner = grad * gain
    mean = jnp.mean(inner, axis=-1, keepdims=True)
    along = jnp.mean(inner * unit, axis=-1, keepdims=True)
    return root * (inner - mean - unit * along)


def store_turned(depth, place, block, spare_ref, keep_ref, send_ref, base, cols):
    rows = block.shape[1] >> depth
    spare_ref[...] = block.T
    core = place & 1
    for pair in range(1 << (depth - 1)):
        step = pair ^ (place >> 1)
        bits = [(step >> bit) & 1 for bit in range(depth - 1)]
        for owner, ref, start in ((core, keep_ref, 0), (1 - core, send_ref, base)):
            first = jnp.where(owner == 0, bits[1], bits[2])
            second = jnp.where(owner == 0, bits[2], bits[1])
            where = ((bits[0] * 2 + first) * 2 + second) * rows + start
            source = pl.multiple_of((2 * pair + owner) * rows, 16)
            ref[pl.ds(pl.multiple_of(where, 16), rows), cols] = spare_ref[pl.ds(source, rows), :]


def norm_one_kernel(
    depth, place_ref, ctx_a_ref, ctx_b_ref, w_a_ref, w_b_ref, x_ref, par_ref,
    unit_ref, root_ref, low_ref, hidden_ref, tokens_ref, send_ref, sum_ref, spare_ref,
):
    for cols in pieces_of(x_ref.shape[1], 256):
        sum_ref[:, cols] = dot_nn(ctx_a_ref[...], w_a_ref[:, cols]) + dot_nn(
            ctx_b_ref[...], w_b_ref[:, cols]
        )
    for rows in pieces_of(x_ref.shape[0], 128):
        x = x_ref[rows, :]
        unit, root = row_norm(sum_ref[rows, :] + row_of(par_ref, B_OUT) + wide(x))
        unit_ref[rows, :] = unit
        root_ref[rows, :] = root
        hidden = low(unit * row_of(par_ref, GAIN_ONE) + row_of(par_ref, SHIFT_ONE))
        low_ref[rows, :] = hidden
        keep = hidden_ref.shape[0]
        store_turned(depth, place_ref[0], hidden, spare_ref, hidden_ref, send_ref, 0, rows)
        store_turned(depth, place_ref[0], x, spare_ref, tokens_ref, send_ref, keep, rows)
    send_ref[2 * keep : 2 * keep + ctx_a_ref.shape[0], :] = ctx_a_ref[...]
    send_ref[2 * keep + ctx_a_ref.shape[0] :, :] = ctx_b_ref[...]


def norm_one(depth, place, ctx_a, ctx_b, w_a, w_b, x, par):
    length, width = x.shape
    kept = ((width // 2, length), jnp.bfloat16)
    return call(
        partial(norm_one_kernel, depth),
        "norm_one",
        (
            (x.shape, jnp.float32),
            ((length, 1), jnp.float32),
            (x.shape, jnp.bfloat16),
            kept,
            kept,
            ((width + 2 * length, length), jnp.bfloat16),
        ),
        place.reshape(1), ctx_a, ctx_b, w_a, w_b, x, par,
        scalars=1,
        scratch=[pltpu.VMEM(x.shape, jnp.float32), pltpu.VMEM((width, 128), jnp.bfloat16)],
        products=2 * ctx_a.shape[0] * w_a.shape[0] * w_a.shape[1],
    )


def up_kernel(x_ref, w_ref, bias_ref, act_ref, slope_ref):
    for cols in pieces_of(w_ref.shape[1], 256):
        at = cols.start % bias_ref.shape[1]
        row = 2 + cols.start // bias_ref.shape[1]
        bias = bias_ref[row : row + 1, at : at + 256]
        for rows in pieces_of(x_ref.shape[0], 256):
            pre = dot_nn(x_ref[rows, :], w_ref[:, cols]) + bias
            act_ref[rows, cols], slope_ref[rows, cols] = gelu_pair(pre)


def up(x, w, bias):
    flat = ((x.shape[0], w.shape[1]), jnp.bfloat16)
    products = x.shape[0] * w.shape[0] * w.shape[1]
    return call(up_kernel, "up", (flat, flat), x, w, bias, products=products)


def down_kernel(act_ref, w_ref, out_ref):
    for rows in pieces_of(act_ref.shape[0], 256):
        for cols in pieces_of(w_ref.shape[1], 256):
            out_ref[rows, cols] = dot_nn(act_ref[rows, :], w_ref[:, cols])


def down(act, w):
    out = ((act.shape[0], w.shape[1]), jnp.float32)
    products = act.shape[0] * w.shape[0] * w.shape[1]
    return call(down_kernel, "down", (out,), act, w, products=products)[0]


def norm_two_kernel(
    depth, place_ref, ffn_ref, act_ref, w_ref, unit_one_ref, par_ref, grad_ref,
    out_ref, two_ref, low_ref, keep_ref, send_ref, sum_ref, spare_ref,
):
    for cols in pieces_of(w_ref.shape[1], 256):
        two_ref[:, cols] = ffn_ref[:, cols] + dot_nn(act_ref[...], w_ref[:, cols])
    sum_ref[...] = jnp.zeros_like(sum_ref)
    for rows in pieces_of(act_ref.shape[0], 128):
        hidden = unit_one_ref[rows, :] * row_of(par_ref, GAIN_ONE) + row_of(par_ref, SHIFT_ONE)
        unit, root = row_norm(two_ref[rows, :] + row_of(par_ref, B_DOWN) + hidden)
        gain = row_of(par_ref, GAIN_TWO)
        out_ref[rows, :] = low(unit * gain + row_of(par_ref, SHIFT_TWO))
        grad = wide(grad_ref[rows, :])
        two = row_norm_back(grad, gain, unit, root)
        two_ref[rows, :] = two
        two_low = low(two)
        low_ref[rows, :] = two_low
        store_turned(depth, place_ref[0], two_low, spare_ref, keep_ref, send_ref, 0, rows)
        for i, term in enumerate((two, grad * unit, grad)):
            sum_ref[i : i + 1, :] += jnp.sum(term, axis=0, keepdims=True)


def norm_two(depth, place, ffn, act, w, unit_one, par, grad_out):
    shape = grad_out.shape
    flat, kept = (shape, jnp.bfloat16), ((shape[1] // 2, shape[0]), jnp.bfloat16)
    return call(
        partial(norm_two_kernel, depth),
        "norm_two",
        (flat, (shape, jnp.float32), flat, kept, kept, ((3, shape[1]), jnp.float32)),
        place.reshape(1), ffn, act, w, unit_one, par, grad_out,
        scalars=1,
        scratch=[pltpu.VMEM((shape[1], 128), jnp.bfloat16)],
        products=act.shape[0] * w.shape[0] * w.shape[1],
    )


def pre_kernel(grad_ref, w_ref, slope_ref, out_ref, sum_ref):
    for cols in pieces_of(w_ref.shape[0], 256):
        total = 0.0
        for rows in pieces_of(grad_ref.shape[0], 256):
            grad = low(dot_nt(grad_ref[rows, :], w_ref[cols, :]) * wide(slope_ref[rows, cols]))
            out_ref[rows, cols] = grad
            total = total + jnp.sum(wide(grad), axis=0, keepdims=True)
        sum_ref[:, cols] = total


def pre_back(grad, w, slope):
    return call(
        pre_kernel, "pre_back", ((slope.shape, jnp.bfloat16), ((1, slope.shape[1]), jnp.float32)),
        grad, w, slope,
        products=grad.shape[0] * w.shape[0] * w.shape[1],
    )


def one_kernel(
    depth, place_ref, pre_a_ref, pre_b_ref, w_a_ref, w_b_ref, two_ref, unit_ref, root_ref, par_ref,
    one_ref, low_ref, keep_ref, send_ref, sum_ref, spare_ref,
):
    for cols in pieces_of(one_ref.shape[1], 256):
        one_ref[:, cols] = dot_nt(pre_a_ref[...], w_a_ref[cols, :]) + dot_nt(
            pre_b_ref[...], w_b_ref[cols, :]
        )
    sum_ref[...] = jnp.zeros_like(sum_ref)
    for rows in pieces_of(pre_a_ref.shape[0], 128):
        grad = one_ref[rows, :] + two_ref[rows, :]
        unit = unit_ref[rows, :]
        one = row_norm_back(grad, row_of(par_ref, GAIN_ONE), unit, root_ref[rows, :])
        one_ref[rows, :] = one
        one_low = low(one)
        low_ref[rows, :] = one_low
        store_turned(depth, place_ref[0], one_low, spare_ref, keep_ref, send_ref, 0, rows)
        for i, term in enumerate((one, grad * unit, grad)):
            sum_ref[i : i + 1, :] += jnp.sum(term, axis=0, keepdims=True)


def one_back(depth, place, pre_a, pre_b, w_a, w_b, two, unit, root, par):
    shape = two.shape
    return call(
        partial(one_kernel, depth),
        "one_back",
        (
            (shape, jnp.float32),
            (shape, jnp.bfloat16),
            ((shape[1] // 2, shape[0]), jnp.bfloat16),
            ((shape[1] // 2, shape[0]), jnp.bfloat16),
            ((3, shape[1]), jnp.float32),
        ),
        place.reshape(1), pre_a, pre_b, w_a, w_b, two, unit, root, par,
        scalars=1,
        scratch=[pltpu.VMEM((shape[1], 128), jnp.bfloat16)],
        products=2 * pre_a.shape[0] * w_a.shape[0] * w_a.shape[1],
    )


def input_kernel(one_ref, a_ref, b_ref, *refs):
    weights, out_ref = refs[:6], refs[6]
    width = weights[0].shape[1]
    for rows in pieces_of(one_ref.shape[0], 256):
        for cols in pieces_of(one_ref.shape[1], 256):
            total = one_ref[rows, cols]
            for i, w_ref in enumerate(weights):
                grad_ref = (a_ref, b_ref)[i // 3]
                part = slice((i % 3) * width, (i % 3 + 1) * width)
                total = total + dot_nt(grad_ref[rows, part], w_ref[cols, :])
            out_ref[rows, cols] = low(total)


def input_back(grad_one, grad_a, grad_b, weights):
    return call(
        input_kernel, "input_back", ((grad_one.shape, jnp.bfloat16),),
        grad_one, grad_a, grad_b, *weights,
        products=2 * grad_a.shape[0] * grad_a.shape[1] * grad_one.shape[1],
    )[0]


def take_kernel(index_ref, *refs):
    weights, (one_ref, up_ref, down_ref), sems = refs[:6], refs[6:9], refs[9]
    copies = []

    def start(source, target):
        copies.append(pltpu.make_async_copy(source, target, sems.at[len(copies)]))
        copies[-1].start()

    def rows_of(ref):
        rows = ref.shape[0] // 8
        return pl.ds(pl.multiple_of(index_ref[0] * rows, 16), rows)

    at = 0
    cols = one_ref.shape[1]
    for ref in weights[:4]:
        rows = ref.shape[0] // 8
        for col in range(0, ref.shape[1], cols):
            start(ref.at[rows_of(ref), col : col + cols], one_ref.at[at : at + rows])
            at += rows
    start(weights[4].at[rows_of(weights[4])], up_ref)
    rows = weights[5].shape[0] // 4
    start(weights[5].at[pl.ds(pl.multiple_of(index_ref[8] * rows, 16), rows)], down_ref)
    for copy in copies:
        copy.wait()


def take(indices, weights):
    blocks = [(w.shape[0] // 8, w.shape[1]) for w in weights]
    local = blocks[0][1]
    one = (sum(rows * cols for rows, cols in blocks[:4]) // local, local)
    shapes = [one, blocks[4], (2 * blocks[5][0], blocks[5][1])]
    parts = sum(cols // local for _, cols in blocks[:4]) + 2
    return pl.pallas_call(
        take_kernel,
        in_specs=[pl.BlockSpec(memory_space=pltpu.SMEM)]
        + [pl.BlockSpec(memory_space=pltpu.HBM) for _ in weights],
        out_specs=tuple(in_vmem(3)),
        out_shape=tuple(jax.ShapeDtypeStruct(shape, jnp.bfloat16) for shape in shapes),
        scratch_shapes=[pltpu.SemaphoreType.DMA((parts,))],
        cost_estimate=pl.CostEstimate(
            flops=0, transcendentals=0, bytes_accessed=4 * sum(r * c for r, c in shapes)
        ),
        compiler_params=pltpu.CompilerParams(vmem_limit_bytes=16 << 20),
        name="take",
    )(indices, *weights)


def kept_kernel(starts, core_ref, rows_ref, near_ref, far_ref, more_rows_ref, more_near_ref, more_far_ref, kept_ref, sent_ref):
    half = rows_ref.shape[0] // 2
    length = near_ref.shape[0]
    pairs = ((near_ref, more_near_ref, starts[1]), (far_ref, more_far_ref, starts[2]))

    def part(row, side, cols):
        ref, more_ref, start = pairs[side]
        rows, more = slice(row * half, (row + 1) * half), starts[0] + row * half
        total = dot_nn(rows_ref[rows, :], ref[:, cols])
        return low(
            total
            + dot_nn(more_rows_ref[more : more + half, :], more_ref[start : start + length, cols])
        )

    for cols in pieces_of(near_ref.shape[1], 512):
        kept_ref[0, :, cols] = part(0, 0, cols)
        sent_ref[1, :, cols] = part(1, 1, cols)
        one, two = part(1, 0, cols), part(0, 1, cols)

        @pl.when(core_ref[0] == 0)
        def _():
            kept_ref[1, :, cols] = one
            sent_ref[0, :, cols] = two

        @pl.when(core_ref[0] != 0)
        def _():
            kept_ref[1, :, cols] = two
            sent_ref[0, :, cols] = one


def far_kernel(core_ref, rows_ref, near_ref, far_ref, more_rows_ref, more_near_ref, more_far_ref, kept_ref, sent_ref):
    half = rows_ref.shape[0] // 2
    part = half // 4
    pairs = ((near_ref, more_near_ref), (far_ref, more_far_ref))
    for cols in pieces_of(near_ref.shape[1], 512):
        for row in range(2):
            rows = slice(row * half, (row + 1) * half)
            for side, (ref, more_ref) in enumerate(pairs):
                total = dot_nn(rows_ref[rows, :], ref[:, cols])
                total = low(total + dot_nn(more_rows_ref[rows, :], more_ref[:, cols]))
                first = jnp.where(core_ref[0] == 0, side, row)
                second = jnp.where(core_ref[0] == 0, row, side)
                for n in range(2):
                    kept_ref[n, first, second, :, cols] = total[n * part : (n + 1) * part]
                    sent_ref[n, first, second, :, cols] = total[(2 + n) * part : (3 + n) * part]


def grad_kept_far(core, rows, near, far, more):
    shape = ((2, 2, 2, rows.shape[0] // 8, near.shape[1]), jnp.bfloat16)
    return call(
        far_kernel, "grad_kept_far", (shape, shape), core.reshape(1), rows, near, far, *more,
        scalars=1,
        products=4 * rows.shape[0] * near.shape[0] * near.shape[1],
    )


def grad_kept(core, rows, near, far, more, starts):
    shape = ((2, rows.shape[0] // 2, near.shape[1]), jnp.bfloat16)
    return call(
        partial(kept_kernel, starts), "grad_kept", (shape, shape),
        core.reshape(1), rows, near, far, *more,
        scalars=1,
        products=4 * rows.shape[0] * near.shape[0] * near.shape[1],
    )


def gelu_pair(pre):
    cdf = 0.5 * (1.0 + lax.erf(pre * (1.0 / math.sqrt(2.0))))
    pdf = jnp.exp(-0.5 * pre * pre) * (1.0 / math.sqrt(2.0 * math.pi))
    return (pre * cdf).astype(jnp.bfloat16), (cdf + pre * pdf).astype(jnp.bfloat16)


def lay_kernel(layout, index_ref, *refs):
    ins, outs = refs[: len(layout)], refs[len(layout) :]
    for source, places in zip(ins, layout):
        for slot, unit, at, rows, which, col in places:
            offset = pl.multiple_of(index_ref[slot] * unit, 16)
            outs[which][pl.ds(offset, rows), col : col + source.shape[1]] = source[
                at : at + rows, :
            ]


def lay(indices, sources, layout, shapes):
    outs = tuple((shape, jnp.bfloat16) for shape in shapes)
    return call(partial(lay_kernel, layout), "lay", outs, indices, *sources, scalars=1)


def tie(*values):
    return lax.optimization_barrier(values)


def add_low(former, latter):
    return (former.astype(jnp.float32) + latter.astype(jnp.float32)).astype(jnp.bfloat16)


class Reduction:
    def __init__(self, kept, sent, step, send_over):
        self.kept = kept
        self.send_over = send_over
        self.flying = send_over(sent, step)

    def send(self, step):
        rows = self.kept.shape[0] // 2
        self.flying = self.send_over(self.kept[rows:], step)
        self.kept = self.kept[:rows]

    def land(self, last=False):
        total = self.kept.astype(jnp.float32) + self.flying.astype(jnp.float32)
        self.kept = total if last else total.astype(jnp.bfloat16)
        self.flying = None


def row_on_device(
    groups,
    hidden_in,
    segment_ids,
    out_grad,
    w_query,
    b_query,
    w_key,
    w_value,
    b_value,
    w_out,
    b_out,
    attn_gain,
    attn_shift,
    w_up,
    b_up,
    w_down,
    b_down,
    ffn_gain,
    ffn_shift,
):
    side = lax.axis_index("tensor")
    place = lax.axis_index("dp")
    half = hidden_in.shape[1]
    width = hidden_in.shape[2]
    local = w_query.shape[1]
    depth = groups.bit_length() - 1
    f32 = jnp.float32
    bf16 = jnp.bfloat16

    def over(block):
        return lax.ppermute(block, "tensor", [(0, 1), (1, 0)])

    def across(block, mask):
        return lax.ppermute(block, "dp", [(i, i ^ mask) for i in range(groups)])

    sides = 2

    def by_core(block, ways):
        pairs = []
        for i in range(groups):
            mask, flip = ways[i & 1]
            pairs += [(i * sides + s, (i ^ mask) * sides + (s ^ flip)) for s in range(sides)]
        return lax.ppermute(block, ("dp", "tensor"), pairs)

    ways = {
        "one": ((0, 1), (2, 0)),
        "two": ((2, 0), (0, 1)),
        "near": ((2, 0), (4, 0)),
        "far": ((4, 0), (2, 0)),
        "three": ((4, 0), (8, 0)),
        "four": ((8, 0), (4, 0)),
    }

    def send(block, step):
        return across(block, 1 << step) if isinstance(step, int) else by_core(block, ways[step])

    def pick(pair):
        return lax.dynamic_index_in_dim(pair, side, 0, keepdims=False), lax.dynamic_index_in_dim(
            pair, 1 - side, 0, keepdims=False
        )

    core = place & 1
    eighth = place & 7
    first, second = 2 << core, 4 >> core
    low_bit, high_bit = (place >> 1) & 1, 2 + ((place >> 2) & 1)
    quarter = jnp.where(core == 0, low_bit, high_bit)
    other = jnp.where(core == 0, high_bit, low_bit)
    indices = jnp.stack(
        [eighth ^ mask for mask in (0, first, second, 6, 1, second ^ 1, first ^ 1, 7)]
        + [quarter, quarter ^ 1, other, other ^ 1]
    )
    eighths = ((0, 1), (2, 3), (4, 5), (6, 7))

    def second_hop(piece, got):
        held = jnp.concatenate([piece, got], axis=0)
        return held, send(held, "far")

    def gathered(sources, slots, cuts, shapes):
        layout = []
        for source in slots:
            rows = sources[len(layout)].shape[0] // len(source)
            layout.append(
                tuple(
                    (slot, unit, i * rows + at, count, which, col)
                    for i, slot in enumerate(source)
                    for at, count, unit, which, col in cuts
                )
            )
        return lay(indices, sources, tuple(layout), shapes)

    tokens_own, tokens_away = pick(hidden_in)
    tokens_away, indices = tie(tokens_away, indices)
    fly_tokens = over(tokens_away)
    piece_one, piece_up, piece_down = take(indices, (w_query, w_key, w_value, w_out, w_up, w_down))
    fly_one = over(piece_one)
    biases = jnp.concatenate([b_query, b_value, b_up])
    par = jnp.stack([b_out, attn_gain, attn_shift, b_down, ffn_gain, ffn_shift]).astype(f32)
    seg_own, _ = pick(segment_ids[:, 0])
    seg = jnp.where(
        side == 0, seg_own, jnp.concatenate([seg_own[half:], seg_own[:half]], axis=0)
    )
    cut = b_query.shape[0]
    tokens_got, biases, piece_up, par, seg = tie(fly_tokens, biases, piece_up, par, seg)
    fly_biases = over(biases)
    biases = biases.reshape(-1, cut).astype(f32)
    tokens_low = jnp.concatenate([tokens_own, tokens_got], axis=0)
    *qkv_a, ctx_a, lse_a = heads(tokens_low, w_query, w_key, w_value, biases, seg)
    ctx_a, one, biases_b, piece_up, piece_down = tie(
        ctx_a, fly_one, fly_biases, piece_up, piece_down
    )
    biases_b = biases_b.reshape(-1, cut).astype(f32)
    fly_one = send(one, "near")
    fly_up_x = over(piece_up)
    ctx_a, fly_one, up_piece, piece_down = tie(ctx_a, fly_one, fly_up_x, piece_down)
    one_held, fly_one = second_hop(one, fly_one)
    one_core = across(one_held, 1)
    fly_up = send(up_piece, "near")
    part = piece_down.shape[0] // 2
    fly_down_a = over(piece_down[:part])
    ctx_a, one_last, one_core, fly_up, down_a, piece_down = tie(
        ctx_a, fly_one, one_core, fly_up, fly_down_a, piece_down
    )
    one_last_core = across(one_last, 1)
    up_held, fly_up = second_hop(up_piece, fly_up)
    up_core = across(up_held, 1)
    fly_down_b = over(piece_down[part:])
    one_last_core, ctx_a = tie(one_last_core, ctx_a)
    rows = width // 8
    small_rows = local // 8
    w_query_b, w_key_b, w_value_b, w_out_b = gathered(
        (one_held, one_last, one_core, one_last_core),
        eighths,
        tuple((i * rows, rows, rows, i, 0) for i in range(3))
        + tuple(
            (3 * rows + i * small_rows, small_rows, small_rows, 3, i * local)
            for i in range(width // local)
        ),
        (w_query.shape, w_key.shape, w_value.shape, w_out.shape),
    )
    *qkv_b, ctx_b, lse_b = heads(tokens_low, w_query_b, w_key_b, w_value_b, biases_b, seg)
    ctx_b, up_last, up_core, down_b, out_grad = tie(ctx_b, fly_up, up_core, fly_down_b, out_grad)
    up_last_core = across(up_last, 1)
    down_piece = jnp.concatenate([down_a, down_b], axis=0)
    fly_down = send(down_piece, "near")
    down_core = across(down_piece, 1)
    grads_own, grads_away = pick(out_grad)
    fly_grads = over(grads_away)
    unit_one, root_one, hidden_low, hidden_rows, tokens_rows, shared = norm_one(
        depth, place, ctx_a, ctx_b, w_out, w_out_b, tokens_low, par
    )
    act_a, slope_a = up(hidden_low, w_up, biases)
    ffn_a = down(act_a, w_down)
    ffn_a, up_last_core, hidden_low = tie(ffn_a, up_last_core, hidden_low)
    (w_up_b,) = gathered(
        (up_held, up_last, up_core, up_last_core),
        eighths,
        ((0, rows, rows, 0, 0),),
        (w_up.shape,),
    )
    act_b, slope_b = up(hidden_low, w_up_b, biases_b)
    act_b, fly_down, down_core, fly_grads, down_piece = tie(
        act_b, fly_down, down_core, fly_grads, down_piece
    )
    down_last_core = across(fly_down, 1)
    act_b, act_a, down_last_core, shared = tie(act_b, act_a, down_last_core, shared)
    fly_act_a = across(act_a, 1)
    fly_act_b = across(act_b, 1)
    fly_shared = across(shared, 1)
    part = w_down.shape[0] // 4
    (w_down_b,) = gathered(
        (down_piece, fly_down, down_core, down_last_core),
        ((8,), (9,), (10,), (11,)),
        ((0, part, part, 0, 0),),
        (w_down.shape,),
    )
    grad_out = jnp.concatenate([grads_own, fly_grads], axis=0)
    output, grad_two, grad_two_low, two_rows, two_sent, sums_two = norm_two(
        depth, place, ffn_a, act_b, w_down_b, unit_one, par, grad_out
    )

    def land(carry, *reductions, last=False):
        carry, flying = tie(carry, [red.flying for red in reductions])
        for red, got in zip(reductions, flying):
            red.flying = got
            red.land(last)
        return carry

    def reduction(rows, near, far, more, *starts):
        kept, sent = tie(*grad_kept(core, rows, near, far, more, starts))
        return Reduction(kept, sent, "one", send)

    def blocks_of(red):
        kept = red.kept.reshape(-1, red.kept.shape[-1])
        red.kept = kept.reshape(2, kept.shape[0] // 2, kept.shape[1])

    two_rows, two_sent, grad_two_low, more_act_a, more_act_b = tie(
        two_rows, two_sent, grad_two_low, fly_act_a, fly_act_b
    )
    more_two = across(two_sent, 1)
    pre_b, sum_pre_b = pre_back(grad_two_low, w_down_b, slope_b)
    pre_b, grad_two_low, shared = tie(pre_b, grad_two_low, fly_shared)
    fly_pre_b = across(pre_b, 1)
    pre_a, sum_pre_a = pre_back(grad_two_low, w_down, slope_a)
    two_rows, more_two, pre_a = tie(two_rows, more_two, pre_a)
    kept, sent = tie(
        *grad_kept_far(core, two_rows, act_a, act_b, (more_two, more_act_a, more_act_b))
    )
    red_down = Reduction(kept, sent, "three", send)
    pre_a, red_down.kept, more_pre_b = tie(pre_a, red_down.kept, fly_pre_b)
    fly_pre_a = across(pre_a, 1)
    grad_one, grad_one_low, one_rows, one_sent, sums_one = one_back(
        depth, place, pre_a, pre_b, w_up, w_up_b, grad_two, unit_one, root_one, par
    )
    grad_one_low, one_rows, one_sent, pre_a, pre_b, hidden_rows, more_pre_a = tie(
        grad_one_low, one_rows, one_sent, pre_a, pre_b, hidden_rows, fly_pre_a
    )
    red_up = reduction(hidden_rows, pre_a, pre_b, (shared, more_pre_a, more_pre_b), 0, 0, 0)
    grad_one_low, one_rows, one_sent, red_up.kept = tie(
        grad_one_low, one_rows, one_sent, red_up.kept
    )
    more_one = across(one_sent, 1)
    grad_qkv_b, sum_qkv_b = heads_back(qkv_b, lse_b, seg, grad_one_low, w_out_b)
    grad_one_low, grad_qkv_b, more_one, one_rows = tie(
        grad_one_low, grad_qkv_b, more_one, one_rows
    )
    fly_qkv_b = across(grad_qkv_b, 1)
    red_out = reduction(
        one_rows, ctx_a, ctx_b, (more_one, shared, shared), 0, width, width + 2 * half
    )
    grad_one_low, red_out.kept = tie(grad_one_low, red_out.kept)
    grad_qkv_a, sum_qkv_a = heads_back(qkv_a, lse_a, seg, grad_one_low, w_out)
    grad_qkv_a = land(grad_qkv_a, red_down)
    blocks_of(red_down)
    grad_qkv_a, more_qkv_b, red_down.kept = land((grad_qkv_a, fly_qkv_b, red_down.kept), red_up)
    red_up.send("two")
    red_down.send("four")
    fly_qkv_a = across(grad_qkv_a, 1)
    grad_qkv_a, more_qkv_a = tie(grad_qkv_a, fly_qkv_a)
    red_qkv = reduction(
        tokens_rows, grad_qkv_a, grad_qkv_b, (shared, more_qkv_a, more_qkv_b), width // 2, 0, 0
    )
    grad_qkv_a, grad_qkv_b, red_qkv.kept = tie(grad_qkv_a, grad_qkv_b, red_qkv.kept)
    grad_in = input_back(
        grad_one, grad_qkv_a, grad_qkv_b, (w_query, w_key, w_value, w_query_b, w_key_b, w_value_b)
    )
    near = [sum_qkv_a[0, :cut], sum_qkv_a[0, 2 * cut :], sum_pre_a[0]]
    far = [sum_qkv_b[0, :cut], sum_qkv_b[0, 2 * cut :], sum_pre_b[0]]
    small = jnp.concatenate(near + far + [sums_one.reshape(-1), sums_two.reshape(-1)])
    size = 2 * cut + b_up.shape[0]
    small, grad_in = land((small, grad_in), red_up)
    blocks_of(red_up)
    red_up.send("three")
    more = across(small, 1)
    small, grad_in = land((small, grad_in), red_down)
    blocks_of(red_down)
    red_down.send("one")
    small, more, grad_in = land((small, more, grad_in), red_out)
    red_out.send("two")
    small = small + more
    small, grad_in = land((small, grad_in), red_qkv)
    red_qkv.send("two")
    more = across(small, 8)
    small, more, grad_in = land((small, more, grad_in), red_down)
    blocks_of(red_down)
    red_down.send("two")
    small = small + more
    fly_in = over(grad_in[half:])
    small = land(small, red_out)
    blocks_of(red_out)
    red_out.send("three")
    more = across(small, 4)
    small, more, output = land((small, more, output), red_qkv)
    blocks_of(red_qkv)
    red_qkv.send("three")
    small = small + more
    got = over(small[size:])
    small = jnp.concatenate([small[:size], small[2 * size :]])
    small = land(small, red_down, last=True)
    small, output = land((small, output), red_up)
    blocks_of(red_up)
    red_up.send("four")
    fly_output = over(output[half:])
    small, got = land((small, got), red_qkv)
    blocks_of(red_qkv)
    red_qkv.send("four")
    small = small + got
    got = across(small, 2)
    small, fly_in = land((small, fly_in), red_out)
    blocks_of(red_out)
    red_out.send("four")
    small, got, fly_output = tie(small, got, fly_output)
    small = small + got
    small = land(small, red_up, last=True)
    small = land(small, red_out, red_qkv, last=True)

    pieces = []
    at = 0
    for size in (cut, cut, b_up.shape[0]) + (width,) * 6:
        pieces.append(small[at : at + size])
        at += size

    def to_owners(mine, theirs):
        return jnp.where(side == 0, jnp.stack([mine, theirs]), jnp.stack([theirs, mine]))

    red_out, red_up, red_down, grad_qkv = (
        red.kept.reshape(-1, red.kept.shape[-1]) for red in (red_out, red_up, red_down, red_qkv)
    )
    return (
        to_owners(output[:half], fly_output),
        to_owners(grad_in[:half], fly_in),
        grad_qkv[:, :local],
        pieces[0],
        grad_qkv[:, local : 2 * local],
        grad_qkv[:, 2 * local :],
        pieces[1],
        red_out.T,
        pieces[3],
        pieces[4],
        pieces[5],
        red_up,
        pieces[2],
        red_down.T,
        pieces[6],
        pieces[7],
        pieces[8],
    )


def solution(mesh):
    placed = (
        P(None, ("dp", "tensor"), None),
        P(None, "dp", None),
        P(None, ("dp", "tensor"), None),
        P(None, "tensor"),
        P("tensor"),
        P(None, "tensor"),
        P(None, "tensor"),
        P("tensor"),
        P("tensor", None),
        P(),
        P(),
        P(),
        P(None, "tensor"),
        P("tensor"),
        P("tensor", None),
        P(),
        P(),
        P(),
    )
    body = on_device
    groups = mesh.shape["dp"]
    if mesh.shape["tensor"] == MICRO and groups == 16:
        body = partial(row_on_device, groups)
    return jax.shard_map(
        body,
        mesh=mesh,
        in_specs=placed,
        out_specs=(
            P(None, ("dp", "tensor"), None),
            P(None, ("dp", "tensor"), None),
            P("dp", "tensor"),
            P("tensor"),
            P("dp", "tensor"),
            P("dp", "tensor"),
            P("tensor"),
            P("tensor", "dp"),
            P(),
            P(),
            P(),
            P("dp", "tensor"),
            P("tensor"),
            P("tensor", "dp"),
            P(),
            P(),
            P(),
        ),
        check_vma=False,
    )
```

```python
from functools import partial, reduce
import math

import jax
import jax.numpy as jnp
from jax import lax
from jax.experimental import pallas as pl
from jax.experimental.pallas import tpu as pltpu
from jax.sharding import PartitionSpec as P

HD = 64
MICRO = 2


def layer_norm(inputs, scale_vec, offset):
    centre = inputs - jnp.mean(inputs, axis=-1, keepdims=True)
    spread = jnp.mean(centre * centre, axis=-1, keepdims=True)
    return centre * lax.rsqrt(spread + 1e-12) * scale_vec + offset


def gelu_exact(inputs):
    return jax.nn.gelu(inputs, approximate=False)


def matmul(former, latter):
    return jnp.dot(former, latter, preferred_element_type=jnp.float32)


def inner_rows(former, latter):
    return lax.dot_general(
        former, latter, (((0,), (0,)), ((), ())), preferred_element_type=jnp.float32
    )


def inner_cols(former, latter):
    return lax.dot_general(
        former, latter, (((1,), (1,)), ((), ())), preferred_element_type=jnp.float32
    )


def head_split(block):
    return block.reshape(block.shape[0], block.shape[1] // HD, HD)


def masked_scores(queries, key_rows, seg_row):
    scores = jnp.einsum(
        "qhd,khd->hqk",
        head_split(queries),
        head_split(key_rows),
        preferred_element_type=jnp.float32,
    ) * (1.0 / math.sqrt(HD))
    same_doc = seg_row[:, None] == seg_row[None, :]
    return jnp.where(same_doc[None], scores, -1e30)


def attend_row(packed):
    queries, key_rows, value_rows, seg_row = packed
    scores = masked_scores(queries, key_rows, seg_row)
    highest = jnp.max(scores, axis=-1, keepdims=True)
    logsum = highest + jnp.log(jnp.sum(jnp.exp(scores - highest), axis=-1, keepdims=True))
    probs_low = jnp.exp(scores - logsum).astype(jnp.bfloat16)
    context = jnp.einsum(
        "hqk,khd->qhd", probs_low, head_split(value_rows), preferred_element_type=jnp.float32
    )
    return (context.reshape(queries.shape).astype(jnp.bfloat16), logsum[..., 0])


def attend_back(packed):
    queries, key_rows, value_rows, seg_row, logsum, grad_ctx = packed
    scores = masked_scores(queries, key_rows, seg_row)
    probs = jnp.exp(scores - logsum[..., None])
    grad_heads = head_split(grad_ctx)
    grad_probs = jnp.einsum(
        "qhd,khd->hqk", grad_heads, head_split(value_rows), preferred_element_type=jnp.float32
    )
    centred = grad_probs - jnp.sum(probs * grad_probs, axis=-1, keepdims=True)
    grad_scores = (probs * centred * (1.0 / math.sqrt(HD))).astype(jnp.bfloat16)
    grad_query = jnp.einsum(
        "hqk,khd->qhd", grad_scores, head_split(key_rows), preferred_element_type=jnp.float32
    )
    grad_key = jnp.einsum(
        "hqk,qhd->khd", grad_scores, head_split(queries), preferred_element_type=jnp.float32
    )
    grad_value = jnp.einsum(
        "hqk,qhd->khd", probs.astype(jnp.bfloat16), grad_heads, preferred_element_type=jnp.float32
    )
    flat_shape = queries.shape
    return jnp.concatenate(
        [
            grad_query.reshape(flat_shape),
            grad_key.reshape(flat_shape),
            grad_value.reshape(flat_shape),
        ],
        axis=1,
    ).astype(jnp.bfloat16)


def add_trees(former, latter):
    return jax.tree.map(jnp.add, former, latter)


def on_device(
    hidden_in,
    segment_ids,
    out_grad,
    w_query,
    b_query,
    w_key,
    w_value,
    b_value,
    w_out,
    b_out,
    attn_gain,
    attn_shift,
    w_up,
    b_up,
    w_down,
    b_down,
    ffn_gain,
    ffn_shift,
):
    local_width = w_query.shape[1]
    packed_rows = segment_ids.shape[1]
    length = segment_ids.shape[2]
    w_qkv = jnp.concatenate([w_query, w_key, w_value], axis=1)
    b_qkv = jnp.concatenate([b_query, jnp.zeros_like(b_query), b_value]).astype(jnp.float32)
    b_out32 = b_out.astype(jnp.float32)
    b_up32 = b_up.astype(jnp.float32)
    b_down32 = b_down.astype(jnp.float32)
    attn_gain32 = attn_gain.astype(jnp.float32)
    attn_shift32 = attn_shift.astype(jnp.float32)
    ffn_gain32 = ffn_gain.astype(jnp.float32)
    ffn_shift32 = ffn_shift.astype(jnp.float32)

    def to_rows(block):
        return block.reshape(packed_rows, length, block.shape[1])

    outputs = []
    input_grads = []
    weight_terms = []
    small_terms = []
    for micro_step in range(MICRO):
        tokens_low = hidden_in[micro_step]
        tokens = tokens_low.astype(jnp.float32)
        seg_rows = segment_ids[micro_step]
        full_rows = lax.all_gather(tokens_low, "tensor", axis=0, tiled=True)
        qkv_low = (matmul(full_rows, w_qkv) + b_qkv).astype(jnp.bfloat16)
        queries = qkv_low[:, :local_width]
        key_rows = qkv_low[:, local_width : 2 * local_width]
        value_rows = qkv_low[:, 2 * local_width :]
        context, logsums = lax.map(
            attend_row, (to_rows(queries), to_rows(key_rows), to_rows(value_rows), seg_rows)
        )
        context = context.reshape(-1, local_width)
        attn_part = lax.psum_scatter(
            matmul(context, w_out).astype(jnp.bfloat16), "tensor", scatter_dimension=0, tiled=True
        ).astype(jnp.float32)
        resid_one = attn_part + b_out32 + tokens
        hidden_one, norm_one_back = jax.vjp(layer_norm, resid_one, attn_gain32, attn_shift32)
        hidden_low = hidden_one.astype(jnp.bfloat16)
        hidden_rows = lax.all_gather(hidden_low, "tensor", axis=0, tiled=True)
        pre_act = matmul(hidden_rows, w_up) + b_up32
        activation, gelu_back = jax.vjp(gelu_exact, pre_act)
        gelu_low = activation.astype(jnp.bfloat16)
        ffn_part = lax.psum_scatter(
            matmul(gelu_low, w_down).astype(jnp.bfloat16), "tensor", scatter_dimension=0, tiled=True
        ).astype(jnp.float32)
        resid_two = ffn_part + b_down32 + hidden_one
        result, norm_two_back = jax.vjp(layer_norm, resid_two, ffn_gain32, ffn_shift32)
        outputs.append(result.astype(jnp.bfloat16))
        grad_two, grad_ffn_gain, grad_ffn_shift = norm_two_back(
            out_grad[micro_step].astype(jnp.float32)
        )
        grad_two_low = grad_two.astype(jnp.bfloat16)
        grad_two_rows = lax.all_gather(grad_two_low, "tensor", axis=0, tiled=True)
        grad_down = inner_rows(gelu_low, grad_two_rows)
        grad_act = inner_cols(grad_two_rows, w_down)
        grad_pre = gelu_back(grad_act)[0].astype(jnp.bfloat16)
        grad_up = inner_rows(hidden_rows, grad_pre)
        grad_hidden = (
            lax.psum_scatter(
                inner_cols(grad_pre, w_up).astype(jnp.bfloat16),
                "tensor",
                scatter_dimension=0,
                tiled=True,
            ).astype(jnp.float32)
            + grad_two
        )
        grad_one, grad_attn_gain, grad_attn_shift = norm_one_back(grad_hidden)
        grad_one_low = grad_one.astype(jnp.bfloat16)
        grad_one_rows = lax.all_gather(grad_one_low, "tensor", axis=0, tiled=True)
        grad_wout = inner_rows(context, grad_one_rows)
        grad_ctx = inner_cols(grad_one_rows, w_out).astype(jnp.bfloat16)
        grad_qkv = lax.map(
            attend_back,
            (
                to_rows(queries),
                to_rows(key_rows),
                to_rows(value_rows),
                seg_rows,
                logsums,
                to_rows(grad_ctx),
            ),
        )
        grad_qkv = grad_qkv.reshape(-1, 3 * local_width)
        grad_wqkv = inner_rows(full_rows, grad_qkv)
        grad_in = (
            lax.psum_scatter(
                inner_cols(grad_qkv, w_qkv).astype(jnp.bfloat16),
                "tensor",
                scatter_dimension=0,
                tiled=True,
            ).astype(jnp.float32)
            + grad_one
        )
        input_grads.append(grad_in.astype(jnp.bfloat16))
        small_terms.append(
            (
                jnp.sum(grad_qkv.astype(jnp.float32), axis=0),
                jnp.sum(grad_pre.astype(jnp.float32), axis=0),
                jnp.sum(grad_one, axis=0),
                grad_attn_gain,
                grad_attn_shift,
                jnp.sum(grad_two, axis=0),
                grad_ffn_gain,
                grad_ffn_shift,
            )
        )
        weight_set = (grad_wqkv, grad_up, grad_wout, grad_down)
        weight_terms.append(weight_set)
    summed = reduce(add_trees, weight_terms)
    summed = (
        lax.psum_scatter(
            summed[0].astype(jnp.bfloat16), "dp", scatter_dimension=0, tiled=True
        ).astype(jnp.float32),
        lax.psum_scatter(
            summed[1].astype(jnp.bfloat16), "dp", scatter_dimension=0, tiled=True
        ).astype(jnp.float32),
        lax.psum_scatter(
            summed[2].astype(jnp.bfloat16), "dp", scatter_dimension=1, tiled=True
        ).astype(jnp.float32),
        lax.psum_scatter(
            summed[3].astype(jnp.bfloat16), "dp", scatter_dimension=1, tiled=True
        ).astype(jnp.float32),
    )
    red_qkv, red_up, red_wout, red_down = summed
    small = reduce(add_trees, small_terms)
    bias_qkv, bias_up = lax.psum((small[0], small[1]), "dp")
    norm_bout, norm_again, norm_ashift, norm_bdown, norm_fgain, norm_fshift = lax.psum(
        (small[2], small[3], small[4], small[5], small[6], small[7]), ("dp", "tensor")
    )
    output = jnp.stack(outputs, axis=0)
    grad_input = jnp.stack(input_grads, axis=0)
    return (
        output,
        grad_input,
        red_qkv[:, :local_width],
        bias_qkv[:local_width],
        red_qkv[:, local_width : 2 * local_width],
        red_qkv[:, 2 * local_width :],
        bias_qkv[2 * local_width :],
        red_wout,
        norm_bout,
        norm_again,
        norm_ashift,
        red_up,
        bias_up,
        red_down,
        norm_bdown,
        norm_fgain,
        norm_fshift,
    )


def dot_nn(former, latter):
    return jnp.dot(former, latter, preferred_element_type=jnp.float32)


def dot_tn(former, latter):
    return lax.dot_general(
        former, latter, (((0,), (0,)), ((), ())), preferred_element_type=jnp.float32
    )


def dot_nt(former, latter):
    return lax.dot_general(
        former, latter, (((1,), (1,)), ((), ())), preferred_element_type=jnp.float32
    )


def head_pair(block):
    lane = lax.broadcasted_iota(jnp.int32, block.shape, 1)
    zero = jnp.zeros_like(block)
    return (jnp.where(lane < HD, block, zero), jnp.where(lane < HD, zero, block))


def in_vmem(count):
    return [pl.BlockSpec(memory_space=pltpu.VMEM) for _ in range(count)]


def call(kernel, name, outs, *args, scalars=0, scratch=(), products=0):
    out_shape = tuple(jax.ShapeDtypeStruct(shape, dtype) for shape, dtype in outs)
    moved = sum(math.prod(a.shape) * a.dtype.itemsize for a in (*args, *out_shape))
    return pl.pallas_call(
        kernel,
        out_shape=out_shape,
        in_specs=[pl.BlockSpec(memory_space=pltpu.SMEM) for _ in range(scalars)]
        + in_vmem(len(args) - scalars),
        out_specs=tuple(in_vmem(len(outs))),
        scratch_shapes=list(scratch),
        compiler_params=pltpu.CompilerParams(vmem_limit_bytes=8 << 20),
        cost_estimate=pl.CostEstimate(
            flops=2 * products, transcendentals=0, bytes_accessed=moved
        ),
        name=name,
    )(*args)


def pieces_of(total, most):
    return [slice(at, min(at + most, total)) for at in range(0, total, most)]


def low(block):
    return block.astype(jnp.bfloat16)


def wide(block):
    return block.astype(jnp.float32)


def heads_kernel(
    seg_col_ref, seg_row_ref, x_ref, wq_ref, wk_ref, wv_ref, bias_ref,
    q_ref, k_ref, v_ref, ctx_ref, lse_ref, mask_ref,
):
    mask_ref[...] = jnp.where(seg_col_ref[...] == seg_row_ref[...], 0.0, -1e30)
    for rows in pieces_of(x_ref.shape[0], 256):
        x = x_ref[rows, :]
        for cols in pieces_of(wq_ref.shape[1], 256):
            q_ref[rows, cols] = low(dot_nn(x, wq_ref[:, cols]) + bias_ref[0:1, cols])
            k_ref[rows, cols] = low(dot_nn(x, wk_ref[:, cols]))
            v_ref[rows, cols] = low(dot_nn(x, wv_ref[:, cols]) + bias_ref[1:2, cols])
    for i in range(q_ref.shape[1] // (2 * HD)):
        cols = slice(2 * HD * i, 2 * HD * (i + 1))
        q_pair = q_ref[:, cols] * jnp.bfloat16(1.0 / math.sqrt(HD))
        outs = []
        for h, q_one in enumerate(head_pair(q_pair)):
            scores = dot_nt(k_ref[:, cols], q_one) + mask_ref[...]
            highest = jnp.max(scores, axis=0, keepdims=True)
            raised = jnp.exp(scores - highest)
            total = jnp.sum(raised, axis=0, keepdims=True)
            lse_ref[i, h : h + 1, :] = highest + jnp.log(total)
            mixed = dot_tn(v_ref[:, cols], low(raised))
            outs.append(mixed[h * HD : (h + 1) * HD] * (1.0 / total))
        ctx_ref[:, cols] = low(jnp.concatenate(outs, axis=0).T)


def heads(x, w_q, w_k, w_v, bias, seg):
    length, width = x.shape[0], w_q.shape[1]
    flat = ((length, width), jnp.bfloat16)
    return call(
        heads_kernel,
        "heads",
        (flat, flat, flat, flat, ((width // (2 * HD), 2, length), jnp.float32)),
        seg[:, None], seg[None, :], x, w_q, w_k, w_v, bias,
        products=length * width * (3 * x.shape[1] + 2 * length),
        scratch=[pltpu.VMEM((length, length), jnp.float32)],
    )


def heads_back_kernel(
    seg_col_ref, seg_row_ref, q_ref, k_ref, v_ref, lse_ref, g_ref, w_ref,
    grad_ref, sum_ref, ctx_ref, mask_ref,
):
    mask_ref[...] = jnp.where(seg_col_ref[...] == seg_row_ref[...], 0.0, -1e30)
    scale = 1.0 / math.sqrt(HD)
    width = q_ref.shape[1]
    for rows in pieces_of(g_ref.shape[0], 256):
        for cols in pieces_of(width, 256):
            ctx_ref[rows, cols] = low(dot_nt(g_ref[rows, :], w_ref[cols, :]))
    for i in range(width // (2 * HD)):
        cols = slice(2 * HD * i, 2 * HD * (i + 1))
        q_pair = q_ref[:, cols] * jnp.bfloat16(scale)
        grad_q, grad_k, grad_v = [], 0.0, 0.0
        for h, (q_one, g_one) in enumerate(zip(head_pair(q_pair), head_pair(ctx_ref[:, cols]))):
            scores = dot_nt(k_ref[:, cols], q_one) + mask_ref[...]
            probs = jnp.exp(scores - lse_ref[i, h : h + 1, :])
            grad_p = dot_nt(v_ref[:, cols], g_one)
            delta = jnp.sum(probs * grad_p, axis=0, keepdims=True)
            grad_s = low(probs * (grad_p - delta))
            grad_v = grad_v + dot_nn(low(probs), g_one)
            grad_k = grad_k + dot_nn(grad_s, q_one)
            grad_q.append(dot_tn(k_ref[:, cols], grad_s)[h * HD : (h + 1) * HD])
        grad_q = (jnp.concatenate(grad_q, axis=0) * scale).T
        for n, grad in enumerate((grad_q, grad_k, grad_v)):
            there = slice(n * width + 2 * HD * i, n * width + 2 * HD * (i + 1))
            grad = low(grad)
            grad_ref[:, there] = grad
            sum_ref[:, there] = jnp.sum(wide(grad), axis=0, keepdims=True)


def heads_back(qkv, lse, seg, grad_one_low, w_out):
    length, width = qkv[0].shape
    return call(
        heads_back_kernel,
        "heads_back",
        (((length, 3 * width), jnp.bfloat16), ((1, 3 * width), jnp.float32)),
        seg[:, None], seg[None, :], *qkv, lse, grad_one_low, w_out,
        products=length * width * (w_out.shape[1] + 5 * length),
        scratch=[
            pltpu.VMEM((length, width), jnp.bfloat16),
            pltpu.VMEM((length, length), jnp.float32),
        ],
    )


B_OUT, GAIN_ONE, SHIFT_ONE, B_DOWN, GAIN_TWO, SHIFT_TWO = range(6)


def row_of(ref, row):
    return ref[row : row + 1, :]


def row_norm(resid):
    centre = resid - jnp.mean(resid, axis=-1, keepdims=True)
    root = lax.rsqrt(jnp.mean(centre * centre, axis=-1, keepdims=True) + 1e-12)
    return centre * root, root


def row_norm_back(grad, gain, unit, root):
    inner = grad * gain
    mean = jnp.mean(inner, axis=-1, keepdims=True)
    along = jnp.mean(inner * unit, axis=-1, keepdims=True)
    return root * (inner - mean - unit * along)


def store_turned(depth, place, block, spare_ref, keep_ref, send_ref, base, cols):
    rows = block.shape[1] >> depth
    spare_ref[...] = block.T
    core = place & 1
    for pair in range(1 << (depth - 1)):
        step = pair ^ (place >> 1)
        bits = [(step >> bit) & 1 for bit in range(depth - 1)]
        for owner, ref, start in ((core, keep_ref, 0), (1 - core, send_ref, base)):
            first = jnp.where(owner == 0, bits[1], bits[2])
            second = jnp.where(owner == 0, bits[2], bits[1])
            where = ((bits[0] * 2 + first) * 2 + second) * rows + start
            source = pl.multiple_of((2 * pair + owner) * rows, 16)
            ref[pl.ds(pl.multiple_of(where, 16), rows), cols] = spare_ref[pl.ds(source, rows), :]


def norm_one_kernel(
    depth, place_ref, ctx_a_ref, ctx_b_ref, w_a_ref, w_b_ref, x_ref, par_ref,
    unit_ref, root_ref, low_ref, hidden_ref, tokens_ref, send_ref, sum_ref, spare_ref,
):
    for cols in pieces_of(x_ref.shape[1], 256):
        sum_ref[:, cols] = dot_nn(ctx_a_ref[...], w_a_ref[:, cols]) + dot_nn(
            ctx_b_ref[...], w_b_ref[:, cols]
        )
    for rows in pieces_of(x_ref.shape[0], 128):
        x = x_ref[rows, :]
        unit, root = row_norm(sum_ref[rows, :] + row_of(par_ref, B_OUT) + wide(x))
        unit_ref[rows, :] = unit
        root_ref[rows, :] = root
        hidden = low(unit * row_of(par_ref, GAIN_ONE) + row_of(par_ref, SHIFT_ONE))
        low_ref[rows, :] = hidden
        keep = hidden_ref.shape[0]
        store_turned(depth, place_ref[0], hidden, spare_ref, hidden_ref, send_ref, 0, rows)
        store_turned(depth, place_ref[0], x, spare_ref, tokens_ref, send_ref, keep, rows)
    send_ref[2 * keep : 2 * keep + ctx_a_ref.shape[0], :] = ctx_a_ref[...]
    send_ref[2 * keep + ctx_a_ref.shape[0] :, :] = ctx_b_ref[...]


def norm_one(depth, place, ctx_a, ctx_b, w_a, w_b, x, par):
    length, width = x.shape
    kept = ((width // 2, length), jnp.bfloat16)
    return call(
        partial(norm_one_kernel, depth),
        "norm_one",
        (
            (x.shape, jnp.float32),
            ((length, 1), jnp.float32),
            (x.shape, jnp.bfloat16),
            kept,
            kept,
            ((width + 2 * length, length), jnp.bfloat16),
        ),
        place.reshape(1), ctx_a, ctx_b, w_a, w_b, x, par,
        scalars=1,
        scratch=[pltpu.VMEM(x.shape, jnp.float32), pltpu.VMEM((width, 128), jnp.bfloat16)],
        products=2 * ctx_a.shape[0] * w_a.shape[0] * w_a.shape[1],
    )


def up_kernel(x_ref, w_ref, bias_ref, act_ref, slope_ref):
    for cols in pieces_of(w_ref.shape[1], 256):
        at = cols.start % bias_ref.shape[1]
        row = 2 + cols.start // bias_ref.shape[1]
        bias = bias_ref[row : row + 1, at : at + 256]
        for rows in pieces_of(x_ref.shape[0], 256):
            pre = dot_nn(x_ref[rows, :], w_ref[:, cols]) + bias
            act_ref[rows, cols], slope_ref[rows, cols] = gelu_pair(pre)


def up(x, w, bias):
    flat = ((x.shape[0], w.shape[1]), jnp.bfloat16)
    products = x.shape[0] * w.shape[0] * w.shape[1]
    return call(up_kernel, "up", (flat, flat), x, w, bias, products=products)


def down_kernel(act_ref, w_ref, out_ref):
    for rows in pieces_of(act_ref.shape[0], 256):
        for cols in pieces_of(w_ref.shape[1], 256):
            out_ref[rows, cols] = dot_nn(act_ref[rows, :], w_ref[:, cols])


def down(act, w):
    out = ((act.shape[0], w.shape[1]), jnp.float32)
    products = act.shape[0] * w.shape[0] * w.shape[1]
    return call(down_kernel, "down", (out,), act, w, products=products)[0]


def norm_two_kernel(
    depth, place_ref, ffn_ref, act_ref, w_ref, unit_one_ref, par_ref, grad_ref,
    out_ref, two_ref, low_ref, keep_ref, send_ref, sum_ref, spare_ref,
):
    for cols in pieces_of(w_ref.shape[1], 256):
        two_ref[:, cols] = ffn_ref[:, cols] + dot_nn(act_ref[...], w_ref[:, cols])
    sum_ref[...] = jnp.zeros_like(sum_ref)
    for rows in pieces_of(act_ref.shape[0], 128):
        hidden = unit_one_ref[rows, :] * row_of(par_ref, GAIN_ONE) + row_of(par_ref, SHIFT_ONE)
        unit, root = row_norm(two_ref[rows, :] + row_of(par_ref, B_DOWN) + hidden)
        gain = row_of(par_ref, GAIN_TWO)
        out_ref[rows, :] = low(unit * gain + row_of(par_ref, SHIFT_TWO))
        grad = wide(grad_ref[rows, :])
        two = row_norm_back(grad, gain, unit, root)
        two_ref[rows, :] = two
        two_low = low(two)
        low_ref[rows, :] = two_low
        store_turned(depth, place_ref[0], two_low, spare_ref, keep_ref, send_ref, 0, rows)
        for i, term in enumerate((two, grad * unit, grad)):
            sum_ref[i : i + 1, :] += jnp.sum(term, axis=0, keepdims=True)


def norm_two(depth, place, ffn, act, w, unit_one, par, grad_out):
    shape = grad_out.shape
    flat, kept = (shape, jnp.bfloat16), ((shape[1] // 2, shape[0]), jnp.bfloat16)
    return call(
        partial(norm_two_kernel, depth),
        "norm_two",
        (flat, (shape, jnp.float32), flat, kept, kept, ((3, shape[1]), jnp.float32)),
        place.reshape(1), ffn, act, w, unit_one, par, grad_out,
        scalars=1,
        scratch=[pltpu.VMEM((shape[1], 128), jnp.bfloat16)],
        products=act.shape[0] * w.shape[0] * w.shape[1],
    )


def pre_kernel(grad_ref, w_ref, slope_ref, out_ref, sum_ref):
    for cols in pieces_of(w_ref.shape[0], 256):
        total = 0.0
        for rows in pieces_of(grad_ref.shape[0], 256):
            grad = low(dot_nt(grad_ref[rows, :], w_ref[cols, :]) * wide(slope_ref[rows, cols]))
            out_ref[rows, cols] = grad
            total = total + jnp.sum(wide(grad), axis=0, keepdims=True)
        sum_ref[:, cols] = total


def pre_back(grad, w, slope):
    return call(
        pre_kernel, "pre_back", ((slope.shape, jnp.bfloat16), ((1, slope.shape[1]), jnp.float32)),
        grad, w, slope,
        products=grad.shape[0] * w.shape[0] * w.shape[1],
    )


def one_kernel(
    depth, place_ref, pre_a_ref, pre_b_ref, w_a_ref, w_b_ref, two_ref, unit_ref, root_ref, par_ref,
    one_ref, low_ref, keep_ref, send_ref, sum_ref, spare_ref,
):
    for cols in pieces_of(one_ref.shape[1], 256):
        one_ref[:, cols] = dot_nt(pre_a_ref[...], w_a_ref[cols, :]) + dot_nt(
            pre_b_ref[...], w_b_ref[cols, :]
        )
    sum_ref[...] = jnp.zeros_like(sum_ref)
    for rows in pieces_of(pre_a_ref.shape[0], 128):
        grad = one_ref[rows, :] + two_ref[rows, :]
        unit = unit_ref[rows, :]
        one = row_norm_back(grad, row_of(par_ref, GAIN_ONE), unit, root_ref[rows, :])
        one_ref[rows, :] = one
        one_low = low(one)
        low_ref[rows, :] = one_low
        store_turned(depth, place_ref[0], one_low, spare_ref, keep_ref, send_ref, 0, rows)
        for i, term in enumerate((one, grad * unit, grad)):
            sum_ref[i : i + 1, :] += jnp.sum(term, axis=0, keepdims=True)


def one_back(depth, place, pre_a, pre_b, w_a, w_b, two, unit, root, par):
    shape = two.shape
    return call(
        partial(one_kernel, depth),
        "one_back",
        (
            (shape, jnp.float32),
            (shape, jnp.bfloat16),
            ((shape[1] // 2, shape[0]), jnp.bfloat16),
            ((shape[1] // 2, shape[0]), jnp.bfloat16),
            ((3, shape[1]), jnp.float32),
        ),
        place.reshape(1), pre_a, pre_b, w_a, w_b, two, unit, root, par,
        scalars=1,
        scratch=[pltpu.VMEM((shape[1], 128), jnp.bfloat16)],
        products=2 * pre_a.shape[0] * w_a.shape[0] * w_a.shape[1],
    )


def input_kernel(one_ref, a_ref, b_ref, *refs):
    weights, out_ref = refs[:6], refs[6]
    width = weights[0].shape[1]
    for rows in pieces_of(one_ref.shape[0], 256):
        for cols in pieces_of(one_ref.shape[1], 256):
            total = one_ref[rows, cols]
            for i, w_ref in enumerate(weights):
                grad_ref = (a_ref, b_ref)[i // 3]
                part = slice((i % 3) * width, (i % 3 + 1) * width)
                total = total + dot_nt(grad_ref[rows, part], w_ref[cols, :])
            out_ref[rows, cols] = low(total)


def input_back(grad_one, grad_a, grad_b, weights):
    return call(
        input_kernel, "input_back", ((grad_one.shape, jnp.bfloat16),),
        grad_one, grad_a, grad_b, *weights,
        products=2 * grad_a.shape[0] * grad_a.shape[1] * grad_one.shape[1],
    )[0]


def take_kernel(index_ref, *refs):
    weights, (one_ref, up_ref, down_ref), sems = refs[:6], refs[6:9], refs[9]
    copies = []

    def start(source, target):
        copies.append(pltpu.make_async_copy(source, target, sems.at[len(copies)]))
        copies[-1].start()

    def rows_of(ref):
        rows = ref.shape[0] // 8
        return pl.ds(pl.multiple_of(index_ref[0] * rows, 16), rows)

    at = 0
    cols = one_ref.shape[1]
    for ref in weights[:4]:
        rows = ref.shape[0] // 8
        for col in range(0, ref.shape[1], cols):
            start(ref.at[rows_of(ref), col : col + cols], one_ref.at[at : at + rows])
            at += rows
    start(weights[4].at[rows_of(weights[4])], up_ref)
    rows = weights[5].shape[0] // 4
    start(weights[5].at[pl.ds(pl.multiple_of(index_ref[8] * rows, 16), rows)], down_ref)
    for copy in copies:
        copy.wait()


def take(indices, weights):
    blocks = [(w.shape[0] // 8, w.shape[1]) for w in weights]
    local = blocks[0][1]
    one = (sum(rows * cols for rows, cols in blocks[:4]) // local, local)
    shapes = [one, blocks[4], (2 * blocks[5][0], blocks[5][1])]
    parts = sum(cols // local for _, cols in blocks[:4]) + 2
    return pl.pallas_call(
        take_kernel,
        in_specs=[pl.BlockSpec(memory_space=pltpu.SMEM)]
        + [pl.BlockSpec(memory_space=pltpu.HBM) for _ in weights],
        out_specs=tuple(in_vmem(3)),
        out_shape=tuple(jax.ShapeDtypeStruct(shape, jnp.bfloat16) for shape in shapes),
        scratch_shapes=[pltpu.SemaphoreType.DMA((parts,))],
        cost_estimate=pl.CostEstimate(
            flops=0, transcendentals=0, bytes_accessed=4 * sum(r * c for r, c in shapes)
        ),
        compiler_params=pltpu.CompilerParams(vmem_limit_bytes=8 << 20),
        name="take",
    )(indices, *weights)


def kept_kernel(starts, core_ref, rows_ref, near_ref, far_ref, more_rows_ref, more_near_ref, more_far_ref, kept_ref, sent_ref):
    half = rows_ref.shape[0] // 2
    length = near_ref.shape[0]
    pairs = ((near_ref, more_near_ref, starts[1]), (far_ref, more_far_ref, starts[2]))

    def part(row, side, cols):
        ref, more_ref, start = pairs[side]
        rows, more = slice(row * half, (row + 1) * half), starts[0] + row * half
        total = dot_nn(rows_ref[rows, :], ref[:, cols])
        return low(
            total
            + dot_nn(more_rows_ref[more : more + half, :], more_ref[start : start + length, cols])
        )

    for cols in pieces_of(near_ref.shape[1], 512):
        kept_ref[0, :, cols] = part(0, 0, cols)
        sent_ref[1, :, cols] = part(1, 1, cols)
        one, two = part(1, 0, cols), part(0, 1, cols)

        @pl.when(core_ref[0] == 0)
        def _():
            kept_ref[1, :, cols] = one
            sent_ref[0, :, cols] = two

        @pl.when(core_ref[0] != 0)
        def _():
            kept_ref[1, :, cols] = two
            sent_ref[0, :, cols] = one


def far_kernel(core_ref, rows_ref, near_ref, far_ref, more_rows_ref, more_near_ref, more_far_ref, kept_ref, sent_ref):
    half = rows_ref.shape[0] // 2
    part = half // 4
    pairs = ((near_ref, more_near_ref), (far_ref, more_far_ref))
    for cols in pieces_of(near_ref.shape[1], 512):
        for row in range(2):
            rows = slice(row * half, (row + 1) * half)
            for side, (ref, more_ref) in enumerate(pairs):
                total = dot_nn(rows_ref[rows, :], ref[:, cols])
                total = low(total + dot_nn(more_rows_ref[rows, :], more_ref[:, cols]))
                first = jnp.where(core_ref[0] == 0, side, row)
                second = jnp.where(core_ref[0] == 0, row, side)
                for n in range(2):
                    kept_ref[n, first, second, :, cols] = total[n * part : (n + 1) * part]
                    sent_ref[n, first, second, :, cols] = total[(2 + n) * part : (3 + n) * part]


def grad_kept_far(core, rows, near, far, more):
    shape = ((2, 2, 2, rows.shape[0] // 8, near.shape[1]), jnp.bfloat16)
    return call(
        far_kernel, "grad_kept_far", (shape, shape), core.reshape(1), rows, near, far, *more,
        scalars=1,
        products=4 * rows.shape[0] * near.shape[0] * near.shape[1],
    )


def grad_kept(core, rows, near, far, more, starts):
    shape = ((2, rows.shape[0] // 2, near.shape[1]), jnp.bfloat16)
    return call(
        partial(kept_kernel, starts), "grad_kept", (shape, shape),
        core.reshape(1), rows, near, far, *more,
        scalars=1,
        products=4 * rows.shape[0] * near.shape[0] * near.shape[1],
    )


def gelu_pair(pre):
    cdf = 0.5 * (1.0 + lax.erf(pre * (1.0 / math.sqrt(2.0))))
    pdf = jnp.exp(-0.5 * pre * pre) * (1.0 / math.sqrt(2.0 * math.pi))
    return (pre * cdf).astype(jnp.bfloat16), (cdf + pre * pdf).astype(jnp.bfloat16)


def lay_kernel(layout, index_ref, *refs):
    ins, outs = refs[: len(layout)], refs[len(layout) :]
    for source, places in zip(ins, layout):
        for slot, unit, at, rows, which, col in places:
            offset = pl.multiple_of(index_ref[slot] * unit, 16)
            outs[which][pl.ds(offset, rows), col : col + source.shape[1]] = source[
                at : at + rows, :
            ]


def lay(indices, sources, layout, shapes):
    outs = tuple((shape, jnp.bfloat16) for shape in shapes)
    return call(partial(lay_kernel, layout), "lay", outs, indices, *sources, scalars=1)


def tie(*values):
    return lax.optimization_barrier(values)


def add_low(former, latter):
    return (former.astype(jnp.float32) + latter.astype(jnp.float32)).astype(jnp.bfloat16)


class Reduction:
    def __init__(self, kept, sent, step, send_over):
        self.kept = kept
        self.send_over = send_over
        self.flying = send_over(sent, step)

    def send(self, step):
        rows = self.kept.shape[0] // 2
        self.flying = self.send_over(self.kept[rows:], step)
        self.kept = self.kept[:rows]

    def land(self, last=False):
        total = self.kept.astype(jnp.float32) + self.flying.astype(jnp.float32)
        self.kept = total if last else total.astype(jnp.bfloat16)
        self.flying = None


def row_on_device(
    groups,
    hidden_in,
    segment_ids,
    out_grad,
    w_query,
    b_query,
    w_key,
    w_value,
    b_value,
    w_out,
    b_out,
    attn_gain,
    attn_shift,
    w_up,
    b_up,
    w_down,
    b_down,
    ffn_gain,
    ffn_shift,
):
    side = lax.axis_index("tensor")
    place = lax.axis_index("dp")
    half = hidden_in.shape[1]
    width = hidden_in.shape[2]
    local = w_query.shape[1]
    depth = groups.bit_length() - 1
    f32 = jnp.float32
    bf16 = jnp.bfloat16

    def over(block):
        return lax.ppermute(block, "tensor", [(0, 1), (1, 0)])

    def across(block, mask):
        return lax.ppermute(block, "dp", [(i, i ^ mask) for i in range(groups)])

    sides = 2

    def by_core(block, ways):
        pairs = []
        for i in range(groups):
            mask, flip = ways[i & 1]
            pairs += [(i * sides + s, (i ^ mask) * sides + (s ^ flip)) for s in range(sides)]
        return lax.ppermute(block, ("dp", "tensor"), pairs)

    ways = {
        "one": ((0, 1), (2, 0)),
        "two": ((2, 0), (0, 1)),
        "near": ((2, 0), (4, 0)),
        "far": ((4, 0), (2, 0)),
        "three": ((4, 0), (8, 0)),
        "four": ((8, 0), (4, 0)),
    }

    def send(block, step):
        return across(block, 1 << step) if isinstance(step, int) else by_core(block, ways[step])

    def pick(pair):
        return lax.dynamic_index_in_dim(pair, side, 0, keepdims=False), lax.dynamic_index_in_dim(
            pair, 1 - side, 0, keepdims=False
        )

    core = place & 1
    eighth = place & 7
    first, second = 2 << core, 4 >> core
    low_bit, high_bit = (place >> 1) & 1, 2 + ((place >> 2) & 1)
    quarter = jnp.where(core == 0, low_bit, high_bit)
    other = jnp.where(core == 0, high_bit, low_bit)
    indices = jnp.stack(
        [eighth ^ mask for mask in (0, first, second, 6, 1, second ^ 1, first ^ 1, 7)]
        + [quarter, quarter ^ 1, other, other ^ 1]
    )
    eighths = ((0, 1), (2, 3), (4, 5), (6, 7))

    def second_hop(piece, got):
        held = jnp.concatenate([piece, got], axis=0)
        return held, send(held, "far")

    def gathered(sources, slots, cuts, shapes):
        layout = []
        for source in slots:
            rows = sources[len(layout)].shape[0] // len(source)
            layout.append(
                tuple(
                    (slot, unit, i * rows + at, count, which, col)
                    for i, slot in enumerate(source)
                    for at, count, unit, which, col in cuts
                )
            )
        return lay(indices, sources, tuple(layout), shapes)

    tokens_own, tokens_away = pick(hidden_in)
    tokens_away, indices = tie(tokens_away, indices)
    fly_tokens = over(tokens_away)
    piece_one, piece_up, piece_down = take(indices, (w_query, w_key, w_value, w_out, w_up, w_down))
    fly_one = over(piece_one)
    biases = jnp.concatenate([b_query, b_value, b_up])
    par = jnp.stack([b_out, attn_gain, attn_shift, b_down, ffn_gain, ffn_shift]).astype(f32)
    seg_own, _ = pick(segment_ids[:, 0])
    seg = jnp.where(
        side == 0, seg_own, jnp.concatenate([seg_own[half:], seg_own[:half]], axis=0)
    )
    cut = b_query.shape[0]
    tokens_got, biases, piece_up, par, seg = tie(fly_tokens, biases, piece_up, par, seg)
    fly_biases = over(biases)
    biases = biases.reshape(-1, cut).astype(f32)
    tokens_low = jnp.concatenate([tokens_own, tokens_got], axis=0)
    *qkv_a, ctx_a, lse_a = heads(tokens_low, w_query, w_key, w_value, biases, seg)
    ctx_a, one, biases_b, piece_up, piece_down = tie(
        ctx_a, fly_one, fly_biases, piece_up, piece_down
    )
    biases_b = biases_b.reshape(-1, cut).astype(f32)
    fly_one = send(one, "near")
    fly_up_x = over(piece_up)
    ctx_a, fly_one, up_piece, piece_down = tie(ctx_a, fly_one, fly_up_x, piece_down)
    one_held, fly_one = second_hop(one, fly_one)
    one_core = across(one_held, 1)
    fly_up = send(up_piece, "near")
    part = piece_down.shape[0] * 11 // 16
    fly_down_a = over(piece_down[:part])
    ctx_a, one_last, one_core, fly_up, down_a, piece_down = tie(
        ctx_a, fly_one, one_core, fly_up, fly_down_a, piece_down
    )
    one_last_core = across(one_last, 1)
    up_held, fly_up = second_hop(up_piece, fly_up)
    up_core = across(up_held, 1)
    fly_down_b = over(piece_down[part:])
    one_last_core, ctx_a = tie(one_last_core, ctx_a)
    rows = width // 8
    small_rows = local // 8
    w_query_b, w_key_b, w_value_b, w_out_b = gathered(
        (one_held, one_last, one_core, one_last_core),
        eighths,
        tuple((i * rows, rows, rows, i, 0) for i in range(3))
        + tuple(
            (3 * rows + i * small_rows, small_rows, small_rows, 3, i * local)
            for i in range(width // local)
        ),
        (w_query.shape, w_key.shape, w_value.shape, w_out.shape),
    )
    *qkv_b, ctx_b, lse_b = heads(tokens_low, w_query_b, w_key_b, w_value_b, biases_b, seg)
    ctx_b, up_last, up_core, down_b, out_grad = tie(ctx_b, fly_up, up_core, fly_down_b, out_grad)
    up_last_core = across(up_last, 1)
    down_piece = jnp.concatenate([down_a, down_b], axis=0)
    fly_down = send(down_piece, "near")
    down_core = across(down_piece, 1)
    grads_own, grads_away = pick(out_grad)
    fly_grads = over(grads_away)
    unit_one, root_one, hidden_low, hidden_rows, tokens_rows, shared = norm_one(
        depth, place, ctx_a, ctx_b, w_out, w_out_b, tokens_low, par
    )
    act_a, slope_a = up(hidden_low, w_up, biases)
    ffn_a = down(act_a, w_down)
    ffn_a, up_last_core, hidden_low, fly_down, fly_grads = tie(
        ffn_a, up_last_core, hidden_low, fly_down, fly_grads
    )
    down_last_core = across(fly_down, 1)
    (w_up_b,) = gathered(
        (up_held, up_last, up_core, up_last_core),
        eighths,
        ((0, rows, rows, 0, 0),),
        (w_up.shape,),
    )
    act_b, slope_b = up(hidden_low, w_up_b, biases_b)
    act_b, act_a, down_core, down_last_core, shared = tie(
        act_b, act_a, down_core, down_last_core, shared
    )
    fly_act_a = across(act_a, 1)
    fly_act_b = across(act_b, 1)
    fly_shared = across(shared, 1)
    part = w_down.shape[0] // 4
    (w_down_b,) = gathered(
        (down_piece, fly_down, down_core, down_last_core),
        ((8,), (9,), (10,), (11,)),
        ((0, part, part, 0, 0),),
        (w_down.shape,),
    )
    grad_out = jnp.concatenate([grads_own, fly_grads], axis=0)
    output, grad_two, grad_two_low, two_rows, two_sent, sums_two = norm_two(
        depth, place, ffn_a, act_b, w_down_b, unit_one, par, grad_out
    )

    def land(carry, *reductions, last=False):
        carry, flying = tie(carry, [red.flying for red in reductions])
        for red, got in zip(reductions, flying):
            red.flying = got
            red.land(last)
        return carry

    def reduction(rows, near, far, more, *starts):
        kept, sent = tie(*grad_kept(core, rows, near, far, more, starts))
        return Reduction(kept, sent, "one", send)

    def blocks_of(red):
        kept = red.kept.reshape(-1, red.kept.shape[-1])
        red.kept = kept.reshape(2, kept.shape[0] // 2, kept.shape[1])

    two_rows, two_sent, grad_two_low, more_act_a, more_act_b = tie(
        two_rows, two_sent, grad_two_low, fly_act_a, fly_act_b
    )
    more_two = across(two_sent, 1)
    pre_b, sum_pre_b = pre_back(grad_two_low, w_down_b, slope_b)
    pre_b, grad_two_low, shared = tie(pre_b, grad_two_low, fly_shared)
    fly_pre_b = across(pre_b, 1)
    pre_a, sum_pre_a = pre_back(grad_two_low, w_down, slope_a)
    two_rows, more_two, pre_a = tie(two_rows, more_two, pre_a)
    kept, sent = tie(
        *grad_kept_far(core, two_rows, act_a, act_b, (more_two, more_act_a, more_act_b))
    )
    red_down = Reduction(kept, sent, "three", send)
    pre_a, red_down.kept, more_pre_b = tie(pre_a, red_down.kept, fly_pre_b)
    fly_pre_a = across(pre_a, 1)
    grad_one, grad_one_low, one_rows, one_sent, sums_one = one_back(
        depth, place, pre_a, pre_b, w_up, w_up_b, grad_two, unit_one, root_one, par
    )
    grad_one_low, one_rows, one_sent, pre_a, pre_b, hidden_rows, more_pre_a = tie(
        grad_one_low, one_rows, one_sent, pre_a, pre_b, hidden_rows, fly_pre_a
    )
    red_up = reduction(hidden_rows, pre_a, pre_b, (shared, more_pre_a, more_pre_b), 0, 0, 0)
    grad_one_low, one_rows, one_sent, red_up.kept = tie(
        grad_one_low, one_rows, one_sent, red_up.kept
    )
    more_one = across(one_sent, 1)
    grad_qkv_b, sum_qkv_b = heads_back(qkv_b, lse_b, seg, grad_one_low, w_out_b)
    grad_one_low, grad_qkv_b, more_one, one_rows = tie(
        grad_one_low, grad_qkv_b, more_one, one_rows
    )
    fly_qkv_b = across(grad_qkv_b, 1)
    red_out = reduction(
        one_rows, ctx_a, ctx_b, (more_one, shared, shared), 0, width, width + 2 * half
    )
    grad_one_low, red_out.kept = tie(grad_one_low, red_out.kept)
    grad_qkv_a, sum_qkv_a = heads_back(qkv_a, lse_a, seg, grad_one_low, w_out)
    grad_qkv_a = land(grad_qkv_a, red_down)
    blocks_of(red_down)
    grad_qkv_a, more_qkv_b, red_down.kept = land((grad_qkv_a, fly_qkv_b, red_down.kept), red_up)
    red_up.send("two")
    red_down.send("four")
    fly_qkv_a = across(grad_qkv_a, 1)
    grad_qkv_a, more_qkv_a = tie(grad_qkv_a, fly_qkv_a)
    red_qkv = reduction(
        tokens_rows, grad_qkv_a, grad_qkv_b, (shared, more_qkv_a, more_qkv_b), width // 2, 0, 0
    )
    grad_qkv_a, grad_qkv_b, red_qkv.kept = tie(grad_qkv_a, grad_qkv_b, red_qkv.kept)
    grad_in = input_back(
        grad_one, grad_qkv_a, grad_qkv_b, (w_query, w_key, w_value, w_query_b, w_key_b, w_value_b)
    )
    near = [sum_qkv_a[0, :cut], sum_qkv_a[0, 2 * cut :], sum_pre_a[0]]
    far = [sum_qkv_b[0, :cut], sum_qkv_b[0, 2 * cut :], sum_pre_b[0]]
    small = jnp.concatenate(near + far + [sums_one.reshape(-1), sums_two.reshape(-1)])
    size = 2 * cut + b_up.shape[0]
    small, grad_in = land((small, grad_in), red_up)
    blocks_of(red_up)
    red_up.send("three")
    more = across(small, 1)
    small, grad_in = land((small, grad_in), red_down)
    blocks_of(red_down)
    red_down.send("one")
    small, more, grad_in = land((small, more, grad_in), red_out)
    red_out.send("two")
    small = small + more
    small, grad_in = land((small, grad_in), red_qkv)
    red_qkv.send("two")
    more = across(small, 8)
    small, more, grad_in = land((small, more, grad_in), red_down)
    blocks_of(red_down)
    red_down.send("two")
    small = small + more
    fly_in = over(grad_in[half:])
    small = land(small, red_out)
    blocks_of(red_out)
    red_out.send("three")
    small, output = land((small, output), red_qkv)
    blocks_of(red_qkv)
    red_qkv.send("three")
    more = across(small, 4)
    small = land(small, red_down, last=True)
    small, more, output = land((small, more, output), red_up)
    blocks_of(red_up)
    red_up.send("four")
    fly_output = over(output[half:])
    small = small + more
    got = over(small[size:])
    small = jnp.concatenate([small[:size], small[2 * size :]])
    small, got = land((small, got), red_qkv)
    blocks_of(red_qkv)
    red_qkv.send("four")
    small = small + got
    got = across(small, 2)
    small, fly_in = land((small, fly_in), red_out)
    blocks_of(red_out)
    red_out.send("four")
    small, got, fly_output = tie(small, got, fly_output)
    small = small + got
    small = land(small, red_up, last=True)

    pieces = []
    at = 0
    for size in (cut, cut, b_up.shape[0]) + (width,) * 6:
        pieces.append(small[at : at + size])
        at += size

    def to_owners(mine, theirs):
        return jnp.where(side == 0, jnp.stack([mine, theirs]), jnp.stack([theirs, mine]))

    output = to_owners(output[:half], fly_output)
    grad_in = to_owners(grad_in[:half], fly_in)
    pieces, output, grad_in = land((pieces, output, grad_in), red_out, red_qkv, last=True)
    red_out, red_up, red_down, grad_qkv = (
        red.kept.reshape(-1, red.kept.shape[-1]) for red in (red_out, red_up, red_down, red_qkv)
    )
    return (
        output,
        grad_in,
        grad_qkv[:, :local],
        pieces[0],
        grad_qkv[:, local : 2 * local],
        grad_qkv[:, 2 * local :],
        pieces[1],
        red_out.T,
        pieces[3],
        pieces[4],
        pieces[5],
        red_up,
        pieces[2],
        red_down.T,
        pieces[6],
        pieces[7],
        pieces[8],
    )


def solution(mesh):
    placed = (
        P(None, ("dp", "tensor"), None),
        P(None, "dp", None),
        P(None, ("dp", "tensor"), None),
        P(None, "tensor"),
        P("tensor"),
        P(None, "tensor"),
        P(None, "tensor"),
        P("tensor"),
        P("tensor", None),
        P(),
        P(),
        P(),
        P(None, "tensor"),
        P("tensor"),
        P("tensor", None),
        P(),
        P(),
        P(),
    )
    body = on_device
    groups = mesh.shape["dp"]
    if mesh.shape["tensor"] == MICRO and groups == 16:
        body = partial(row_on_device, groups)
    return jax.shard_map(
        body,
        mesh=mesh,
        in_specs=placed,
        out_specs=(
            P(None, ("dp", "tensor"), None),
            P(None, ("dp", "tensor"), None),
            P("dp", "tensor"),
            P("tensor"),
            P("dp", "tensor"),
            P("dp", "tensor"),
            P("tensor"),
            P("tensor", "dp"),
            P(),
            P(),
            P(),
            P("dp", "tensor"),
            P("tensor"),
            P("tensor", "dp"),
            P(),
            P(),
            P(),
        ),
        check_vma=False,
    )
```

```python
from functools import partial, reduce
import math

import jax
import jax.numpy as jnp
from jax import lax
from jax.experimental import pallas as pl
from jax.experimental.pallas import tpu as pltpu
from jax.sharding import PartitionSpec as P

HD = 64
MICRO = 2


def layer_norm(inputs, scale_vec, offset):
    centre = inputs - jnp.mean(inputs, axis=-1, keepdims=True)
    spread = jnp.mean(centre * centre, axis=-1, keepdims=True)
    return centre * lax.rsqrt(spread + 1e-12) * scale_vec + offset


def gelu_exact(inputs):
    return jax.nn.gelu(inputs, approximate=False)


def matmul(former, latter):
    return jnp.dot(former, latter, preferred_element_type=jnp.float32)


def inner_rows(former, latter):
    return lax.dot_general(
        former, latter, (((0,), (0,)), ((), ())), preferred_element_type=jnp.float32
    )


def inner_cols(former, latter):
    return lax.dot_general(
        former, latter, (((1,), (1,)), ((), ())), preferred_element_type=jnp.float32
    )


def head_split(block):
    return block.reshape(block.shape[0], block.shape[1] // HD, HD)


def masked_scores(queries, key_rows, seg_row):
    scores = jnp.einsum(
        "qhd,khd->hqk",
        head_split(queries),
        head_split(key_rows),
        preferred_element_type=jnp.float32,
    ) * (1.0 / math.sqrt(HD))
    same_doc = seg_row[:, None] == seg_row[None, :]
    return jnp.where(same_doc[None], scores, -1e30)


def attend_row(packed):
    queries, key_rows, value_rows, seg_row = packed
    scores = masked_scores(queries, key_rows, seg_row)
    highest = jnp.max(scores, axis=-1, keepdims=True)
    logsum = highest + jnp.log(jnp.sum(jnp.exp(scores - highest), axis=-1, keepdims=True))
    probs_low = jnp.exp(scores - logsum).astype(jnp.bfloat16)
    context = jnp.einsum(
        "hqk,khd->qhd", probs_low, head_split(value_rows), preferred_element_type=jnp.float32
    )
    return (context.reshape(queries.shape).astype(jnp.bfloat16), logsum[..., 0])


def attend_back(packed):
    queries, key_rows, value_rows, seg_row, logsum, grad_ctx = packed
    scores = masked_scores(queries, key_rows, seg_row)
    probs = jnp.exp(scores - logsum[..., None])
    grad_heads = head_split(grad_ctx)
    grad_probs = jnp.einsum(
        "qhd,khd->hqk", grad_heads, head_split(value_rows), preferred_element_type=jnp.float32
    )
    centred = grad_probs - jnp.sum(probs * grad_probs, axis=-1, keepdims=True)
    grad_scores = (probs * centred * (1.0 / math.sqrt(HD))).astype(jnp.bfloat16)
    grad_query = jnp.einsum(
        "hqk,khd->qhd", grad_scores, head_split(key_rows), preferred_element_type=jnp.float32
    )
    grad_key = jnp.einsum(
        "hqk,qhd->khd", grad_scores, head_split(queries), preferred_element_type=jnp.float32
    )
    grad_value = jnp.einsum(
        "hqk,qhd->khd", probs.astype(jnp.bfloat16), grad_heads, preferred_element_type=jnp.float32
    )
    flat_shape = queries.shape
    return jnp.concatenate(
        [
            grad_query.reshape(flat_shape),
            grad_key.reshape(flat_shape),
            grad_value.reshape(flat_shape),
        ],
        axis=1,
    ).astype(jnp.bfloat16)


def add_trees(former, latter):
    return jax.tree.map(jnp.add, former, latter)


def on_device(
    hidden_in,
    segment_ids,
    out_grad,
    w_query,
    b_query,
    w_key,
    w_value,
    b_value,
    w_out,
    b_out,
    attn_gain,
    attn_shift,
    w_up,
    b_up,
    w_down,
    b_down,
    ffn_gain,
    ffn_shift,
):
    local_width = w_query.shape[1]
    packed_rows = segment_ids.shape[1]
    length = segment_ids.shape[2]
    w_qkv = jnp.concatenate([w_query, w_key, w_value], axis=1)
    b_qkv = jnp.concatenate([b_query, jnp.zeros_like(b_query), b_value]).astype(jnp.float32)
    b_out32 = b_out.astype(jnp.float32)
    b_up32 = b_up.astype(jnp.float32)
    b_down32 = b_down.astype(jnp.float32)
    attn_gain32 = attn_gain.astype(jnp.float32)
    attn_shift32 = attn_shift.astype(jnp.float32)
    ffn_gain32 = ffn_gain.astype(jnp.float32)
    ffn_shift32 = ffn_shift.astype(jnp.float32)

    def to_rows(block):
        return block.reshape(packed_rows, length, block.shape[1])

    outputs = []
    input_grads = []
    weight_terms = []
    small_terms = []
    for micro_step in range(MICRO):
        tokens_low = hidden_in[micro_step]
        tokens = tokens_low.astype(jnp.float32)
        seg_rows = segment_ids[micro_step]
        full_rows = lax.all_gather(tokens_low, "tensor", axis=0, tiled=True)
        qkv_low = (matmul(full_rows, w_qkv) + b_qkv).astype(jnp.bfloat16)
        queries = qkv_low[:, :local_width]
        key_rows = qkv_low[:, local_width : 2 * local_width]
        value_rows = qkv_low[:, 2 * local_width :]
        context, logsums = lax.map(
            attend_row, (to_rows(queries), to_rows(key_rows), to_rows(value_rows), seg_rows)
        )
        context = context.reshape(-1, local_width)
        attn_part = lax.psum_scatter(
            matmul(context, w_out).astype(jnp.bfloat16), "tensor", scatter_dimension=0, tiled=True
        ).astype(jnp.float32)
        resid_one = attn_part + b_out32 + tokens
        hidden_one, norm_one_back = jax.vjp(layer_norm, resid_one, attn_gain32, attn_shift32)
        hidden_low = hidden_one.astype(jnp.bfloat16)
        hidden_rows = lax.all_gather(hidden_low, "tensor", axis=0, tiled=True)
        pre_act = matmul(hidden_rows, w_up) + b_up32
        activation, gelu_back = jax.vjp(gelu_exact, pre_act)
        gelu_low = activation.astype(jnp.bfloat16)
        ffn_part = lax.psum_scatter(
            matmul(gelu_low, w_down).astype(jnp.bfloat16), "tensor", scatter_dimension=0, tiled=True
        ).astype(jnp.float32)
        resid_two = ffn_part + b_down32 + hidden_one
        result, norm_two_back = jax.vjp(layer_norm, resid_two, ffn_gain32, ffn_shift32)
        outputs.append(result.astype(jnp.bfloat16))
        grad_two, grad_ffn_gain, grad_ffn_shift = norm_two_back(
            out_grad[micro_step].astype(jnp.float32)
        )
        grad_two_low = grad_two.astype(jnp.bfloat16)
        grad_two_rows = lax.all_gather(grad_two_low, "tensor", axis=0, tiled=True)
        grad_down = inner_rows(gelu_low, grad_two_rows)
        grad_act = inner_cols(grad_two_rows, w_down)
        grad_pre = gelu_back(grad_act)[0].astype(jnp.bfloat16)
        grad_up = inner_rows(hidden_rows, grad_pre)
        grad_hidden = (
            lax.psum_scatter(
                inner_cols(grad_pre, w_up).astype(jnp.bfloat16),
                "tensor",
                scatter_dimension=0,
                tiled=True,
            ).astype(jnp.float32)
            + grad_two
        )
        grad_one, grad_attn_gain, grad_attn_shift = norm_one_back(grad_hidden)
        grad_one_low = grad_one.astype(jnp.bfloat16)
        grad_one_rows = lax.all_gather(grad_one_low, "tensor", axis=0, tiled=True)
        grad_wout = inner_rows(context, grad_one_rows)
        grad_ctx = inner_cols(grad_one_rows, w_out).astype(jnp.bfloat16)
        grad_qkv = lax.map(
            attend_back,
            (
                to_rows(queries),
                to_rows(key_rows),
                to_rows(value_rows),
                seg_rows,
                logsums,
                to_rows(grad_ctx),
            ),
        )
        grad_qkv = grad_qkv.reshape(-1, 3 * local_width)
        grad_wqkv = inner_rows(full_rows, grad_qkv)
        grad_in = (
            lax.psum_scatter(
                inner_cols(grad_qkv, w_qkv).astype(jnp.bfloat16),
                "tensor",
                scatter_dimension=0,
                tiled=True,
            ).astype(jnp.float32)
            + grad_one
        )
        input_grads.append(grad_in.astype(jnp.bfloat16))
        small_terms.append(
            (
                jnp.sum(grad_qkv.astype(jnp.float32), axis=0),
                jnp.sum(grad_pre.astype(jnp.float32), axis=0),
                jnp.sum(grad_one, axis=0),
                grad_attn_gain,
                grad_attn_shift,
                jnp.sum(grad_two, axis=0),
                grad_ffn_gain,
                grad_ffn_shift,
            )
        )
        weight_set = (grad_wqkv, grad_up, grad_wout, grad_down)
        weight_terms.append(weight_set)
    summed = reduce(add_trees, weight_terms)
    summed = (
        lax.psum_scatter(
            summed[0].astype(jnp.bfloat16), "dp", scatter_dimension=0, tiled=True
        ).astype(jnp.float32),
        lax.psum_scatter(
            summed[1].astype(jnp.bfloat16), "dp", scatter_dimension=0, tiled=True
        ).astype(jnp.float32),
        lax.psum_scatter(
            summed[2].astype(jnp.bfloat16), "dp", scatter_dimension=1, tiled=True
        ).astype(jnp.float32),
        lax.psum_scatter(
            summed[3].astype(jnp.bfloat16), "dp", scatter_dimension=1, tiled=True
        ).astype(jnp.float32),
    )
    red_qkv, red_up, red_wout, red_down = summed
    small = reduce(add_trees, small_terms)
    bias_qkv, bias_up = lax.psum((small[0], small[1]), "dp")
    norm_bout, norm_again, norm_ashift, norm_bdown, norm_fgain, norm_fshift = lax.psum(
        (small[2], small[3], small[4], small[5], small[6], small[7]), ("dp", "tensor")
    )
    output = jnp.stack(outputs, axis=0)
    grad_input = jnp.stack(input_grads, axis=0)
    return (
        output,
        grad_input,
        red_qkv[:, :local_width],
        bias_qkv[:local_width],
        red_qkv[:, local_width : 2 * local_width],
        red_qkv[:, 2 * local_width :],
        bias_qkv[2 * local_width :],
        red_wout,
        norm_bout,
        norm_again,
        norm_ashift,
        red_up,
        bias_up,
        red_down,
        norm_bdown,
        norm_fgain,
        norm_fshift,
    )


def dot_nn(former, latter):
    return jnp.dot(former, latter, preferred_element_type=jnp.float32)


def dot_tn(former, latter):
    return lax.dot_general(
        former, latter, (((0,), (0,)), ((), ())), preferred_element_type=jnp.float32
    )


def dot_nt(former, latter):
    return lax.dot_general(
        former, latter, (((1,), (1,)), ((), ())), preferred_element_type=jnp.float32
    )


def head_pair(block):
    lane = lax.broadcasted_iota(jnp.int32, block.shape, 1)
    zero = jnp.zeros_like(block)
    return (jnp.where(lane < HD, block, zero), jnp.where(lane < HD, zero, block))


def in_vmem(count):
    return [pl.BlockSpec(memory_space=pltpu.VMEM) for _ in range(count)]


def call(kernel, name, outs, *args, scalars=0, scratch=(), products=0):
    out_shape = tuple(jax.ShapeDtypeStruct(shape, dtype) for shape, dtype in outs)
    moved = sum(math.prod(a.shape) * a.dtype.itemsize for a in (*args, *out_shape))
    return pl.pallas_call(
        kernel,
        out_shape=out_shape,
        in_specs=[pl.BlockSpec(memory_space=pltpu.SMEM) for _ in range(scalars)]
        + in_vmem(len(args) - scalars),
        out_specs=tuple(in_vmem(len(outs))),
        scratch_shapes=list(scratch),
        compiler_params=pltpu.CompilerParams(vmem_limit_bytes=8 << 20),
        cost_estimate=pl.CostEstimate(
            flops=2 * products, transcendentals=0, bytes_accessed=moved
        ),
        name=name,
    )(*args)


def pieces_of(total, most):
    return [slice(at, min(at + most, total)) for at in range(0, total, most)]


def low(block):
    return block.astype(jnp.bfloat16)


def wide(block):
    return block.astype(jnp.float32)


def heads_kernel(
    seg_col_ref, seg_row_ref, x_ref, wq_ref, wk_ref, wv_ref, bias_ref,
    q_ref, k_ref, v_ref, ctx_ref, lse_ref, mask_ref,
):
    mask_ref[...] = jnp.where(seg_col_ref[...] == seg_row_ref[...], 0.0, -1e30)
    for rows in pieces_of(x_ref.shape[0], 256):
        x = x_ref[rows, :]
        for cols in pieces_of(wq_ref.shape[1], 256):
            q_ref[rows, cols] = low(dot_nn(x, wq_ref[:, cols]) + bias_ref[0:1, cols])
            k_ref[rows, cols] = low(dot_nn(x, wk_ref[:, cols]))
            v_ref[rows, cols] = low(dot_nn(x, wv_ref[:, cols]) + bias_ref[1:2, cols])
    for i in range(q_ref.shape[1] // (2 * HD)):
        cols = slice(2 * HD * i, 2 * HD * (i + 1))
        q_pair = q_ref[:, cols] * jnp.bfloat16(1.0 / math.sqrt(HD))
        outs = []
        for h, q_one in enumerate(head_pair(q_pair)):
            scores = dot_nt(k_ref[:, cols], q_one) + mask_ref[...]
            highest = jnp.max(scores, axis=0, keepdims=True)
            raised = jnp.exp(scores - highest)
            total = jnp.sum(raised, axis=0, keepdims=True)
            lse_ref[i, h : h + 1, :] = highest + jnp.log(total)
            mixed = dot_tn(v_ref[:, cols], low(raised))
            outs.append(mixed[h * HD : (h + 1) * HD] * (1.0 / total))
        ctx_ref[:, cols] = low(jnp.concatenate(outs, axis=0).T)


def heads(x, w_q, w_k, w_v, bias, seg):
    length, width = x.shape[0], w_q.shape[1]
    flat = ((length, width), jnp.bfloat16)
    return call(
        heads_kernel,
        "heads",
        (flat, flat, flat, flat, ((width // (2 * HD), 2, length), jnp.float32)),
        seg[:, None], seg[None, :], x, w_q, w_k, w_v, bias,
        products=length * width * (3 * x.shape[1] + 2 * length),
        scratch=[pltpu.VMEM((length, length), jnp.float32)],
    )


def heads_back_kernel(
    seg_col_ref, seg_row_ref, q_ref, k_ref, v_ref, lse_ref, g_ref, w_ref,
    grad_ref, sum_ref, ctx_ref, mask_ref,
):
    mask_ref[...] = jnp.where(seg_col_ref[...] == seg_row_ref[...], 0.0, -1e30)
    scale = 1.0 / math.sqrt(HD)
    width = q_ref.shape[1]
    for rows in pieces_of(g_ref.shape[0], 256):
        for cols in pieces_of(width, 256):
            ctx_ref[rows, cols] = low(dot_nt(g_ref[rows, :], w_ref[cols, :]))
    for i in range(width // (2 * HD)):
        cols = slice(2 * HD * i, 2 * HD * (i + 1))
        q_pair = q_ref[:, cols] * jnp.bfloat16(scale)
        grad_q, grad_k, grad_v = [], 0.0, 0.0
        for h, (q_one, g_one) in enumerate(zip(head_pair(q_pair), head_pair(ctx_ref[:, cols]))):
            scores = dot_nt(k_ref[:, cols], q_one) + mask_ref[...]
            probs = jnp.exp(scores - lse_ref[i, h : h + 1, :])
            grad_p = dot_nt(v_ref[:, cols], g_one)
            delta = jnp.sum(probs * grad_p, axis=0, keepdims=True)
            grad_s = low(probs * (grad_p - delta))
            grad_v = grad_v + dot_nn(low(probs), g_one)
            grad_k = grad_k + dot_nn(grad_s, q_one)
            grad_q.append(dot_tn(k_ref[:, cols], grad_s)[h * HD : (h + 1) * HD])
        grad_q = (jnp.concatenate(grad_q, axis=0) * scale).T
        for n, grad in enumerate((grad_q, grad_k, grad_v)):
            there = slice(n * width + 2 * HD * i, n * width + 2 * HD * (i + 1))
            grad = low(grad)
            grad_ref[:, there] = grad
            sum_ref[:, there] = jnp.sum(wide(grad), axis=0, keepdims=True)


def heads_back(qkv, lse, seg, grad_one_low, w_out):
    length, width = qkv[0].shape
    return call(
        heads_back_kernel,
        "heads_back",
        (((length, 3 * width), jnp.bfloat16), ((1, 3 * width), jnp.float32)),
        seg[:, None], seg[None, :], *qkv, lse, grad_one_low, w_out,
        products=length * width * (w_out.shape[1] + 5 * length),
        scratch=[
            pltpu.VMEM((length, width), jnp.bfloat16),
            pltpu.VMEM((length, length), jnp.float32),
        ],
    )


B_OUT, GAIN_ONE, SHIFT_ONE, B_DOWN, GAIN_TWO, SHIFT_TWO = range(6)


def row_of(ref, row):
    return ref[row : row + 1, :]


def row_norm(resid):
    centre = resid - jnp.mean(resid, axis=-1, keepdims=True)
    root = lax.rsqrt(jnp.mean(centre * centre, axis=-1, keepdims=True) + 1e-12)
    return centre * root, root


def row_norm_back(grad, gain, unit, root):
    inner = grad * gain
    mean = jnp.mean(inner, axis=-1, keepdims=True)
    along = jnp.mean(inner * unit, axis=-1, keepdims=True)
    return root * (inner - mean - unit * along)


def store_turned(depth, place, block, spare_ref, keep_ref, send_ref, base, cols):
    rows = block.shape[1] >> depth
    spare_ref[...] = block.T
    core = place & 1
    for pair in range(1 << (depth - 1)):
        step = pair ^ (place >> 1)
        bits = [(step >> bit) & 1 for bit in range(depth - 1)]
        for owner, ref, start in ((core, keep_ref, 0), (1 - core, send_ref, base)):
            first = jnp.where(owner == 0, bits[1], bits[2])
            second = jnp.where(owner == 0, bits[2], bits[1])
            where = ((bits[0] * 2 + first) * 2 + second) * rows + start
            source = pl.multiple_of((2 * pair + owner) * rows, 16)
            ref[pl.ds(pl.multiple_of(where, 16), rows), cols] = spare_ref[pl.ds(source, rows), :]


def norm_one_kernel(
    depth, place_ref, ctx_a_ref, ctx_b_ref, w_a_ref, w_b_ref, x_ref, par_ref,
    unit_ref, root_ref, low_ref, hidden_ref, tokens_ref, send_ref, sum_ref, spare_ref,
):
    for cols in pieces_of(x_ref.shape[1], 256):
        sum_ref[:, cols] = dot_nn(ctx_a_ref[...], w_a_ref[:, cols]) + dot_nn(
            ctx_b_ref[...], w_b_ref[:, cols]
        )
    for rows in pieces_of(x_ref.shape[0], 128):
        x = x_ref[rows, :]
        unit, root = row_norm(sum_ref[rows, :] + row_of(par_ref, B_OUT) + wide(x))
        unit_ref[rows, :] = unit
        root_ref[rows, :] = root
        hidden = low(unit * row_of(par_ref, GAIN_ONE) + row_of(par_ref, SHIFT_ONE))
        low_ref[rows, :] = hidden
        keep = hidden_ref.shape[0]
        store_turned(depth, place_ref[0], hidden, spare_ref, hidden_ref, send_ref, 0, rows)
        store_turned(depth, place_ref[0], x, spare_ref, tokens_ref, send_ref, keep, rows)
    send_ref[2 * keep : 2 * keep + ctx_a_ref.shape[0], :] = ctx_a_ref[...]
    send_ref[2 * keep + ctx_a_ref.shape[0] :, :] = ctx_b_ref[...]


def norm_one(depth, place, ctx_a, ctx_b, w_a, w_b, x, par):
    length, width = x.shape
    kept = ((width // 2, length), jnp.bfloat16)
    return call(
        partial(norm_one_kernel, depth),
        "norm_one",
        (
            (x.shape, jnp.float32),
            ((length, 1), jnp.float32),
            (x.shape, jnp.bfloat16),
            kept,
            kept,
            ((width + 2 * length, length), jnp.bfloat16),
        ),
        place.reshape(1), ctx_a, ctx_b, w_a, w_b, x, par,
        scalars=1,
        scratch=[pltpu.VMEM(x.shape, jnp.float32), pltpu.VMEM((width, 128), jnp.bfloat16)],
        products=2 * ctx_a.shape[0] * w_a.shape[0] * w_a.shape[1],
    )


def up_kernel(x_ref, w_ref, bias_ref, act_ref, slope_ref):
    for cols in pieces_of(w_ref.shape[1], 256):
        at = cols.start % bias_ref.shape[1]
        row = 2 + cols.start // bias_ref.shape[1]
        bias = bias_ref[row : row + 1, at : at + 256]
        for rows in pieces_of(x_ref.shape[0], 256):
            pre = dot_nn(x_ref[rows, :], w_ref[:, cols]) + bias
            act_ref[rows, cols], slope_ref[rows, cols] = gelu_pair(pre)


def up(x, w, bias):
    flat = ((x.shape[0], w.shape[1]), jnp.bfloat16)
    products = x.shape[0] * w.shape[0] * w.shape[1]
    return call(up_kernel, "up", (flat, flat), x, w, bias, products=products)


def down_kernel(act_ref, w_ref, out_ref):
    for rows in pieces_of(act_ref.shape[0], 256):
        for cols in pieces_of(w_ref.shape[1], 256):
            out_ref[rows, cols] = dot_nn(act_ref[rows, :], w_ref[:, cols])


def down(act, w):
    out = ((act.shape[0], w.shape[1]), jnp.float32)
    products = act.shape[0] * w.shape[0] * w.shape[1]
    return call(down_kernel, "down", (out,), act, w, products=products)[0]


def norm_two_kernel(
    depth, place_ref, ffn_ref, act_ref, w_ref, unit_one_ref, par_ref, grad_ref,
    out_ref, two_ref, low_ref, keep_ref, send_ref, sum_ref, spare_ref,
):
    for cols in pieces_of(w_ref.shape[1], 256):
        two_ref[:, cols] = ffn_ref[:, cols] + dot_nn(act_ref[...], w_ref[:, cols])
    sum_ref[...] = jnp.zeros_like(sum_ref)
    for rows in pieces_of(act_ref.shape[0], 128):
        hidden = unit_one_ref[rows, :] * row_of(par_ref, GAIN_ONE) + row_of(par_ref, SHIFT_ONE)
        unit, root = row_norm(two_ref[rows, :] + row_of(par_ref, B_DOWN) + hidden)
        gain = row_of(par_ref, GAIN_TWO)
        out_ref[rows, :] = low(unit * gain + row_of(par_ref, SHIFT_TWO))
        grad = wide(grad_ref[rows, :])
        two = row_norm_back(grad, gain, unit, root)
        two_ref[rows, :] = two
        two_low = low(two)
        low_ref[rows, :] = two_low
        store_turned(depth, place_ref[0], two_low, spare_ref, keep_ref, send_ref, 0, rows)
        for i, term in enumerate((two, grad * unit, grad)):
            sum_ref[i : i + 1, :] += jnp.sum(term, axis=0, keepdims=True)


def norm_two(depth, place, ffn, act, w, unit_one, par, grad_out):
    shape = grad_out.shape
    flat, kept = (shape, jnp.bfloat16), ((shape[1] // 2, shape[0]), jnp.bfloat16)
    return call(
        partial(norm_two_kernel, depth),
        "norm_two",
        (flat, (shape, jnp.float32), flat, kept, kept, ((3, shape[1]), jnp.float32)),
        place.reshape(1), ffn, act, w, unit_one, par, grad_out,
        scalars=1,
        scratch=[pltpu.VMEM((shape[1], 128), jnp.bfloat16)],
        products=act.shape[0] * w.shape[0] * w.shape[1],
    )


def pre_kernel(grad_ref, w_ref, slope_ref, out_ref, sum_ref):
    for cols in pieces_of(w_ref.shape[0], 256):
        total = 0.0
        for rows in pieces_of(grad_ref.shape[0], 256):
            grad = low(dot_nt(grad_ref[rows, :], w_ref[cols, :]) * wide(slope_ref[rows, cols]))
            out_ref[rows, cols] = grad
            total = total + jnp.sum(wide(grad), axis=0, keepdims=True)
        sum_ref[:, cols] = total


def pre_back(grad, w, slope):
    return call(
        pre_kernel, "pre_back", ((slope.shape, jnp.bfloat16), ((1, slope.shape[1]), jnp.float32)),
        grad, w, slope,
        products=grad.shape[0] * w.shape[0] * w.shape[1],
    )


def one_kernel(
    depth, place_ref, pre_a_ref, pre_b_ref, w_a_ref, w_b_ref, two_ref, unit_ref, root_ref, par_ref,
    one_ref, low_ref, keep_ref, send_ref, sum_ref, spare_ref,
):
    for cols in pieces_of(one_ref.shape[1], 256):
        one_ref[:, cols] = dot_nt(pre_a_ref[...], w_a_ref[cols, :]) + dot_nt(
            pre_b_ref[...], w_b_ref[cols, :]
        )
    sum_ref[...] = jnp.zeros_like(sum_ref)
    for rows in pieces_of(pre_a_ref.shape[0], 128):
        grad = one_ref[rows, :] + two_ref[rows, :]
        unit = unit_ref[rows, :]
        one = row_norm_back(grad, row_of(par_ref, GAIN_ONE), unit, root_ref[rows, :])
        one_ref[rows, :] = one
        one_low = low(one)
        low_ref[rows, :] = one_low
        store_turned(depth, place_ref[0], one_low, spare_ref, keep_ref, send_ref, 0, rows)
        for i, term in enumerate((one, grad * unit, grad)):
            sum_ref[i : i + 1, :] += jnp.sum(term, axis=0, keepdims=True)


def one_back(depth, place, pre_a, pre_b, w_a, w_b, two, unit, root, par):
    shape = two.shape
    return call(
        partial(one_kernel, depth),
        "one_back",
        (
            (shape, jnp.float32),
            (shape, jnp.bfloat16),
            ((shape[1] // 2, shape[0]), jnp.bfloat16),
            ((shape[1] // 2, shape[0]), jnp.bfloat16),
            ((3, shape[1]), jnp.float32),
        ),
        place.reshape(1), pre_a, pre_b, w_a, w_b, two, unit, root, par,
        scalars=1,
        scratch=[pltpu.VMEM((shape[1], 128), jnp.bfloat16)],
        products=2 * pre_a.shape[0] * w_a.shape[0] * w_a.shape[1],
    )


def input_kernel(one_ref, a_ref, b_ref, *refs):
    weights, out_ref = refs[:6], refs[6]
    width = weights[0].shape[1]
    for rows in pieces_of(one_ref.shape[0], 256):
        for cols in pieces_of(one_ref.shape[1], 256):
            total = one_ref[rows, cols]
            for i, w_ref in enumerate(weights):
                grad_ref = (a_ref, b_ref)[i // 3]
                part = slice((i % 3) * width, (i % 3 + 1) * width)
                total = total + dot_nt(grad_ref[rows, part], w_ref[cols, :])
            out_ref[rows, cols] = low(total)


def input_back(grad_one, grad_a, grad_b, weights):
    return call(
        input_kernel, "input_back", ((grad_one.shape, jnp.bfloat16),),
        grad_one, grad_a, grad_b, *weights,
        products=2 * grad_a.shape[0] * grad_a.shape[1] * grad_one.shape[1],
    )[0]


def take_kernel(index_ref, *refs):
    weights, (one_ref, up_ref, down_ref), sems = refs[:6], refs[6:9], refs[9]
    copies = []

    def start(source, target):
        copies.append(pltpu.make_async_copy(source, target, sems.at[len(copies)]))
        copies[-1].start()

    def rows_of(ref):
        rows = ref.shape[0] // 8
        return pl.ds(pl.multiple_of(index_ref[0] * rows, 16), rows)

    at = 0
    cols = one_ref.shape[1]
    for ref in weights[:4]:
        rows = ref.shape[0] // 8
        for col in range(0, ref.shape[1], cols):
            start(ref.at[rows_of(ref), col : col + cols], one_ref.at[at : at + rows])
            at += rows
    start(weights[4].at[rows_of(weights[4])], up_ref)
    rows = weights[5].shape[0] // 4
    start(weights[5].at[pl.ds(pl.multiple_of(index_ref[8] * rows, 16), rows)], down_ref)
    for copy in copies:
        copy.wait()


def take(indices, weights):
    blocks = [(w.shape[0] // 8, w.shape[1]) for w in weights]
    local = blocks[0][1]
    one = (sum(rows * cols for rows, cols in blocks[:4]) // local, local)
    shapes = [one, blocks[4], (2 * blocks[5][0], blocks[5][1])]
    parts = sum(cols // local for _, cols in blocks[:4]) + 2
    return pl.pallas_call(
        take_kernel,
        in_specs=[pl.BlockSpec(memory_space=pltpu.SMEM)]
        + [pl.BlockSpec(memory_space=pltpu.HBM) for _ in weights],
        out_specs=tuple(in_vmem(3)),
        out_shape=tuple(jax.ShapeDtypeStruct(shape, jnp.bfloat16) for shape in shapes),
        scratch_shapes=[pltpu.SemaphoreType.DMA((parts,))],
        cost_estimate=pl.CostEstimate(
            flops=0, transcendentals=0, bytes_accessed=4 * sum(r * c for r, c in shapes)
        ),
        compiler_params=pltpu.CompilerParams(vmem_limit_bytes=8 << 20),
        name="take",
    )(indices, *weights)


def kept_kernel(starts, core_ref, rows_ref, near_ref, far_ref, more_rows_ref, more_near_ref, more_far_ref, kept_ref, sent_ref):
    half = rows_ref.shape[0] // 2
    length = near_ref.shape[0]
    pairs = ((near_ref, more_near_ref, starts[1]), (far_ref, more_far_ref, starts[2]))

    def part(row, side, cols):
        ref, more_ref, start = pairs[side]
        rows, more = slice(row * half, (row + 1) * half), starts[0] + row * half
        total = dot_nn(rows_ref[rows, :], ref[:, cols])
        return low(
            total
            + dot_nn(more_rows_ref[more : more + half, :], more_ref[start : start + length, cols])
        )

    for cols in pieces_of(near_ref.shape[1], 512):
        kept_ref[0, :, cols] = part(0, 0, cols)
        sent_ref[1, :, cols] = part(1, 1, cols)
        one, two = part(1, 0, cols), part(0, 1, cols)

        @pl.when(core_ref[0] == 0)
        def _():
            kept_ref[1, :, cols] = one
            sent_ref[0, :, cols] = two

        @pl.when(core_ref[0] != 0)
        def _():
            kept_ref[1, :, cols] = two
            sent_ref[0, :, cols] = one


def far_kernel(core_ref, rows_ref, near_ref, far_ref, more_rows_ref, more_near_ref, more_far_ref, kept_ref, sent_ref):
    half = rows_ref.shape[0] // 2
    part = half // 4
    pairs = ((near_ref, more_near_ref), (far_ref, more_far_ref))
    for cols in pieces_of(near_ref.shape[1], 512):
        for row in range(2):
            rows = slice(row * half, (row + 1) * half)
            for side, (ref, more_ref) in enumerate(pairs):
                total = dot_nn(rows_ref[rows, :], ref[:, cols])
                total = low(total + dot_nn(more_rows_ref[rows, :], more_ref[:, cols]))
                first = jnp.where(core_ref[0] == 0, side, row)
                second = jnp.where(core_ref[0] == 0, row, side)
                for n in range(2):
                    kept_ref[n, first, second, :, cols] = total[n * part : (n + 1) * part]
                    sent_ref[n, first, second, :, cols] = total[(2 + n) * part : (3 + n) * part]


def grad_kept_far(core, rows, near, far, more):
    shape = ((2, 2, 2, rows.shape[0] // 8, near.shape[1]), jnp.bfloat16)
    return call(
        far_kernel, "grad_kept_far", (shape, shape), core.reshape(1), rows, near, far, *more,
        scalars=1,
        products=4 * rows.shape[0] * near.shape[0] * near.shape[1],
    )


def grad_kept(core, rows, near, far, more, starts):
    shape = ((2, rows.shape[0] // 2, near.shape[1]), jnp.bfloat16)
    return call(
        partial(kept_kernel, starts), "grad_kept", (shape, shape),
        core.reshape(1), rows, near, far, *more,
        scalars=1,
        products=4 * rows.shape[0] * near.shape[0] * near.shape[1],
    )


def gelu_pair(pre):
    cdf = 0.5 * (1.0 + lax.erf(pre * (1.0 / math.sqrt(2.0))))
    pdf = jnp.exp(-0.5 * pre * pre) * (1.0 / math.sqrt(2.0 * math.pi))
    return (pre * cdf).astype(jnp.bfloat16), (cdf + pre * pdf).astype(jnp.bfloat16)


def lay_kernel(layout, index_ref, *refs):
    ins, outs = refs[: len(layout)], refs[len(layout) :]
    for source, places in zip(ins, layout):
        for slot, unit, at, rows, which, col in places:
            offset = pl.multiple_of(index_ref[slot] * unit, 16)
            outs[which][pl.ds(offset, rows), col : col + source.shape[1]] = source[
                at : at + rows, :
            ]


def lay(indices, sources, layout, shapes):
    outs = tuple((shape, jnp.bfloat16) for shape in shapes)
    return call(partial(lay_kernel, layout), "lay", outs, indices, *sources, scalars=1)


def tie(*values):
    return lax.optimization_barrier(values)


def add_low(former, latter):
    return (former.astype(jnp.float32) + latter.astype(jnp.float32)).astype(jnp.bfloat16)


class Reduction:
    def __init__(self, kept, sent, step, send_over):
        self.kept = kept
        self.send_over = send_over
        self.flying = send_over(sent, step)

    def send(self, step):
        rows = self.kept.shape[0] // 2
        self.flying = self.send_over(self.kept[rows:], step)
        self.kept = self.kept[:rows]

    def land(self, last=False):
        total = self.kept.astype(jnp.float32) + self.flying.astype(jnp.float32)
        self.kept = total if last else total.astype(jnp.bfloat16)
        self.flying = None


def row_on_device(
    groups,
    hidden_in,
    segment_ids,
    out_grad,
    w_query,
    b_query,
    w_key,
    w_value,
    b_value,
    w_out,
    b_out,
    attn_gain,
    attn_shift,
    w_up,
    b_up,
    w_down,
    b_down,
    ffn_gain,
    ffn_shift,
):
    side = lax.axis_index("tensor")
    place = lax.axis_index("dp")
    half = hidden_in.shape[1]
    width = hidden_in.shape[2]
    local = w_query.shape[1]
    depth = groups.bit_length() - 1
    f32 = jnp.float32
    bf16 = jnp.bfloat16

    def over(block):
        return lax.ppermute(block, "tensor", [(0, 1), (1, 0)])

    def across(block, mask):
        return lax.ppermute(block, "dp", [(i, i ^ mask) for i in range(groups)])

    sides = 2

    def by_core(block, ways):
        pairs = []
        for i in range(groups):
            mask, flip = ways[i & 1]
            pairs += [(i * sides + s, (i ^ mask) * sides + (s ^ flip)) for s in range(sides)]
        return lax.ppermute(block, ("dp", "tensor"), pairs)

    ways = {
        "one": ((0, 1), (2, 0)),
        "two": ((2, 0), (0, 1)),
        "near": ((2, 0), (4, 0)),
        "far": ((4, 0), (2, 0)),
        "three": ((4, 0), (8, 0)),
        "four": ((8, 0), (4, 0)),
    }

    def send(block, step):
        return across(block, 1 << step) if isinstance(step, int) else by_core(block, ways[step])

    def pick(pair):
        return lax.dynamic_index_in_dim(pair, side, 0, keepdims=False), lax.dynamic_index_in_dim(
            pair, 1 - side, 0, keepdims=False
        )

    core = place & 1
    eighth = place & 7
    first, second = 2 << core, 4 >> core
    low_bit, high_bit = (place >> 1) & 1, 2 + ((place >> 2) & 1)
    quarter = jnp.where(core == 0, low_bit, high_bit)
    other = jnp.where(core == 0, high_bit, low_bit)
    indices = jnp.stack(
        [eighth ^ mask for mask in (0, first, second, 6, 1, second ^ 1, first ^ 1, 7)]
        + [quarter, quarter ^ 1, other, other ^ 1]
    )
    eighths = ((0, 1), (2, 3), (4, 5), (6, 7))

    def second_hop(piece, got):
        held = jnp.concatenate([piece, got], axis=0)
        return held, send(held, "far")

    def gathered(sources, slots, cuts, shapes):
        layout = []
        for source in slots:
            rows = sources[len(layout)].shape[0] // len(source)
            layout.append(
                tuple(
                    (slot, unit, i * rows + at, count, which, col)
                    for i, slot in enumerate(source)
                    for at, count, unit, which, col in cuts
                )
            )
        return lay(indices, sources, tuple(layout), shapes)

    tokens_own, tokens_away = pick(hidden_in)
    tokens_away, indices = tie(tokens_away, indices)
    fly_tokens = over(tokens_away)
    piece_one, piece_up, piece_down = take(indices, (w_query, w_key, w_value, w_out, w_up, w_down))
    fly_one = over(piece_one)
    biases = jnp.concatenate([b_query, b_value, b_up])
    par = jnp.stack([b_out, attn_gain, attn_shift, b_down, ffn_gain, ffn_shift]).astype(f32)
    seg_own, _ = pick(segment_ids[:, 0])
    seg = jnp.where(
        side == 0, seg_own, jnp.concatenate([seg_own[half:], seg_own[:half]], axis=0)
    )
    cut = b_query.shape[0]
    tokens_got, biases, piece_up, par, seg = tie(fly_tokens, biases, piece_up, par, seg)
    fly_biases = over(biases)
    biases = biases.reshape(-1, cut).astype(f32)
    tokens_low = jnp.concatenate([tokens_own, tokens_got], axis=0)
    *qkv_a, ctx_a, lse_a = heads(tokens_low, w_query, w_key, w_value, biases, seg)
    ctx_a, one, biases_b, piece_up, piece_down = tie(
        ctx_a, fly_one, fly_biases, piece_up, piece_down
    )
    biases_b = biases_b.reshape(-1, cut).astype(f32)
    fly_one = send(one, "near")
    fly_up_x = over(piece_up)
    ctx_a, fly_one, up_piece, piece_down = tie(ctx_a, fly_one, fly_up_x, piece_down)
    one_held, fly_one = second_hop(one, fly_one)
    one_core = across(one_held, 1)
    fly_up = send(up_piece, "near")
    part = piece_down.shape[0] * 11 // 16
    fly_down_a = over(piece_down[:part])
    ctx_a, one_last, one_core, fly_up, down_a, piece_down = tie(
        ctx_a, fly_one, one_core, fly_up, fly_down_a, piece_down
    )
    one_last_core = across(one_last, 1)
    up_held, fly_up = second_hop(up_piece, fly_up)
    up_core = across(up_held, 1)
    fly_down_b = over(piece_down[part:])
    one_last_core, ctx_a = tie(one_last_core, ctx_a)
    rows = width // 8
    small_rows = local // 8
    w_query_b, w_key_b, w_value_b, w_out_b = gathered(
        (one_held, one_last, one_core, one_last_core),
        eighths,
        tuple((i * rows, rows, rows, i, 0) for i in range(3))
        + tuple(
            (3 * rows + i * small_rows, small_rows, small_rows, 3, i * local)
            for i in range(width // local)
        ),
        (w_query.shape, w_key.shape, w_value.shape, w_out.shape),
    )
    *qkv_b, ctx_b, lse_b = heads(tokens_low, w_query_b, w_key_b, w_value_b, biases_b, seg)
    ctx_b, up_last, up_core, down_b, out_grad = tie(ctx_b, fly_up, up_core, fly_down_b, out_grad)
    up_last_core = across(up_last, 1)
    down_piece = jnp.concatenate([down_a, down_b], axis=0)
    fly_down = send(down_piece, "near")
    down_core = across(down_piece, 1)
    grads_own, grads_away = pick(out_grad)
    fly_grads = over(grads_away)
    unit_one, root_one, hidden_low, hidden_rows, tokens_rows, shared = norm_one(
        depth, place, ctx_a, ctx_b, w_out, w_out_b, tokens_low, par
    )
    act_a, slope_a = up(hidden_low, w_up, biases)
    ffn_a = down(act_a, w_down)
    ffn_a, up_last_core, hidden_low = tie(ffn_a, up_last_core, hidden_low)
    (w_up_b,) = gathered(
        (up_held, up_last, up_core, up_last_core),
        eighths,
        ((0, rows, rows, 0, 0),),
        (w_up.shape,),
    )
    w_up_b, hidden_low, fly_down, fly_grads = tie(w_up_b, hidden_low, fly_down, fly_grads)
    down_last_core = across(fly_down, 1)
    act_b, slope_b = up(hidden_low, w_up_b, biases_b)
    act_b, act_a, down_core, down_last_core, shared = tie(
        act_b, act_a, down_core, down_last_core, shared
    )
    fly_act_a = across(act_a, 1)
    fly_act_b = across(act_b, 1)
    fly_shared = across(shared, 1)
    part = w_down.shape[0] // 4
    (w_down_b,) = gathered(
        (down_piece, fly_down, down_core, down_last_core),
        ((8,), (9,), (10,), (11,)),
        ((0, part, part, 0, 0),),
        (w_down.shape,),
    )
    grad_out = jnp.concatenate([grads_own, fly_grads], axis=0)
    output, grad_two, grad_two_low, two_rows, two_sent, sums_two = norm_two(
        depth, place, ffn_a, act_b, w_down_b, unit_one, par, grad_out
    )

    def land(carry, *reductions, last=False):
        carry, flying = tie(carry, [red.flying for red in reductions])
        for red, got in zip(reductions, flying):
            red.flying = got
            red.land(last)
        return carry

    def reduction(rows, near, far, more, *starts):
        kept, sent = tie(*grad_kept(core, rows, near, far, more, starts))
        return Reduction(kept, sent, "one", send)

    def blocks_of(red):
        kept = red.kept.reshape(-1, red.kept.shape[-1])
        red.kept = kept.reshape(2, kept.shape[0] // 2, kept.shape[1])

    two_rows, two_sent, grad_two_low, more_act_a, more_act_b = tie(
        two_rows, two_sent, grad_two_low, fly_act_a, fly_act_b
    )
    more_two = across(two_sent, 1)
    pre_b, sum_pre_b = pre_back(grad_two_low, w_down_b, slope_b)
    pre_b, grad_two_low, shared, more_two = tie(pre_b, grad_two_low, fly_shared, more_two)
    fly_pre_b = across(pre_b, 1)
    pre_a, sum_pre_a = pre_back(grad_two_low, w_down, slope_a)
    two_rows, pre_a = tie(two_rows, pre_a)
    kept, sent = tie(
        *grad_kept_far(core, two_rows, act_a, act_b, (more_two, more_act_a, more_act_b))
    )
    red_down = Reduction(kept, sent, "three", send)
    pre_a, red_down.kept, more_pre_b = tie(pre_a, red_down.kept, fly_pre_b)
    fly_pre_a = across(pre_a, 1)
    grad_one, grad_one_low, one_rows, one_sent, sums_one = one_back(
        depth, place, pre_a, pre_b, w_up, w_up_b, grad_two, unit_one, root_one, par
    )
    grad_one_low, one_rows, one_sent, pre_a, pre_b, hidden_rows, more_pre_a = tie(
        grad_one_low, one_rows, one_sent, pre_a, pre_b, hidden_rows, fly_pre_a
    )
    red_up = reduction(hidden_rows, pre_a, pre_b, (shared, more_pre_a, more_pre_b), 0, 0, 0)
    grad_one_low, one_rows, one_sent, red_up.kept = tie(
        grad_one_low, one_rows, one_sent, red_up.kept
    )
    more_one = across(one_sent, 1)
    grad_qkv_b, sum_qkv_b = heads_back(qkv_b, lse_b, seg, grad_one_low, w_out_b)
    grad_one_low, grad_qkv_b, more_one, one_rows = tie(
        grad_one_low, grad_qkv_b, more_one, one_rows
    )
    fly_qkv_b = across(grad_qkv_b, 1)
    red_out = reduction(
        one_rows, ctx_a, ctx_b, (more_one, shared, shared), 0, width, width + 2 * half
    )
    grad_one_low, red_out.kept = tie(grad_one_low, red_out.kept)
    grad_qkv_a, sum_qkv_a = heads_back(qkv_a, lse_a, seg, grad_one_low, w_out)
    grad_qkv_a = land(grad_qkv_a, red_down)
    blocks_of(red_down)
    grad_qkv_a, more_qkv_b, red_down.kept = land((grad_qkv_a, fly_qkv_b, red_down.kept), red_up)
    red_up.send("two")
    red_down.send("four")
    fly_qkv_a = across(grad_qkv_a, 1)
    grad_qkv_a, more_qkv_a = tie(grad_qkv_a, fly_qkv_a)
    red_qkv = reduction(
        tokens_rows, grad_qkv_a, grad_qkv_b, (shared, more_qkv_a, more_qkv_b), width // 2, 0, 0
    )
    grad_qkv_a, grad_qkv_b, red_qkv.kept = tie(grad_qkv_a, grad_qkv_b, red_qkv.kept)
    grad_in = input_back(
        grad_one, grad_qkv_a, grad_qkv_b, (w_query, w_key, w_value, w_query_b, w_key_b, w_value_b)
    )
    near = [sum_qkv_a[0, :cut], sum_qkv_a[0, 2 * cut :], sum_pre_a[0]]
    far = [sum_qkv_b[0, :cut], sum_qkv_b[0, 2 * cut :], sum_pre_b[0]]
    small = jnp.concatenate(near + far + [sums_one.reshape(-1), sums_two.reshape(-1)])
    size = 2 * cut + b_up.shape[0]
    small, grad_in = land((small, grad_in), red_up)
    blocks_of(red_up)
    red_up.send("three")
    more = across(small, 1)
    small, grad_in = land((small, grad_in), red_down)
    blocks_of(red_down)
    red_down.send("one")
    small, more, grad_in = land((small, more, grad_in), red_out)
    red_out.send("two")
    small = small + more
    small, grad_in = land((small, grad_in), red_qkv)
    red_qkv.send("two")
    more = across(small, 8)
    small, more, grad_in = land((small, more, grad_in), red_down)
    blocks_of(red_down)
    red_down.send("two")
    small = small + more
    fly_in = over(grad_in[half:])
    small = land(small, red_out)
    blocks_of(red_out)
    red_out.send("three")
    small, output = land((small, output), red_qkv)
    blocks_of(red_qkv)
    red_qkv.send("three")
    more = across(small, 4)
    small = land(small, red_down, last=True)
    small, more, output = land((small, more, output), red_up)
    blocks_of(red_up)
    red_up.send("four")
    fly_output = over(output[half:])
    small = small + more
    got = over(small[size:])
    small = jnp.concatenate([small[:size], small[2 * size :]])
    small, got = land((small, got), red_qkv)
    blocks_of(red_qkv)
    red_qkv.send("four")
    small = small + got
    got = across(small, 2)
    small, fly_in = land((small, fly_in), red_out)
    blocks_of(red_out)
    red_out.send("four")
    small, got, fly_output = tie(small, got, fly_output)
    small = small + got
    small = land(small, red_up, last=True)

    pieces = []
    at = 0
    for size in (cut, cut, b_up.shape[0]) + (width,) * 6:
        pieces.append(small[at : at + size])
        at += size

    def to_owners(mine, theirs):
        return jnp.where(side == 0, jnp.stack([mine, theirs]), jnp.stack([theirs, mine]))

    output = to_owners(output[:half], fly_output)
    grad_in = to_owners(grad_in[:half], fly_in)
    pieces, output, grad_in = land((pieces, output, grad_in), red_out, red_qkv, last=True)
    red_out, red_up, red_down, grad_qkv = (
        red.kept.reshape(-1, red.kept.shape[-1]) for red in (red_out, red_up, red_down, red_qkv)
    )
    return (
        output,
        grad_in,
        grad_qkv[:, :local],
        pieces[0],
        grad_qkv[:, local : 2 * local],
        grad_qkv[:, 2 * local :],
        pieces[1],
        red_out.T,
        pieces[3],
        pieces[4],
        pieces[5],
        red_up,
        pieces[2],
        red_down.T,
        pieces[6],
        pieces[7],
        pieces[8],
    )


def solution(mesh):
    placed = (
        P(None, ("dp", "tensor"), None),
        P(None, "dp", None),
        P(None, ("dp", "tensor"), None),
        P(None, "tensor"),
        P("tensor"),
        P(None, "tensor"),
        P(None, "tensor"),
        P("tensor"),
        P("tensor", None),
        P(),
        P(),
        P(),
        P(None, "tensor"),
        P("tensor"),
        P("tensor", None),
        P(),
        P(),
        P(),
    )
    body = on_device
    groups = mesh.shape["dp"]
    if mesh.shape["tensor"] == MICRO and groups == 16:
        body = partial(row_on_device, groups)
    return jax.shard_map(
        body,
        mesh=mesh,
        in_specs=placed,
        out_specs=(
            P(None, ("dp", "tensor"), None),
            P(None, ("dp", "tensor"), None),
            P("dp", "tensor"),
            P("tensor"),
            P("dp", "tensor"),
            P("dp", "tensor"),
            P("tensor"),
            P("tensor", "dp"),
            P(),
            P(),
            P(),
            P("dp", "tensor"),
            P("tensor"),
            P("tensor", "dp"),
            P(),
            P(),
            P(),
        ),
        check_vma=False,
    )
```

```python
from functools import partial, reduce
import math

import jax
import jax.numpy as jnp
from jax import lax
from jax.experimental import pallas as pl
from jax.experimental.pallas import tpu as pltpu
from jax.sharding import PartitionSpec as P

HD = 64
MICRO = 2


def layer_norm(inputs, scale_vec, offset):
    centre = inputs - jnp.mean(inputs, axis=-1, keepdims=True)
    spread = jnp.mean(centre * centre, axis=-1, keepdims=True)
    return centre * lax.rsqrt(spread + 1e-12) * scale_vec + offset


def gelu_exact(inputs):
    return jax.nn.gelu(inputs, approximate=False)


def matmul(former, latter):
    return jnp.dot(former, latter, preferred_element_type=jnp.float32)


def inner_rows(former, latter):
    return lax.dot_general(
        former, latter, (((0,), (0,)), ((), ())), preferred_element_type=jnp.float32
    )


def inner_cols(former, latter):
    return lax.dot_general(
        former, latter, (((1,), (1,)), ((), ())), preferred_element_type=jnp.float32
    )


def head_split(block):
    return block.reshape(block.shape[0], block.shape[1] // HD, HD)


def masked_scores(queries, key_rows, seg_row):
    scores = jnp.einsum(
        "qhd,khd->hqk",
        head_split(queries),
        head_split(key_rows),
        preferred_element_type=jnp.float32,
    ) * (1.0 / math.sqrt(HD))
    same_doc = seg_row[:, None] == seg_row[None, :]
    return jnp.where(same_doc[None], scores, -1e30)


def attend_row(packed):
    queries, key_rows, value_rows, seg_row = packed
    scores = masked_scores(queries, key_rows, seg_row)
    highest = jnp.max(scores, axis=-1, keepdims=True)
    logsum = highest + jnp.log(jnp.sum(jnp.exp(scores - highest), axis=-1, keepdims=True))
    probs_low = jnp.exp(scores - logsum).astype(jnp.bfloat16)
    context = jnp.einsum(
        "hqk,khd->qhd", probs_low, head_split(value_rows), preferred_element_type=jnp.float32
    )
    return (context.reshape(queries.shape).astype(jnp.bfloat16), logsum[..., 0])


def attend_back(packed):
    queries, key_rows, value_rows, seg_row, logsum, grad_ctx = packed
    scores = masked_scores(queries, key_rows, seg_row)
    probs = jnp.exp(scores - logsum[..., None])
    grad_heads = head_split(grad_ctx)
    grad_probs = jnp.einsum(
        "qhd,khd->hqk", grad_heads, head_split(value_rows), preferred_element_type=jnp.float32
    )
    centred = grad_probs - jnp.sum(probs * grad_probs, axis=-1, keepdims=True)
    grad_scores = (probs * centred * (1.0 / math.sqrt(HD))).astype(jnp.bfloat16)
    grad_query = jnp.einsum(
        "hqk,khd->qhd", grad_scores, head_split(key_rows), preferred_element_type=jnp.float32
    )
    grad_key = jnp.einsum(
        "hqk,qhd->khd", grad_scores, head_split(queries), preferred_element_type=jnp.float32
    )
    grad_value = jnp.einsum(
        "hqk,qhd->khd", probs.astype(jnp.bfloat16), grad_heads, preferred_element_type=jnp.float32
    )
    flat_shape = queries.shape
    return jnp.concatenate(
        [
            grad_query.reshape(flat_shape),
            grad_key.reshape(flat_shape),
            grad_value.reshape(flat_shape),
        ],
        axis=1,
    ).astype(jnp.bfloat16)


def add_trees(former, latter):
    return jax.tree.map(jnp.add, former, latter)


def on_device(
    hidden_in,
    segment_ids,
    out_grad,
    w_query,
    b_query,
    w_key,
    w_value,
    b_value,
    w_out,
    b_out,
    attn_gain,
    attn_shift,
    w_up,
    b_up,
    w_down,
    b_down,
    ffn_gain,
    ffn_shift,
):
    local_width = w_query.shape[1]
    packed_rows = segment_ids.shape[1]
    length = segment_ids.shape[2]
    w_qkv = jnp.concatenate([w_query, w_key, w_value], axis=1)
    b_qkv = jnp.concatenate([b_query, jnp.zeros_like(b_query), b_value]).astype(jnp.float32)
    b_out32 = b_out.astype(jnp.float32)
    b_up32 = b_up.astype(jnp.float32)
    b_down32 = b_down.astype(jnp.float32)
    attn_gain32 = attn_gain.astype(jnp.float32)
    attn_shift32 = attn_shift.astype(jnp.float32)
    ffn_gain32 = ffn_gain.astype(jnp.float32)
    ffn_shift32 = ffn_shift.astype(jnp.float32)

    def to_rows(block):
        return block.reshape(packed_rows, length, block.shape[1])

    outputs = []
    input_grads = []
    weight_terms = []
    small_terms = []
    for micro_step in range(MICRO):
        tokens_low = hidden_in[micro_step]
        tokens = tokens_low.astype(jnp.float32)
        seg_rows = segment_ids[micro_step]
        full_rows = lax.all_gather(tokens_low, "tensor", axis=0, tiled=True)
        qkv_low = (matmul(full_rows, w_qkv) + b_qkv).astype(jnp.bfloat16)
        queries = qkv_low[:, :local_width]
        key_rows = qkv_low[:, local_width : 2 * local_width]
        value_rows = qkv_low[:, 2 * local_width :]
        context, logsums = lax.map(
            attend_row, (to_rows(queries), to_rows(key_rows), to_rows(value_rows), seg_rows)
        )
        context = context.reshape(-1, local_width)
        attn_part = lax.psum_scatter(
            matmul(context, w_out).astype(jnp.bfloat16), "tensor", scatter_dimension=0, tiled=True
        ).astype(jnp.float32)
        resid_one = attn_part + b_out32 + tokens
        hidden_one, norm_one_back = jax.vjp(layer_norm, resid_one, attn_gain32, attn_shift32)
        hidden_low = hidden_one.astype(jnp.bfloat16)
        hidden_rows = lax.all_gather(hidden_low, "tensor", axis=0, tiled=True)
        pre_act = matmul(hidden_rows, w_up) + b_up32
        activation, gelu_back = jax.vjp(gelu_exact, pre_act)
        gelu_low = activation.astype(jnp.bfloat16)
        ffn_part = lax.psum_scatter(
            matmul(gelu_low, w_down).astype(jnp.bfloat16), "tensor", scatter_dimension=0, tiled=True
        ).astype(jnp.float32)
        resid_two = ffn_part + b_down32 + hidden_one
        result, norm_two_back = jax.vjp(layer_norm, resid_two, ffn_gain32, ffn_shift32)
        outputs.append(result.astype(jnp.bfloat16))
        grad_two, grad_ffn_gain, grad_ffn_shift = norm_two_back(
            out_grad[micro_step].astype(jnp.float32)
        )
        grad_two_low = grad_two.astype(jnp.bfloat16)
        grad_two_rows = lax.all_gather(grad_two_low, "tensor", axis=0, tiled=True)
        grad_down = inner_rows(gelu_low, grad_two_rows)
        grad_act = inner_cols(grad_two_rows, w_down)
        grad_pre = gelu_back(grad_act)[0].astype(jnp.bfloat16)
        grad_up = inner_rows(hidden_rows, grad_pre)
        grad_hidden = (
            lax.psum_scatter(
                inner_cols(grad_pre, w_up).astype(jnp.bfloat16),
                "tensor",
                scatter_dimension=0,
                tiled=True,
            ).astype(jnp.float32)
            + grad_two
        )
        grad_one, grad_attn_gain, grad_attn_shift = norm_one_back(grad_hidden)
        grad_one_low = grad_one.astype(jnp.bfloat16)
        grad_one_rows = lax.all_gather(grad_one_low, "tensor", axis=0, tiled=True)
        grad_wout = inner_rows(context, grad_one_rows)
        grad_ctx = inner_cols(grad_one_rows, w_out).astype(jnp.bfloat16)
        grad_qkv = lax.map(
            attend_back,
            (
                to_rows(queries),
                to_rows(key_rows),
                to_rows(value_rows),
                seg_rows,
                logsums,
                to_rows(grad_ctx),
            ),
        )
        grad_qkv = grad_qkv.reshape(-1, 3 * local_width)
        grad_wqkv = inner_rows(full_rows, grad_qkv)
        grad_in = (
            lax.psum_scatter(
                inner_cols(grad_qkv, w_qkv).astype(jnp.bfloat16),
                "tensor",
                scatter_dimension=0,
                tiled=True,
            ).astype(jnp.float32)
            + grad_one
        )
        input_grads.append(grad_in.astype(jnp.bfloat16))
        small_terms.append(
            (
                jnp.sum(grad_qkv.astype(jnp.float32), axis=0),
                jnp.sum(grad_pre.astype(jnp.float32), axis=0),
                jnp.sum(grad_one, axis=0),
                grad_attn_gain,
                grad_attn_shift,
                jnp.sum(grad_two, axis=0),
                grad_ffn_gain,
                grad_ffn_shift,
            )
        )
        weight_set = (grad_wqkv, grad_up, grad_wout, grad_down)
        weight_terms.append(weight_set)
    summed = reduce(add_trees, weight_terms)
    summed = (
        lax.psum_scatter(
            summed[0].astype(jnp.bfloat16), "dp", scatter_dimension=0, tiled=True
        ).astype(jnp.float32),
        lax.psum_scatter(
            summed[1].astype(jnp.bfloat16), "dp", scatter_dimension=0, tiled=True
        ).astype(jnp.float32),
        lax.psum_scatter(
            summed[2].astype(jnp.bfloat16), "dp", scatter_dimension=1, tiled=True
        ).astype(jnp.float32),
        lax.psum_scatter(
            summed[3].astype(jnp.bfloat16), "dp", scatter_dimension=1, tiled=True
        ).astype(jnp.float32),
    )
    red_qkv, red_up, red_wout, red_down = summed
    small = reduce(add_trees, small_terms)
    bias_qkv, bias_up = lax.psum((small[0], small[1]), "dp")
    norm_bout, norm_again, norm_ashift, norm_bdown, norm_fgain, norm_fshift = lax.psum(
        (small[2], small[3], small[4], small[5], small[6], small[7]), ("dp", "tensor")
    )
    output = jnp.stack(outputs, axis=0)
    grad_input = jnp.stack(input_grads, axis=0)
    return (
        output,
        grad_input,
        red_qkv[:, :local_width],
        bias_qkv[:local_width],
        red_qkv[:, local_width : 2 * local_width],
        red_qkv[:, 2 * local_width :],
        bias_qkv[2 * local_width :],
        red_wout,
        norm_bout,
        norm_again,
        norm_ashift,
        red_up,
        bias_up,
        red_down,
        norm_bdown,
        norm_fgain,
        norm_fshift,
    )


def dot_nn(former, latter):
    return jnp.dot(former, latter, preferred_element_type=jnp.float32)


def dot_tn(former, latter):
    return lax.dot_general(
        former, latter, (((0,), (0,)), ((), ())), preferred_element_type=jnp.float32
    )


def dot_nt(former, latter):
    return lax.dot_general(
        former, latter, (((1,), (1,)), ((), ())), preferred_element_type=jnp.float32
    )


def head_pair(block):
    lane = lax.broadcasted_iota(jnp.int32, block.shape, 1)
    zero = jnp.zeros_like(block)
    return (jnp.where(lane < HD, block, zero), jnp.where(lane < HD, zero, block))


def in_vmem(count):
    return [pl.BlockSpec(memory_space=pltpu.VMEM) for _ in range(count)]


def call(kernel, name, outs, *args, scalars=0, scratch=(), products=0):
    out_shape = tuple(jax.ShapeDtypeStruct(shape, dtype) for shape, dtype in outs)
    moved = sum(math.prod(a.shape) * a.dtype.itemsize for a in (*args, *out_shape))
    return pl.pallas_call(
        kernel,
        out_shape=out_shape,
        in_specs=[pl.BlockSpec(memory_space=pltpu.SMEM) for _ in range(scalars)]
        + in_vmem(len(args) - scalars),
        out_specs=tuple(in_vmem(len(outs))),
        scratch_shapes=list(scratch),
        compiler_params=pltpu.CompilerParams(vmem_limit_bytes=8 << 20),
        cost_estimate=pl.CostEstimate(
            flops=2 * products, transcendentals=0, bytes_accessed=moved
        ),
        name=name,
    )(*args)


def pieces_of(total, most):
    return [slice(at, min(at + most, total)) for at in range(0, total, most)]


def low(block):
    return block.astype(jnp.bfloat16)


def wide(block):
    return block.astype(jnp.float32)


def heads_kernel(
    seg_col_ref, seg_row_ref, x_ref, wq_ref, wk_ref, wv_ref, bias_ref,
    q_ref, k_ref, v_ref, ctx_ref, lse_ref, mask_ref,
):
    mask_ref[...] = jnp.where(seg_col_ref[...] == seg_row_ref[...], 0.0, -1e30)
    for rows in pieces_of(x_ref.shape[0], 256):
        x = x_ref[rows, :]
        for cols in pieces_of(wq_ref.shape[1], 256):
            q_ref[rows, cols] = low(dot_nn(x, wq_ref[:, cols]) + bias_ref[0:1, cols])
            k_ref[rows, cols] = low(dot_nn(x, wk_ref[:, cols]))
            v_ref[rows, cols] = low(dot_nn(x, wv_ref[:, cols]) + bias_ref[1:2, cols])
    for i in range(q_ref.shape[1] // (2 * HD)):
        cols = slice(2 * HD * i, 2 * HD * (i + 1))
        q_pair = q_ref[:, cols] * jnp.bfloat16(1.0 / math.sqrt(HD))
        outs = []
        for h, q_one in enumerate(head_pair(q_pair)):
            scores = dot_nt(k_ref[:, cols], q_one) + mask_ref[...]
            highest = jnp.max(scores, axis=0, keepdims=True)
            raised = jnp.exp(scores - highest)
            total = jnp.sum(raised, axis=0, keepdims=True)
            lse_ref[i, h : h + 1, :] = highest + jnp.log(total)
            mixed = dot_tn(v_ref[:, cols], low(raised))
            outs.append(mixed[h * HD : (h + 1) * HD] * (1.0 / total))
        ctx_ref[:, cols] = low(jnp.concatenate(outs, axis=0).T)


def heads(x, w_q, w_k, w_v, bias, seg):
    length, width = x.shape[0], w_q.shape[1]
    flat = ((length, width), jnp.bfloat16)
    return call(
        heads_kernel,
        "heads",
        (flat, flat, flat, flat, ((width // (2 * HD), 2, length), jnp.float32)),
        seg[:, None], seg[None, :], x, w_q, w_k, w_v, bias,
        products=length * width * (3 * x.shape[1] + 2 * length),
        scratch=[pltpu.VMEM((length, length), jnp.float32)],
    )


def heads_back_kernel(
    seg_col_ref, seg_row_ref, q_ref, k_ref, v_ref, lse_ref, g_ref, w_ref,
    grad_ref, sum_ref, ctx_ref, mask_ref,
):
    mask_ref[...] = jnp.where(seg_col_ref[...] == seg_row_ref[...], 0.0, -1e30)
    scale = 1.0 / math.sqrt(HD)
    width = q_ref.shape[1]
    for rows in pieces_of(g_ref.shape[0], 256):
        for cols in pieces_of(width, 256):
            ctx_ref[rows, cols] = low(dot_nt(g_ref[rows, :], w_ref[cols, :]))
    for i in range(width // (2 * HD)):
        cols = slice(2 * HD * i, 2 * HD * (i + 1))
        q_pair = q_ref[:, cols] * jnp.bfloat16(scale)
        grad_q, grad_k, grad_v = [], 0.0, 0.0
        for h, (q_one, g_one) in enumerate(zip(head_pair(q_pair), head_pair(ctx_ref[:, cols]))):
            scores = dot_nt(k_ref[:, cols], q_one) + mask_ref[...]
            probs = jnp.exp(scores - lse_ref[i, h : h + 1, :])
            grad_p = dot_nt(v_ref[:, cols], g_one)
            delta = jnp.sum(probs * grad_p, axis=0, keepdims=True)
            grad_s = low(probs * (grad_p - delta))
            grad_v = grad_v + dot_nn(low(probs), g_one)
            grad_k = grad_k + dot_nn(grad_s, q_one)
            grad_q.append(dot_tn(k_ref[:, cols], grad_s)[h * HD : (h + 1) * HD])
        grad_q = (jnp.concatenate(grad_q, axis=0) * scale).T
        for n, grad in enumerate((grad_q, grad_k, grad_v)):
            there = slice(n * width + 2 * HD * i, n * width + 2 * HD * (i + 1))
            grad = low(grad)
            grad_ref[:, there] = grad
            sum_ref[:, there] = jnp.sum(wide(grad), axis=0, keepdims=True)


def heads_back(qkv, lse, seg, grad_one_low, w_out):
    length, width = qkv[0].shape
    return call(
        heads_back_kernel,
        "heads_back",
        (((length, 3 * width), jnp.bfloat16), ((1, 3 * width), jnp.float32)),
        seg[:, None], seg[None, :], *qkv, lse, grad_one_low, w_out,
        products=length * width * (w_out.shape[1] + 5 * length),
        scratch=[
            pltpu.VMEM((length, width), jnp.bfloat16),
            pltpu.VMEM((length, length), jnp.float32),
        ],
    )


B_OUT, GAIN_ONE, SHIFT_ONE, B_DOWN, GAIN_TWO, SHIFT_TWO = range(6)


def row_of(ref, row):
    return ref[row : row + 1, :]


def row_norm(resid):
    centre = resid - jnp.mean(resid, axis=-1, keepdims=True)
    root = lax.rsqrt(jnp.mean(centre * centre, axis=-1, keepdims=True) + 1e-12)
    return centre * root, root


def row_norm_back(grad, gain, unit, root):
    inner = grad * gain
    mean = jnp.mean(inner, axis=-1, keepdims=True)
    along = jnp.mean(inner * unit, axis=-1, keepdims=True)
    return root * (inner - mean - unit * along)


def store_turned(depth, place, block, spare_ref, keep_ref, send_ref, base, cols):
    rows = block.shape[1] >> depth
    spare_ref[...] = block.T
    core = place & 1
    for pair in range(1 << (depth - 1)):
        step = pair ^ (place >> 1)
        bits = [(step >> bit) & 1 for bit in range(depth - 1)]
        for owner, ref, start in ((core, keep_ref, 0), (1 - core, send_ref, base)):
            first = jnp.where(owner == 0, bits[1], bits[2])
            second = jnp.where(owner == 0, bits[2], bits[1])
            where = ((bits[0] * 2 + first) * 2 + second) * rows + start
            source = pl.multiple_of((2 * pair + owner) * rows, 16)
            ref[pl.ds(pl.multiple_of(where, 16), rows), cols] = spare_ref[pl.ds(source, rows), :]


def norm_one_kernel(
    depth, place_ref, ctx_a_ref, ctx_b_ref, w_a_ref, w_b_ref, x_ref, par_ref,
    unit_ref, root_ref, low_ref, hidden_ref, tokens_ref, send_ref, sum_ref, spare_ref,
):
    for cols in pieces_of(x_ref.shape[1], 256):
        sum_ref[:, cols] = dot_nn(ctx_a_ref[...], w_a_ref[:, cols]) + dot_nn(
            ctx_b_ref[...], w_b_ref[:, cols]
        )
    for rows in pieces_of(x_ref.shape[0], 128):
        x = x_ref[rows, :]
        unit, root = row_norm(sum_ref[rows, :] + row_of(par_ref, B_OUT) + wide(x))
        unit_ref[rows, :] = unit
        root_ref[rows, :] = root
        hidden = low(unit * row_of(par_ref, GAIN_ONE) + row_of(par_ref, SHIFT_ONE))
        low_ref[rows, :] = hidden
        keep = hidden_ref.shape[0]
        store_turned(depth, place_ref[0], hidden, spare_ref, hidden_ref, send_ref, 0, rows)
        store_turned(depth, place_ref[0], x, spare_ref, tokens_ref, send_ref, keep, rows)
    send_ref[2 * keep : 2 * keep + ctx_a_ref.shape[0], :] = ctx_a_ref[...]
    send_ref[2 * keep + ctx_a_ref.shape[0] :, :] = ctx_b_ref[...]


def norm_one(depth, place, ctx_a, ctx_b, w_a, w_b, x, par):
    length, width = x.shape
    kept = ((width // 2, length), jnp.bfloat16)
    return call(
        partial(norm_one_kernel, depth),
        "norm_one",
        (
            (x.shape, jnp.float32),
            ((length, 1), jnp.float32),
            (x.shape, jnp.bfloat16),
            kept,
            kept,
            ((width + 2 * length, length), jnp.bfloat16),
        ),
        place.reshape(1), ctx_a, ctx_b, w_a, w_b, x, par,
        scalars=1,
        scratch=[pltpu.VMEM(x.shape, jnp.float32), pltpu.VMEM((width, 128), jnp.bfloat16)],
        products=2 * ctx_a.shape[0] * w_a.shape[0] * w_a.shape[1],
    )


def up_kernel(x_ref, w_ref, bias_ref, act_ref, slope_ref):
    for cols in pieces_of(w_ref.shape[1], 256):
        at = cols.start % bias_ref.shape[1]
        row = 2 + cols.start // bias_ref.shape[1]
        bias = bias_ref[row : row + 1, at : at + 256]
        for rows in pieces_of(x_ref.shape[0], 256):
            pre = dot_nn(x_ref[rows, :], w_ref[:, cols]) + bias
            act_ref[rows, cols], slope_ref[rows, cols] = gelu_pair(pre)


def up(x, w, bias):
    flat = ((x.shape[0], w.shape[1]), jnp.bfloat16)
    products = x.shape[0] * w.shape[0] * w.shape[1]
    return call(up_kernel, "up", (flat, flat), x, w, bias, products=products)


def down_kernel(act_ref, w_ref, out_ref):
    for rows in pieces_of(act_ref.shape[0], 256):
        for cols in pieces_of(w_ref.shape[1], 256):
            out_ref[rows, cols] = dot_nn(act_ref[rows, :], w_ref[:, cols])


def down(act, w):
    out = ((act.shape[0], w.shape[1]), jnp.float32)
    products = act.shape[0] * w.shape[0] * w.shape[1]
    return call(down_kernel, "down", (out,), act, w, products=products)[0]


def norm_two_kernel(
    depth, place_ref, ffn_ref, act_ref, w_ref, unit_one_ref, par_ref, grad_ref,
    out_ref, two_ref, low_ref, keep_ref, send_ref, sum_ref, spare_ref,
):
    for cols in pieces_of(w_ref.shape[1], 256):
        two_ref[:, cols] = ffn_ref[:, cols] + dot_nn(act_ref[...], w_ref[:, cols])
    sum_ref[...] = jnp.zeros_like(sum_ref)
    for rows in pieces_of(act_ref.shape[0], 128):
        hidden = unit_one_ref[rows, :] * row_of(par_ref, GAIN_ONE) + row_of(par_ref, SHIFT_ONE)
        unit, root = row_norm(two_ref[rows, :] + row_of(par_ref, B_DOWN) + hidden)
        gain = row_of(par_ref, GAIN_TWO)
        out_ref[rows, :] = low(unit * gain + row_of(par_ref, SHIFT_TWO))
        grad = wide(grad_ref[rows, :])
        two = row_norm_back(grad, gain, unit, root)
        two_ref[rows, :] = two
        two_low = low(two)
        low_ref[rows, :] = two_low
        store_turned(depth, place_ref[0], two_low, spare_ref, keep_ref, send_ref, 0, rows)
        for i, term in enumerate((two, grad * unit, grad)):
            sum_ref[i : i + 1, :] += jnp.sum(term, axis=0, keepdims=True)


def norm_two(depth, place, ffn, act, w, unit_one, par, grad_out):
    shape = grad_out.shape
    flat, kept = (shape, jnp.bfloat16), ((shape[1] // 2, shape[0]), jnp.bfloat16)
    return call(
        partial(norm_two_kernel, depth),
        "norm_two",
        (flat, (shape, jnp.float32), flat, kept, kept, ((3, shape[1]), jnp.float32)),
        place.reshape(1), ffn, act, w, unit_one, par, grad_out,
        scalars=1,
        scratch=[pltpu.VMEM((shape[1], 128), jnp.bfloat16)],
        products=act.shape[0] * w.shape[0] * w.shape[1],
    )


def pre_kernel(grad_ref, w_ref, slope_ref, out_ref, sum_ref):
    for cols in pieces_of(w_ref.shape[0], 256):
        total = 0.0
        for rows in pieces_of(grad_ref.shape[0], 256):
            grad = low(dot_nt(grad_ref[rows, :], w_ref[cols, :]) * wide(slope_ref[rows, cols]))
            out_ref[rows, cols] = grad
            total = total + jnp.sum(wide(grad), axis=0, keepdims=True)
        sum_ref[:, cols] = total


def pre_back(grad, w, slope):
    return call(
        pre_kernel, "pre_back", ((slope.shape, jnp.bfloat16), ((1, slope.shape[1]), jnp.float32)),
        grad, w, slope,
        products=grad.shape[0] * w.shape[0] * w.shape[1],
    )


def one_kernel(
    depth, place_ref, pre_a_ref, pre_b_ref, w_a_ref, w_b_ref, two_ref, unit_ref, root_ref, par_ref,
    one_ref, low_ref, keep_ref, send_ref, sum_ref, spare_ref,
):
    for cols in pieces_of(one_ref.shape[1], 256):
        one_ref[:, cols] = dot_nt(pre_a_ref[...], w_a_ref[cols, :]) + dot_nt(
            pre_b_ref[...], w_b_ref[cols, :]
        )
    sum_ref[...] = jnp.zeros_like(sum_ref)
    for rows in pieces_of(pre_a_ref.shape[0], 128):
        grad = one_ref[rows, :] + two_ref[rows, :]
        unit = unit_ref[rows, :]
        one = row_norm_back(grad, row_of(par_ref, GAIN_ONE), unit, root_ref[rows, :])
        one_ref[rows, :] = one
        one_low = low(one)
        low_ref[rows, :] = one_low
        store_turned(depth, place_ref[0], one_low, spare_ref, keep_ref, send_ref, 0, rows)
        for i, term in enumerate((one, grad * unit, grad)):
            sum_ref[i : i + 1, :] += jnp.sum(term, axis=0, keepdims=True)


def one_back(depth, place, pre_a, pre_b, w_a, w_b, two, unit, root, par):
    shape = two.shape
    return call(
        partial(one_kernel, depth),
        "one_back",
        (
            (shape, jnp.float32),
            (shape, jnp.bfloat16),
            ((shape[1] // 2, shape[0]), jnp.bfloat16),
            ((shape[1] // 2, shape[0]), jnp.bfloat16),
            ((3, shape[1]), jnp.float32),
        ),
        place.reshape(1), pre_a, pre_b, w_a, w_b, two, unit, root, par,
        scalars=1,
        scratch=[pltpu.VMEM((shape[1], 128), jnp.bfloat16)],
        products=2 * pre_a.shape[0] * w_a.shape[0] * w_a.shape[1],
    )


def input_kernel(one_ref, a_ref, b_ref, *refs):
    weights, out_ref = refs[:6], refs[6]
    width = weights[0].shape[1]
    for rows in pieces_of(one_ref.shape[0], 256):
        for cols in pieces_of(one_ref.shape[1], 256):
            total = one_ref[rows, cols]
            for i, w_ref in enumerate(weights):
                grad_ref = (a_ref, b_ref)[i // 3]
                part = slice((i % 3) * width, (i % 3 + 1) * width)
                total = total + dot_nt(grad_ref[rows, part], w_ref[cols, :])
            out_ref[rows, cols] = low(total)


def input_back(grad_one, grad_a, grad_b, weights):
    return call(
        input_kernel, "input_back", ((grad_one.shape, jnp.bfloat16),),
        grad_one, grad_a, grad_b, *weights,
        products=2 * grad_a.shape[0] * grad_a.shape[1] * grad_one.shape[1],
    )[0]


def take_kernel(index_ref, *refs):
    weights, (one_ref, up_ref, down_ref), sems = refs[:6], refs[6:9], refs[9]
    copies = []

    def start(source, target):
        copies.append(pltpu.make_async_copy(source, target, sems.at[len(copies)]))
        copies[-1].start()

    def rows_of(ref):
        rows = ref.shape[0] // 8
        return pl.ds(pl.multiple_of(index_ref[0] * rows, 16), rows)

    at = 0
    cols = one_ref.shape[1]
    for ref in weights[:4]:
        rows = ref.shape[0] // 8
        for col in range(0, ref.shape[1], cols):
            start(ref.at[rows_of(ref), col : col + cols], one_ref.at[at : at + rows])
            at += rows
    start(weights[4].at[rows_of(weights[4])], up_ref)
    rows = weights[5].shape[0] // 4
    start(weights[5].at[pl.ds(pl.multiple_of(index_ref[8] * rows, 16), rows)], down_ref)
    for copy in copies:
        copy.wait()


def take(indices, weights):
    blocks = [(w.shape[0] // 8, w.shape[1]) for w in weights]
    local = blocks[0][1]
    one = (sum(rows * cols for rows, cols in blocks[:4]) // local, local)
    shapes = [one, blocks[4], (2 * blocks[5][0], blocks[5][1])]
    parts = sum(cols // local for _, cols in blocks[:4]) + 2
    return pl.pallas_call(
        take_kernel,
        in_specs=[pl.BlockSpec(memory_space=pltpu.SMEM)]
        + [pl.BlockSpec(memory_space=pltpu.HBM) for _ in weights],
        out_specs=tuple(in_vmem(3)),
        out_shape=tuple(jax.ShapeDtypeStruct(shape, jnp.bfloat16) for shape in shapes),
        scratch_shapes=[pltpu.SemaphoreType.DMA((parts,))],
        cost_estimate=pl.CostEstimate(
            flops=0, transcendentals=0, bytes_accessed=4 * sum(r * c for r, c in shapes)
        ),
        compiler_params=pltpu.CompilerParams(vmem_limit_bytes=8 << 20),
        name="take",
    )(indices, *weights)


def kept_kernel(starts, core_ref, rows_ref, near_ref, far_ref, more_rows_ref, more_near_ref, more_far_ref, kept_ref, sent_ref):
    half = rows_ref.shape[0] // 2
    length = near_ref.shape[0]
    pairs = ((near_ref, more_near_ref, starts[1]), (far_ref, more_far_ref, starts[2]))

    def part(row, side, cols):
        ref, more_ref, start = pairs[side]
        rows, more = slice(row * half, (row + 1) * half), starts[0] + row * half
        total = dot_nn(rows_ref[rows, :], ref[:, cols])
        return low(
            total
            + dot_nn(more_rows_ref[more : more + half, :], more_ref[start : start + length, cols])
        )

    for cols in pieces_of(near_ref.shape[1], 512):
        kept_ref[0, :, cols] = part(0, 0, cols)
        sent_ref[1, :, cols] = part(1, 1, cols)
        one, two = part(1, 0, cols), part(0, 1, cols)

        @pl.when(core_ref[0] == 0)
        def _():
            kept_ref[1, :, cols] = one
            sent_ref[0, :, cols] = two

        @pl.when(core_ref[0] != 0)
        def _():
            kept_ref[1, :, cols] = two
            sent_ref[0, :, cols] = one


def far_kernel(core_ref, rows_ref, near_ref, far_ref, more_rows_ref, more_near_ref, more_far_ref, kept_ref, sent_ref):
    half = rows_ref.shape[0] // 2
    part = half // 4
    pairs = ((near_ref, more_near_ref), (far_ref, more_far_ref))
    for cols in pieces_of(near_ref.shape[1], 512):
        for row in range(2):
            rows = slice(row * half, (row + 1) * half)
            for side, (ref, more_ref) in enumerate(pairs):
                total = dot_nn(rows_ref[rows, :], ref[:, cols])
                total = low(total + dot_nn(more_rows_ref[rows, :], more_ref[:, cols]))
                first = jnp.where(core_ref[0] == 0, side, row)
                second = jnp.where(core_ref[0] == 0, row, side)
                for n in range(2):
                    kept_ref[n, first, second, :, cols] = total[n * part : (n + 1) * part]
                    sent_ref[n, first, second, :, cols] = total[(2 + n) * part : (3 + n) * part]


def grad_kept_far(core, rows, near, far, more):
    shape = ((2, 2, 2, rows.shape[0] // 8, near.shape[1]), jnp.bfloat16)
    return call(
        far_kernel, "grad_kept_far", (shape, shape), core.reshape(1), rows, near, far, *more,
        scalars=1,
        products=4 * rows.shape[0] * near.shape[0] * near.shape[1],
    )


def grad_kept(core, rows, near, far, more, starts):
    shape = ((2, rows.shape[0] // 2, near.shape[1]), jnp.bfloat16)
    return call(
        partial(kept_kernel, starts), "grad_kept", (shape, shape),
        core.reshape(1), rows, near, far, *more,
        scalars=1,
        products=4 * rows.shape[0] * near.shape[0] * near.shape[1],
    )


def gelu_pair(pre):
    cdf = 0.5 * (1.0 + lax.erf(pre * (1.0 / math.sqrt(2.0))))
    pdf = jnp.exp(-0.5 * pre * pre) * (1.0 / math.sqrt(2.0 * math.pi))
    return (pre * cdf).astype(jnp.bfloat16), (cdf + pre * pdf).astype(jnp.bfloat16)


def lay_kernel(layout, index_ref, *refs):
    ins, outs = refs[: len(layout)], refs[len(layout) :]
    for source, places in zip(ins, layout):
        for slot, unit, at, rows, which, col in places:
            offset = pl.multiple_of(index_ref[slot] * unit, 16)
            outs[which][pl.ds(offset, rows), col : col + source.shape[1]] = source[
                at : at + rows, :
            ]


def lay(indices, sources, layout, shapes):
    outs = tuple((shape, jnp.bfloat16) for shape in shapes)
    return call(partial(lay_kernel, layout), "lay", outs, indices, *sources, scalars=1)


def tie(*values):
    return lax.optimization_barrier(values)


def add_low(former, latter):
    return (former.astype(jnp.float32) + latter.astype(jnp.float32)).astype(jnp.bfloat16)


class Reduction:
    def __init__(self, kept, sent, step, send_over):
        self.kept = kept
        self.send_over = send_over
        self.flying = send_over(sent, step)

    def send(self, step):
        rows = self.kept.shape[0] // 2
        self.flying = self.send_over(self.kept[rows:], step)
        self.kept = self.kept[:rows]

    def land(self, last=False):
        total = self.kept.astype(jnp.float32) + self.flying.astype(jnp.float32)
        self.kept = total if last else total.astype(jnp.bfloat16)
        self.flying = None


def row_on_device(
    groups,
    hidden_in,
    segment_ids,
    out_grad,
    w_query,
    b_query,
    w_key,
    w_value,
    b_value,
    w_out,
    b_out,
    attn_gain,
    attn_shift,
    w_up,
    b_up,
    w_down,
    b_down,
    ffn_gain,
    ffn_shift,
):
    side = lax.axis_index("tensor")
    place = lax.axis_index("dp")
    half = hidden_in.shape[1]
    width = hidden_in.shape[2]
    local = w_query.shape[1]
    depth = groups.bit_length() - 1
    f32 = jnp.float32
    bf16 = jnp.bfloat16

    def over(block):
        return lax.ppermute(block, "tensor", [(0, 1), (1, 0)])

    def across(block, mask):
        return lax.ppermute(block, "dp", [(i, i ^ mask) for i in range(groups)])

    sides = 2

    def by_core(block, ways):
        pairs = []
        for i in range(groups):
            mask, flip = ways[i & 1]
            pairs += [(i * sides + s, (i ^ mask) * sides + (s ^ flip)) for s in range(sides)]
        return lax.ppermute(block, ("dp", "tensor"), pairs)

    ways = {
        "one": ((0, 1), (2, 0)),
        "two": ((2, 0), (0, 1)),
        "near": ((2, 0), (4, 0)),
        "far": ((4, 0), (2, 0)),
        "three": ((4, 0), (8, 0)),
        "four": ((8, 0), (4, 0)),
    }

    def send(block, step):
        return across(block, 1 << step) if isinstance(step, int) else by_core(block, ways[step])

    def pick(pair):
        return lax.dynamic_index_in_dim(pair, side, 0, keepdims=False), lax.dynamic_index_in_dim(
            pair, 1 - side, 0, keepdims=False
        )

    core = place & 1
    eighth = place & 7
    first, second = 2 << core, 4 >> core
    low_bit, high_bit = (place >> 1) & 1, 2 + ((place >> 2) & 1)
    quarter = jnp.where(core == 0, low_bit, high_bit)
    other = jnp.where(core == 0, high_bit, low_bit)
    indices = jnp.stack(
        [eighth ^ mask for mask in (0, first, second, 6, 1, second ^ 1, first ^ 1, 7)]
        + [quarter, quarter ^ 1, other, other ^ 1]
    )
    eighths = ((0, 1), (2, 3), (4, 5), (6, 7))

    def second_hop(piece, got):
        held = jnp.concatenate([piece, got], axis=0)
        return held, send(held, "far")

    def gathered(sources, slots, cuts, shapes):
        layout = []
        for source in slots:
            rows = sources[len(layout)].shape[0] // len(source)
            layout.append(
                tuple(
                    (slot, unit, i * rows + at, count, which, col)
                    for i, slot in enumerate(source)
                    for at, count, unit, which, col in cuts
                )
            )
        return lay(indices, sources, tuple(layout), shapes)

    tokens_own, tokens_away = pick(hidden_in)
    tokens_away, indices = tie(tokens_away, indices)
    fly_tokens = over(tokens_away)
    piece_one, piece_up, piece_down = take(indices, (w_query, w_key, w_value, w_out, w_up, w_down))
    fly_one = over(piece_one)
    biases = jnp.concatenate([b_query, b_value, b_up])
    par = jnp.stack([b_out, attn_gain, attn_shift, b_down, ffn_gain, ffn_shift]).astype(f32)
    seg_own, _ = pick(segment_ids[:, 0])
    seg = jnp.where(
        side == 0, seg_own, jnp.concatenate([seg_own[half:], seg_own[:half]], axis=0)
    )
    cut = b_query.shape[0]
    tokens_got, biases, piece_up, par, seg = tie(fly_tokens, biases, piece_up, par, seg)
    fly_biases = over(biases)
    biases = biases.reshape(-1, cut).astype(f32)
    tokens_low = jnp.concatenate([tokens_own, tokens_got], axis=0)
    *qkv_a, ctx_a, lse_a = heads(tokens_low, w_query, w_key, w_value, biases, seg)
    ctx_a, one, biases_b, piece_up, piece_down = tie(
        ctx_a, fly_one, fly_biases, piece_up, piece_down
    )
    biases_b = biases_b.reshape(-1, cut).astype(f32)
    fly_one = send(one, "near")
    fly_up_x = over(piece_up)
    ctx_a, fly_one, up_piece, piece_down = tie(ctx_a, fly_one, fly_up_x, piece_down)
    one_held, fly_one = second_hop(one, fly_one)
    one_core = across(one_held, 1)
    fly_up = send(up_piece, "near")
    part = piece_down.shape[0] * 11 // 16
    fly_down_a = over(piece_down[:part])
    ctx_a, one_last, one_core, fly_up, down_a, piece_down = tie(
        ctx_a, fly_one, one_core, fly_up, fly_down_a, piece_down
    )
    one_last_core = across(one_last, 1)
    up_held, fly_up = second_hop(up_piece, fly_up)
    up_core = across(up_held, 1)
    fly_down_b = over(piece_down[part:])
    one_last_core, ctx_a = tie(one_last_core, ctx_a)
    rows = width // 8
    small_rows = local // 8
    w_query_b, w_key_b, w_value_b, w_out_b = gathered(
        (one_held, one_last, one_core, one_last_core),
        eighths,
        tuple((i * rows, rows, rows, i, 0) for i in range(3))
        + tuple(
            (3 * rows + i * small_rows, small_rows, small_rows, 3, i * local)
            for i in range(width // local)
        ),
        (w_query.shape, w_key.shape, w_value.shape, w_out.shape),
    )
    *qkv_b, ctx_b, lse_b = heads(tokens_low, w_query_b, w_key_b, w_value_b, biases_b, seg)
    ctx_b, up_last, up_core, down_b, out_grad = tie(ctx_b, fly_up, up_core, fly_down_b, out_grad)
    up_last_core = across(up_last, 1)
    down_piece = jnp.concatenate([down_a, down_b], axis=0)
    fly_down = send(down_piece, "near")
    down_core = across(down_piece, 1)
    grads_own, grads_away = pick(out_grad)
    fly_grads = over(grads_away)
    unit_one, root_one, hidden_low, hidden_rows, tokens_rows, shared = norm_one(
        depth, place, ctx_a, ctx_b, w_out, w_out_b, tokens_low, par
    )
    act_a, slope_a = up(hidden_low, w_up, biases)
    ffn_a = down(act_a, w_down)
    ffn_a, up_last_core, hidden_low = tie(ffn_a, up_last_core, hidden_low)
    (w_up_b,) = gathered(
        (up_held, up_last, up_core, up_last_core),
        eighths,
        ((0, rows, rows, 0, 0),),
        (w_up.shape,),
    )
    w_up_b, hidden_low, fly_down, fly_grads = tie(w_up_b, hidden_low, fly_down, fly_grads)
    down_last_core = across(fly_down, 1)
    act_b, slope_b = up(hidden_low, w_up_b, biases_b)
    act_b, act_a, down_core, down_last_core, shared = tie(
        act_b, act_a, down_core, down_last_core, shared
    )
    fly_act_a = across(act_a, 1)
    fly_act_b = across(act_b, 1)
    fly_shared = across(shared, 1)
    part = w_down.shape[0] // 4
    (w_down_b,) = gathered(
        (down_piece, fly_down, down_core, down_last_core),
        ((8,), (9,), (10,), (11,)),
        ((0, part, part, 0, 0),),
        (w_down.shape,),
    )
    grad_out = jnp.concatenate([grads_own, fly_grads], axis=0)
    output, grad_two, grad_two_low, two_rows, two_sent, sums_two = norm_two(
        depth, place, ffn_a, act_b, w_down_b, unit_one, par, grad_out
    )

    def land(carry, *reductions, last=False):
        carry, flying = tie(carry, [red.flying for red in reductions])
        for red, got in zip(reductions, flying):
            red.flying = got
            red.land(last)
        return carry

    def reduction(rows, near, far, more, *starts):
        kept, sent = tie(*grad_kept(core, rows, near, far, more, starts))
        return Reduction(kept, sent, "one", send)

    def blocks_of(red):
        kept = red.kept.reshape(-1, red.kept.shape[-1])
        red.kept = kept.reshape(2, kept.shape[0] // 2, kept.shape[1])

    two_rows, two_sent, grad_two_low, more_act_a, more_act_b = tie(
        two_rows, two_sent, grad_two_low, fly_act_a, fly_act_b
    )
    more_two = across(two_sent, 1)
    pre_b, sum_pre_b = pre_back(grad_two_low, w_down_b, slope_b)
    pre_b, grad_two_low, shared, more_two = tie(pre_b, grad_two_low, fly_shared, more_two)
    fly_pre_b = across(pre_b, 1)
    pre_a, sum_pre_a = pre_back(grad_two_low, w_down, slope_a)
    two_rows, pre_a = tie(two_rows, pre_a)
    kept, sent = tie(
        *grad_kept_far(core, two_rows, act_a, act_b, (more_two, more_act_a, more_act_b))
    )
    red_down = Reduction(kept, sent, "three", send)
    pre_a, red_down.kept, more_pre_b = tie(pre_a, red_down.kept, fly_pre_b)
    fly_pre_a = across(pre_a, 1)
    grad_one, grad_one_low, one_rows, one_sent, sums_one = one_back(
        depth, place, pre_a, pre_b, w_up, w_up_b, grad_two, unit_one, root_one, par
    )
    grad_one_low, one_rows, one_sent, pre_a, pre_b, hidden_rows, more_pre_a = tie(
        grad_one_low, one_rows, one_sent, pre_a, pre_b, hidden_rows, fly_pre_a
    )
    red_up = reduction(hidden_rows, pre_a, pre_b, (shared, more_pre_a, more_pre_b), 0, 0, 0)
    grad_one_low, one_rows, one_sent, red_up.kept = tie(
        grad_one_low, one_rows, one_sent, red_up.kept
    )
    more_one = across(one_sent, 1)
    grad_qkv_b, sum_qkv_b = heads_back(qkv_b, lse_b, seg, grad_one_low, w_out_b)
    grad_one_low, grad_qkv_b, more_one, one_rows = tie(
        grad_one_low, grad_qkv_b, more_one, one_rows
    )
    fly_qkv_b = across(grad_qkv_b, 1)
    red_out = reduction(
        one_rows, ctx_a, ctx_b, (more_one, shared, shared), 0, width, width + 2 * half
    )
    grad_one_low, red_out.kept = tie(grad_one_low, red_out.kept)
    grad_qkv_a, sum_qkv_a = heads_back(qkv_a, lse_a, seg, grad_one_low, w_out)
    grad_qkv_a = land(grad_qkv_a, red_down)
    blocks_of(red_down)
    grad_qkv_a, more_qkv_b, red_down.kept = land((grad_qkv_a, fly_qkv_b, red_down.kept), red_up)
    red_up.send("two")
    red_down.send("four")
    fly_qkv_a = across(grad_qkv_a, 1)
    grad_qkv_a, more_qkv_a = tie(grad_qkv_a, fly_qkv_a)
    red_qkv = reduction(
        tokens_rows, grad_qkv_a, grad_qkv_b, (shared, more_qkv_a, more_qkv_b), width // 2, 0, 0
    )
    grad_qkv_a, grad_qkv_b, red_qkv.kept = tie(grad_qkv_a, grad_qkv_b, red_qkv.kept)
    grad_in = input_back(
        grad_one, grad_qkv_a, grad_qkv_b, (w_query, w_key, w_value, w_query_b, w_key_b, w_value_b)
    )
    near = [sum_qkv_a[0, :cut], sum_qkv_a[0, 2 * cut :], sum_pre_a[0]]
    far = [sum_qkv_b[0, :cut], sum_qkv_b[0, 2 * cut :], sum_pre_b[0]]
    small = jnp.concatenate(near + far + [sums_one.reshape(-1), sums_two.reshape(-1)])
    size = 2 * cut + b_up.shape[0]
    small, grad_in = land((small, grad_in), red_up)
    blocks_of(red_up)
    red_up.send("three")
    more = across(small, 1)
    small, grad_in = land((small, grad_in), red_down)
    blocks_of(red_down)
    red_down.send("one")
    small, more, grad_in = land((small, more, grad_in), red_out)
    red_out.send("two")
    small = small + more
    small, grad_in = land((small, grad_in), red_qkv)
    red_qkv.send("two")
    more = across(small, 8)
    small, more, grad_in = land((small, more, grad_in), red_down)
    blocks_of(red_down)
    red_down.send("two")
    small = small + more
    fly_in = over(grad_in[half:])
    small, output = land((small, output), red_qkv)
    blocks_of(red_qkv)
    red_qkv.send("three")
    small, output = land((small, output), red_out)
    blocks_of(red_out)
    red_out.send("three")
    more = across(small, 4)
    small = land(small, red_down, last=True)
    small, more, output = land((small, more, output), red_up)
    blocks_of(red_up)
    red_up.send("four")
    fly_output = over(output[half:])
    small = small + more
    got = over(small[size:])
    small = jnp.concatenate([small[:size], small[2 * size :]])
    small, got = land((small, got), red_qkv)
    blocks_of(red_qkv)
    red_qkv.send("four")
    small = small + got
    got = across(small, 2)
    small, fly_in = land((small, fly_in), red_out)
    blocks_of(red_out)
    red_out.send("four")
    small, got, fly_output = tie(small, got, fly_output)
    small = small + got
    small = land(small, red_up, last=True)

    pieces = []
    at = 0
    for size in (cut, cut, b_up.shape[0]) + (width,) * 6:
        pieces.append(small[at : at + size])
        at += size

    def to_owners(mine, theirs):
        return jnp.where(side == 0, jnp.stack([mine, theirs]), jnp.stack([theirs, mine]))

    output = to_owners(output[:half], fly_output)
    grad_in = to_owners(grad_in[:half], fly_in)
    pieces, output, grad_in = land((pieces, output, grad_in), red_out, red_qkv, last=True)
    red_out, red_up, red_down, grad_qkv = (
        red.kept.reshape(-1, red.kept.shape[-1]) for red in (red_out, red_up, red_down, red_qkv)
    )
    return (
        output,
        grad_in,
        grad_qkv[:, :local],
        pieces[0],
        grad_qkv[:, local : 2 * local],
        grad_qkv[:, 2 * local :],
        pieces[1],
        red_out.T,
        pieces[3],
        pieces[4],
        pieces[5],
        red_up,
        pieces[2],
        red_down.T,
        pieces[6],
        pieces[7],
        pieces[8],
    )


def solution(mesh):
    placed = (
        P(None, ("dp", "tensor"), None),
        P(None, "dp", None),
        P(None, ("dp", "tensor"), None),
        P(None, "tensor"),
        P("tensor"),
        P(None, "tensor"),
        P(None, "tensor"),
        P("tensor"),
        P("tensor", None),
        P(),
        P(),
        P(),
        P(None, "tensor"),
        P("tensor"),
        P("tensor", None),
        P(),
        P(),
        P(),
    )
    body = on_device
    groups = mesh.shape["dp"]
    if mesh.shape["tensor"] == MICRO and groups == 16:
        body = partial(row_on_device, groups)
    return jax.shard_map(
        body,
        mesh=mesh,
        in_specs=placed,
        out_specs=(
            P(None, ("dp", "tensor"), None),
            P(None, ("dp", "tensor"), None),
            P("dp", "tensor"),
            P("tensor"),
            P("dp", "tensor"),
            P("dp", "tensor"),
            P("tensor"),
            P("tensor", "dp"),
            P(),
            P(),
            P(),
            P("dp", "tensor"),
            P("tensor"),
            P("tensor", "dp"),
            P(),
            P(),
            P(),
        ),
        check_vma=False,
    )
```
